512 devices in a mesh: head: 32 (over x_lo, z), ctx: 8 (over y, core), dp: 2 (over x_hi).
Axes of the slice: x: 4 (x_hi: 2, x_lo: 2; x = x_hi * 2 + x_lo), y: 4, z: 16, core: 2. Of those that a mesh axis runs over, the one named last changes fastest.
Arguments:
- query_nope: bfloat16 [2, 1024, 128, 128], P('dp', 'ctx', 'head'), may hold values from -6 to 6
- query_rope: bfloat16 [2, 1024, 128, 64], P('dp', 'ctx', 'head'), may hold values from -10 to 10
- query_pos: int32 [2, 1024], P('dp', 'ctx'), may hold values from 64 to 1023
- latent_cache: bfloat16 [2, 16, 64, 576], P('dp', 'ctx'), may hold values from -6 to 6
- block_table: int32 [2, 16], P('dp'), may hold values from 0 to 15, each once within a row
- key_up: bfloat16 [128, 128, 512], P('head'), may hold values from -0.5 to 0.5
- value_up: bfloat16 [128, 512, 128], P('head'), may hold values from -0.25 to 0.25
- grad_out: bfloat16 [2, 1024, 128, 128], P('dp', 'ctx', 'head'), may hold values from -6 to 6
Outputs:
- grad_query_nope: float32 [2, 1024, 128, 128], P('dp', 'ctx', 'head')
- grad_query_rope: float32 [2, 1024, 128, 64], P('dp', 'ctx', 'head')
- grad_cache: float32 [2, 16, 64, 576], P('dp', 'ctx')
- grad_key_up: float32 [128, 128, 512], P('head', ('ctx', 'dp'))
- grad_value_up: float32 [128, 512, 128], P('head', ('ctx', 'dp'))
The draws below stay inside these ranges and needn't reach their ends.
Inputs may be any that keep to these rules, and one draw needn't show every extreme that they name: Each row is a permutation: logical block b of sequence s lies in physical block block_table[s, b].
All inputs are finite; a program needn't handle non-finite values.
Results may differ from the reference program's by a relative error of at most 0.025.
Values may be sent and summed in bfloat16 or wider, within the bound.
A program may use at most 64 MiB of HBM per device.

```python
import jax
import jax.numpy as jnp
from jax import lax

H = 128
DNOPE = 128
LAT = 512
ROPE = 64
DV = 128
PAGE = 64
Q_DEV = 128
SEQS = 2
Q = 1024
BLOCKS = 16
KEYS = 1024
N_CTX = 8


def draw_query_rope(key, part):
    full_shape = (SEQS, Q, H, ROPE)
    drawn = jnp.clip(jax.random.normal(jax.random.fold_in(key, 11), full_shape, jnp.float32), -4.0, 4.0)
    return drawn.astype(jnp.bfloat16)


def draw_latent_cache(key, part):
    full_shape = (SEQS, BLOCKS, PAGE, LAT + ROPE)
    drawn = jnp.clip(jax.random.normal(jax.random.fold_in(key, 23), full_shape, jnp.float32), -4.0, 4.0)
    return drawn.astype(jnp.bfloat16)


def place_ends(values, rng, low, largest):
    dims = values.shape
    place = [jax.random.randint(jax.random.fold_in(rng, axis), (), 0, dims[axis]) for axis in range(len(dims))]
    values = values.at[tuple(place)].set(low)
    longest = dims.index(max(dims))
    place[longest] = (place[longest] + 1) % dims[longest]
    return values.at[tuple(place)].set(largest)


def block_scale(stream_key, dims, cuts, least, largest):
    level = 1.0
    for axis_at, shards_of in cuts:
        draws = jax.random.uniform(jax.random.fold_in(jax.random.fold_in(stream_key, 6), axis_at), (shards_of,), jnp.float32, least / len(cuts), largest / len(cuts))
        level = level * jnp.repeat(jnp.exp(draws), dims[axis_at] // shards_of).reshape((-1,) + (1,) * (len(dims) - 1 - axis_at))
    return level


def scatter_about(rng, dims, spread, limit, pieces=(), kind=jnp.bfloat16):
    values = jax.random.normal(rng, dims, jnp.float32) * spread
    if len(pieces) > 0:
        values = block_scale(rng, dims, pieces, -0.22, 0.18) * values
    return jnp.clip(values, min=-limit, max=limit).astype(kind)


def setup_inputs(seed: int = 0) -> dict:
    splits = jax.random.split(jax.random.key(seed), 9)
    return {
        "query_nope": scatter_about(splits[0], (SEQS, Q, H, DNOPE), 1.0, 6.0, ((0, 2), (1, 8), (2, 32))),
        "query_rope": draw_query_rope(jax.random.fold_in(splits[8], 71), 0),
        "query_pos": place_ends(jax.random.randint(splits[2], (SEQS, Q), PAGE, KEYS), jax.random.fold_in(splits[2], 1), PAGE, KEYS - 1).astype(jnp.int32),
        "latent_cache": draw_latent_cache(jax.random.fold_in(splits[8], 71), 0),
        "block_table": jax.vmap(lambda own: jax.random.permutation(own, BLOCKS))(jax.random.split(splits[4], SEQS)).reshape((SEQS, BLOCKS)).astype(jnp.int32),
        "key_up": scatter_about(splits[5], (H, DNOPE, LAT), DNOPE ** -0.5, 0.5, ((0, 32),)),
        "value_up": scatter_about(splits[6], (H, LAT, DV), LAT ** -0.5, 0.25, ((0, 32),)),
        "grad_out": scatter_about(splits[7], (SEQS, Q, H, DV), 1.0, 6.0, ((0, 2), (1, 8), (2, 32))),
    }


softmax_scale = 192.0 ** -0.5


def head_terms(key_rows, key_pos, query_position, nope_rows, rope_rows, key_map, value_map, out_grad):
    query_latent = jnp.dot(nope_rows, key_map, preferred_element_type=jnp.float32).astype(jnp.bfloat16)
    query_rows = jnp.concatenate([query_latent, rope_rows], axis=1)
    scores = jnp.dot(query_rows, key_rows.T, preferred_element_type=jnp.float32) * softmax_scale
    visible = key_pos[None, :] <= query_position[:, None]
    scores = jnp.where(visible, scores, -jnp.inf)
    row_max = jnp.max(scores, axis=1, keepdims=True)
    weights = jnp.exp(scores - row_max)
    attn_probs = weights / jnp.sum(weights, axis=1, keepdims=True)
    probs_b = attn_probs.astype(jnp.bfloat16)
    value_rows = key_rows[:, :LAT]
    attn_out = jnp.dot(probs_b, value_rows, preferred_element_type=jnp.float32).astype(jnp.bfloat16)
    grad_latent = jnp.dot(out_grad, value_map.T, preferred_element_type=jnp.float32).astype(jnp.bfloat16)
    grad_probs = jnp.dot(grad_latent, value_rows.T, preferred_element_type=jnp.float32)
    row_delta = jnp.sum(attn_probs * grad_probs, axis=1, keepdims=True)
    grad_scores = (attn_probs * (grad_probs - row_delta) * softmax_scale).astype(jnp.bfloat16)
    grad_query = jnp.dot(grad_scores, key_rows, preferred_element_type=jnp.float32)
    grad_rope = grad_query[:, LAT:]
    grad_qlatent = grad_query[:, :LAT].astype(jnp.bfloat16)
    grad_nope = jnp.dot(grad_qlatent, key_map.T, preferred_element_type=jnp.float32)
    nope_blocks = nope_rows.astype(jnp.float32).reshape(N_CTX, Q_DEV, DNOPE)
    qlat_blocks = grad_qlatent.astype(jnp.float32).reshape(N_CTX, Q_DEV, LAT)
    key_part = jnp.einsum("bqn,bql->bnl", nope_blocks, qlat_blocks).astype(jnp.bfloat16)
    out_blocks = attn_out.astype(jnp.float32).reshape(N_CTX, Q_DEV, LAT)
    grad_blocks = out_grad.astype(jnp.float32).reshape(N_CTX, Q_DEV, DV)
    value_part = jnp.einsum("bql,bqv->blv", out_blocks, grad_blocks).astype(jnp.bfloat16)
    key_part = lax.optimization_barrier(key_part)
    value_part = lax.optimization_barrier(value_part)
    grad_keys = jnp.dot(grad_scores.T, query_rows, preferred_element_type=jnp.float32)
    grad_values = jnp.dot(probs_b.T, grad_latent, preferred_element_type=jnp.float32)
    grad_keys = grad_keys + jnp.pad(grad_values, ((0, 0), (0, ROPE)))
    key_total = jnp.sum(key_part.astype(jnp.float32), axis=0)
    value_total = jnp.sum(value_part.astype(jnp.float32), axis=0)
    return grad_nope, grad_rope, key_total, value_total, grad_keys


def reference(query_nope, query_rope, query_pos, latent_cache, block_table, key_up, value_up, grad_out):
    nope_list, rope_list, cache_list = [], [], []
    key_total = jnp.zeros((H, DNOPE, LAT), jnp.float32)
    value_total = jnp.zeros((H, LAT, DV), jnp.float32)
    key_pos = jnp.arange(KEYS, dtype=jnp.int32)
    for sequence in range(SEQS):
        slot_table = block_table[sequence].astype(jnp.int32)
        key_rows = latent_cache[sequence][slot_table].reshape(KEYS, LAT + ROPE)
        query_position = query_pos[sequence]

        def head_step(running, head_inputs):
            nope_rows, rope_rows, key_map, value_map, out_grad = head_inputs
            grad_nope, grad_rope, key_part, value_part, grad_keys = head_terms(
                key_rows, key_pos, query_position, nope_rows, rope_rows, key_map, value_map, out_grad)
            return running + grad_keys, (grad_nope, grad_rope, key_part, value_part)

        head_inputs = (jnp.swapaxes(query_nope[sequence], 0, 1), jnp.swapaxes(query_rope[sequence], 0, 1),
                       key_up, value_up, jnp.swapaxes(grad_out[sequence], 0, 1))
        grad_keys, (grad_nope, grad_rope, key_part, value_part) = lax.scan(
            head_step, jnp.zeros((KEYS, LAT + ROPE), jnp.float32), head_inputs)
        physical = jnp.zeros((BLOCKS, PAGE, LAT + ROPE), jnp.float32)
        physical = physical.at[slot_table].set(grad_keys.reshape(BLOCKS, PAGE, LAT + ROPE))
        nope_list.append(jnp.swapaxes(grad_nope, 0, 1))
        rope_list.append(jnp.swapaxes(grad_rope, 0, 1))
        cache_list.append(physical)
        key_total = key_total + key_part
        value_total = value_total + value_part
    return (jnp.stack(nope_list), jnp.stack(rope_list), jnp.stack(cache_list), key_total, value_total)
```

```python
import jax
import jax.numpy as jnp
from jax import lax
from jax.experimental import pallas as pl
from jax.experimental.pallas import tpu as pltpu
from jax.sharding import PartitionSpec as P

softmax_scale = 192.0 ** (-0.5)
MESH = pl.DeviceIdType.MESH
NY = 4
NZ = 16
f32 = jnp.float32
bf16 = jnp.bfloat16


class Copies:
    def __init__(self, send_sems, recv_sems):
        self.send_sems, self.recv_sems, self.made = send_sems, recv_sems, []

    def start(self, src, dst, device):
        at = len(self.made)
        copy = pltpu.make_async_remote_copy(
            src_ref=src,
            dst_ref=dst,
            send_sem=self.send_sems.at[at],
            recv_sem=self.recv_sems.at[at],
            device_id=device,
            device_id_type=MESH,
        )
        copy.start()
        self.made.append(copy)
        return copy

    def finish(self):
        for copy in self.made:
            copy.wait_send()


def entry_barrier(devices):
    barrier = pltpu.get_barrier_semaphore()
    for device in devices:
        pl.semaphore_signal(barrier, inc=1, device_id=device, device_id_type=MESH)
    pl.semaphore_wait(barrier, len(devices))


def total(*terms):
    terms = [term.astype(f32) for term in terms]
    result = terms[0]
    for term in terms[1:]:
        result = result + term
    return result


def gather_kernel(own_ref, all_ref, send_sems, recv_sems, own_sem):
    ctx = lax.axis_index("ctx")
    y, core = ctx // 2, ctx % 2

    def at(step, which):
        return {"ctx": lax.rem(y + step, NY) * 2 + which}

    def slot(step):
        return all_ref.at[lax.rem(y + step, NY) * 2 + core]

    ahead = 1 + 2 * core
    behind = 3 - 2 * core
    sibling = at(0, 1 - core)
    entry_barrier([sibling, at(1, core), at(3, core)])
    copies = Copies(send_sems, recv_sems)
    to_ahead = copies.start(own_ref, slot(0), at(ahead, core))
    to_behind = copies.start(own_ref, slot(0), at(behind, core))
    to_sibling = [copies.start(own_ref, slot(0), sibling)]
    keep = pltpu.make_async_copy(own_ref, slot(0), own_sem)
    keep.start()
    to_ahead.wait_recv()
    onward = copies.start(slot(behind), slot(behind), at(ahead, core))
    to_sibling.append(copies.start(slot(behind), slot(behind), sibling))
    to_behind.wait_recv()
    to_sibling.append(copies.start(slot(ahead), slot(ahead), sibling))
    onward.wait_recv()
    to_sibling.append(copies.start(slot(2), slot(2), sibling))
    for copy in to_sibling:
        copy.wait_recv()
    keep.wait()
    copies.finish()


def gather_rows(own_rows):
    rows, width = own_rows.shape
    return pl.pallas_call(
        gather_kernel,
        out_shape=jax.ShapeDtypeStruct((2 * NY, rows, width), bf16),
        in_specs=[pl.BlockSpec(memory_space=pltpu.VMEM)],
        out_specs=pl.BlockSpec(memory_space=pltpu.VMEM),
        scratch_shapes=[
            pltpu.SemaphoreType.DMA((7,)),
            pltpu.SemaphoreType.DMA((7,)),
            pltpu.SemaphoreType.DMA,
        ],
        compiler_params=pltpu.CompilerParams(collective_id=0, has_side_effects=True),
    )(own_rows)


def reduce_kernel(
    rows_ref, key_ref, value_ref,
    cache_ref, key_out, value_out,
    pair_rows, acc, ring_half, ring_in, block, z_in, piece, piece_in, final, done,
    pair_key, pair_value, key_acc, value_acc, key_half, value_half, key_in, value_in,
    key_sum, value_sum, key_far, value_far,
    send_sems, recv_sems,
):
    ctx = lax.axis_index("ctx")
    head = lax.axis_index("head")
    dp = lax.axis_index("dp")
    y, core = ctx // 2, ctx % 2
    z = lax.rem(head, NZ)
    x_lo = head // NZ
    chips = [lax.rem(y + step, NY) for step in range(NY)]
    sibling = {"ctx": y * 2 + 1 - core}
    up = {"ctx": chips[1] * 2 + core}
    down = {"ctx": chips[3] * 2 + core}
    z_at = [lax.rem(z + step, NZ) for step in range(NZ)]
    z_device = [{"head": x_lo * NZ + place} for place in z_at]
    x_pair = {"head": (1 - x_lo) * NZ + z}
    dp_pair = {"dp": 1 - dp}
    far_first = sorted(range(1, NZ), key=lambda step: -min(step, NZ - step))
    entry_barrier([sibling, up, down, x_pair, dp_pair] + [z_device[step] for step in far_first])
    copies = Copies(send_sems, recv_sems)

    pair = {}
    for step in (2, 1, 3, 0):
        pair[step] = copies.start(rows_ref.at[chips[step], 1 - core], pair_rows.at[step], sibling)
    pair_weights = [
        copies.start(key_ref.at[:, :, 1 - core], pair_key, sibling),
        copies.start(value_ref.at[:, :, 1 - core], pair_value, sibling),
    ]

    def join(step):
        pair[step].wait_recv()
        acc[step] = total(rows_ref[chips[step], core], pair_rows[step]).astype(bf16)

    join(2)
    up_far = copies.start(acc.at[2, 0], ring_half.at[0], up)
    down_far = copies.start(acc.at[2, 1], ring_half.at[1], down)
    join(1)
    up_own = copies.start(acc.at[1, 1], ring_in.at[0, 1], up)
    join(3)
    down_own = copies.start(acc.at[3, 0], ring_in.at[1, 0], down)
    join(0)
    up_far.wait_recv()
    acc[1, 0] = total(acc[1, 0], ring_half[0]).astype(bf16)
    up_both = copies.start(acc.at[1, 0], ring_in.at[0, 0], up)
    down_far.wait_recv()
    acc[3, 1] = total(acc[3, 1], ring_half[1]).astype(bf16)
    down_both = copies.start(acc.at[3, 1], ring_in.at[1, 1], down)

    for copy in pair_weights:
        copy.wait_recv()
    for step in range(NY):
        key_acc[step] = total(key_ref[:, chips[step], core], pair_key[:, chips[step]]).astype(bf16)
        value_acc[step] = total(value_ref[:, chips[step], core], pair_value[:, chips[step]]).astype(bf16)
    low, high = pl.ds(0, 2), pl.ds(2, 2)
    weights_far = [
        copies.start(key_acc.at[2, low], key_half.at[0], up),
        copies.start(value_acc.at[2, low], value_half.at[0], up),
        copies.start(key_acc.at[2, high], key_half.at[1], down),
        copies.start(value_acc.at[2, high], value_half.at[1], down),
    ]
    weights_in = [
        copies.start(key_acc.at[1, high], key_in.at[0, high], up),
        copies.start(value_acc.at[1, high], value_in.at[0, high], up),
        copies.start(key_acc.at[3, low], key_in.at[1, low], down),
        copies.start(value_acc.at[3, low], value_in.at[1, low], down),
    ]

    for copy in (up_own, down_own, up_both, down_both):
        copy.wait_recv()
    block[...] = total(acc[0], ring_in[0], ring_in[1]).astype(bf16).reshape(block.shape)
    scatter = [copies.start(block.at[z_at[step]], z_in.at[step], z_device[step]) for step in far_first]

    for copy in weights_far:
        copy.wait_recv()
    key_acc[1, low] = total(key_acc[1, low], key_half[0]).astype(bf16)
    value_acc[1, low] = total(value_acc[1, low], value_half[0]).astype(bf16)
    key_acc[3, high] = total(key_acc[3, high], key_half[1]).astype(bf16)
    value_acc[3, high] = total(value_acc[3, high], value_half[1]).astype(bf16)
    weights_in += [
        copies.start(key_acc.at[1, low], key_in.at[0, low], up),
        copies.start(value_acc.at[1, low], value_in.at[0, low], up),
        copies.start(key_acc.at[3, high], key_in.at[1, high], down),
        copies.start(value_acc.at[3, high], value_in.at[1, high], down),
    ]

    for copy in scatter:
        copy.wait_recv()
    piece[...] = total(block[z], *[z_in[step] for step in range(1, NZ)]).astype(bf16)
    across = copies.start(piece, piece_in, x_pair)

    for copy in weights_in:
        copy.wait_recv()
    key_sum[...] = total(key_acc[0], key_in[0], key_in[1]).astype(bf16)
    value_sum[...] = total(value_acc[0], value_in[0], value_in[1]).astype(bf16)
    weights_pair = [
        copies.start(key_sum.at[:, 1 - dp], key_far, dp_pair),
        copies.start(value_sum.at[:, 1 - dp], value_far, dp_pair),
    ]

    across.wait_recv()
    done[...] = total(piece[...], piece_in[...]).astype(bf16)
    final[z] = done[...]
    gather = [copies.start(done, final.at[z], z_device[step]) for step in far_first]

    for copy in weights_pair:
        copy.wait_recv()
    key_out[...] = total(key_sum[:, dp], key_far[...])
    value_out[...] = total(value_sum[:, dp], value_far[...])
    for copy in gather:
        copy.wait_recv()
    cache_ref[...] = final[...].astype(f32)
    copies.finish()


def reduce_all(grad_rows, key_part, value_part):
    width = grad_rows.shape[1]
    heads, nope, latent = key_part.shape
    values = value_part.shape[2]
    rows = grad_rows.reshape(NY, 2, 2, 64, width)
    keys = key_part.reshape(heads, NY, 2, 2, nope // 16, latent)
    vals = value_part.reshape(heads, NY, 2, 2, latent // 16, values)
    key_piece = (heads, 2, nope // 16, latent)
    value_piece = (heads, 2, latent // 16, values)
    half_key = (heads // 2,) + key_piece[1:]
    half_value = (heads // 2,) + value_piece[1:]
    n_copies = 4 + 2 + 6 + 8 + 4 + 15 + 1 + 2 + 15
    vmem = pl.BlockSpec(memory_space=pltpu.VMEM)
    cache, key_map, value_map = pl.pallas_call(
        reduce_kernel,
        out_shape=(
            jax.ShapeDtypeStruct((NZ, 8, width), f32),
            jax.ShapeDtypeStruct((heads, nope // 16, latent), f32),
            jax.ShapeDtypeStruct((heads, latent // 16, values), f32),
        ),
        in_specs=[vmem] * 3,
        out_specs=(vmem,) * 3,
        scratch_shapes=[
            pltpu.VMEM((NY, 2, 64, width), bf16),
            pltpu.VMEM((NY, 2, 64, width), bf16),
            pltpu.VMEM((2, 64, width), bf16),
            pltpu.VMEM((2, 2, 64, width), bf16),
            pltpu.VMEM((NZ, 8, width), bf16),
            pltpu.VMEM((NZ, 8, width), bf16),
            pltpu.VMEM((8, width), bf16),
            pltpu.VMEM((8, width), bf16),
            pltpu.VMEM((NZ, 8, width), bf16),
            pltpu.VMEM((8, width), bf16),
            pltpu.VMEM((heads, NY) + key_piece[1:], bf16),
            pltpu.VMEM((heads, NY) + value_piece[1:], bf16),
            pltpu.VMEM((NY,) + key_piece, bf16),
            pltpu.VMEM((NY,) + value_piece, bf16),
            pltpu.VMEM((2,) + half_key, bf16),
            pltpu.VMEM((2,) + half_value, bf16),
            pltpu.VMEM((2,) + key_piece, bf16),
            pltpu.VMEM((2,) + value_piece, bf16),
            pltpu.VMEM(key_piece, bf16),
            pltpu.VMEM(value_piece, bf16),
            pltpu.VMEM((heads, nope // 16, latent), bf16),
            pltpu.VMEM((heads, latent // 16, values), bf16),
            pltpu.SemaphoreType.DMA((n_copies,)),
            pltpu.SemaphoreType.DMA((n_copies,)),
        ],
        compiler_params=pltpu.CompilerParams(collective_id=1, has_side_effects=True),
    )(rows, keys, vals)
    return cache, key_map, value_map


def on_device(
    query_nope, query_rope, query_pos, latent_cache, block_table, key_up, value_up, grad_out
):
    latent_width = key_up.shape[2]
    page_rows = latent_cache.shape[2]
    row_width = latent_cache.shape[3]
    own_rows = latent_cache[0].reshape(-1, row_width)
    key_block = gather_rows(own_rows).reshape(-1, row_width)
    query_latent = jnp.einsum(
        "qhn,hnl->hql", query_nope[0], key_up, preferred_element_type=f32
    ).astype(bf16)
    query_rows = jnp.concatenate([query_latent, jnp.swapaxes(query_rope[0], 0, 1)], axis=2)
    grad_latent = jnp.einsum(
        "qhv,hlv->hql", grad_out[0], value_up, preferred_element_type=f32
    ).astype(bf16)
    query_position = query_pos[0]
    slot_table = block_table[0]

    row_index = jnp.arange(key_block.shape[0], dtype=jnp.int32)
    logical = jnp.sum(
        jnp.where(
            slot_table[None, :] == (row_index // page_rows)[:, None],
            jnp.arange(slot_table.shape[0], dtype=jnp.int32)[None, :],
            0,
        ),
        axis=1,
    )
    position = logical * page_rows + row_index % page_rows
    scores = (
        jnp.einsum("hqc,kc->hqk", query_rows, key_block, preferred_element_type=f32)
        * softmax_scale
    )
    visible = position[None, None, :] <= query_position[None, :, None]
    scores = jnp.where(visible, scores, -jnp.inf)
    grad_probs = jnp.einsum(
        "hql,kl->hqk", grad_latent, key_block[:, :latent_width], preferred_element_type=f32
    )
    weights = jnp.exp(scores - jnp.max(scores, axis=2, keepdims=True))
    denominator = jnp.sum(weights, axis=2, keepdims=True)
    row_delta = jnp.sum(weights * grad_probs, axis=2, keepdims=True) / denominator
    attn_probs = weights / denominator
    probs_b = attn_probs.astype(bf16)
    grad_scores = (attn_probs * (grad_probs - row_delta) * softmax_scale).astype(bf16)
    grad_rows = jnp.einsum("hqk,hqc->kc", grad_scores, query_rows, preferred_element_type=f32)
    grad_values = jnp.einsum("hqk,hql->kl", probs_b, grad_latent, preferred_element_type=f32)
    grad_rows = grad_rows + jnp.pad(grad_values, ((0, 0), (0, row_width - latent_width)))
    grad_query = jnp.einsum("hqk,kc->hqc", grad_scores, key_block, preferred_element_type=f32)
    attn_out = jnp.einsum(
        "hqk,kl->hql", probs_b, key_block[:, :latent_width], preferred_element_type=f32
    ).astype(bf16)
    grad_rope = jnp.swapaxes(grad_query[..., latent_width:], 0, 1)[None]
    grad_qlatent = grad_query[..., :latent_width].astype(bf16)
    grad_nope = jnp.einsum("hql,hnl->qhn", grad_qlatent, key_up, preferred_element_type=f32)[None]
    key_part = jnp.einsum(
        "qhn,hql->hnl", query_nope[0], grad_qlatent, preferred_element_type=f32
    ).astype(bf16)
    value_part = jnp.einsum(
        "hql,qhv->hlv", attn_out, grad_out[0], preferred_element_type=f32
    ).astype(bf16)
    cache_grad, grad_key_map, grad_value_map = reduce_all(
        grad_rows.astype(bf16), key_part, value_part
    )
    return (
        grad_nope,
        grad_rope,
        cache_grad.reshape(latent_cache.shape),
        grad_key_map,
        grad_value_map,
    )


def solution(mesh):
    placed = (
        P("dp", "ctx", "head", None),
        P("dp", "ctx", "head", None),
        P("dp", "ctx"),
        P("dp", "ctx", None, None),
        P("dp", None),
        P("head", None, None),
        P("head", None, None),
        P("dp", "ctx", "head", None),
    )
    return jax.shard_map(
        on_device,
        mesh=mesh,
        in_specs=placed,
        out_specs=(
            P("dp", "ctx", "head", None),
            P("dp", "ctx", "head", None),
            P("dp", "ctx", None, None),
            P("head", ("ctx", "dp"), None),
            P("head", ("ctx", "dp"), None),
        ),
        check_vma=False,
    )
```

```python
import jax
import jax.numpy as jnp
from jax import lax
from jax.experimental import pallas as pl
from jax.experimental.pallas import tpu as pltpu
from jax.sharding import PartitionSpec as P

softmax_scale = 192.0 ** (-0.5)
MESH = pl.DeviceIdType.MESH
NY = 4
NZ = 16
HEADS = 4
f32 = jnp.float32
bf16 = jnp.bfloat16


class Copies:
    def __init__(self, send_sems, recv_sems):
        self.send_sems, self.recv_sems, self.made = send_sems, recv_sems, []

    def start(self, src, dst, device):
        at = len(self.made)
        copy = pltpu.make_async_remote_copy(
            src_ref=src,
            dst_ref=dst,
            send_sem=self.send_sems.at[at],
            recv_sem=self.recv_sems.at[at],
            device_id=device,
            device_id_type=MESH,
        )
        copy.start()
        self.made.append(copy)
        return copy

    def finish(self):
        for copy in self.made:
            copy.wait_send()


def entry_barrier(devices):
    barrier = pltpu.get_barrier_semaphore()
    for device in devices:
        pl.semaphore_signal(barrier, inc=1, device_id=device, device_id_type=MESH)
    pl.semaphore_wait(barrier, len(devices))


def total(*terms):
    terms = [term.astype(f32) for term in terms]
    result = terms[0]
    for term in terms[1:]:
        result = result + term
    return result


def dot(a, b, a_dim, b_dim):
    return lax.dot_general(a, b, (((a_dim,), (b_dim,)), ((), ())), preferred_element_type=f32)


def iota(shape, dim):
    return lax.broadcasted_iota(jnp.int32, shape, dim)


def one_head(values, head):
    return jnp.where(lax.rem(iota(values.shape, 0), HEADS) == head, values.astype(f32), 0.0).astype(bf16)


def gather_kernel(
    own_ref, nope_ref, grad_ref, rope_ref, key_up_ref, value_up_ref,
    all_ref, query_ref, latent_ref,
    send_sems, recv_sems, own_sem,
):
    ctx = lax.axis_index("ctx")
    y, core = ctx // 2, ctx % 2

    def at(step, which):
        return {"ctx": lax.rem(y + step, NY) * 2 + which}

    def slot(step):
        return all_ref.at[lax.rem(y + step, NY) * 2 + core]

    ahead = 1 + 2 * core
    behind = 3 - 2 * core
    sibling = at(0, 1 - core)
    entry_barrier([sibling, at(1, core), at(3, core)])
    copies = Copies(send_sems, recv_sems)
    to_ahead = copies.start(own_ref, slot(0), at(ahead, core))
    to_behind = copies.start(own_ref, slot(0), at(behind, core))
    to_sibling = [copies.start(own_ref, slot(0), sibling)]
    keep = pltpu.make_async_copy(own_ref, slot(0), own_sem)
    keep.start()

    latent = key_up_ref.shape[2]
    rope = rope_ref.shape[0] // HEADS

    @pl.loop(0, nope_ref.shape[0] // 128)
    def _(step):
        rows = pl.ds(step * 128, 128)
        nope, grad = nope_ref[rows, :], grad_ref[rows, :]
        spread = jnp.concatenate([one_head(nope, head) for head in range(HEADS)], axis=1)
        up = key_up_ref[...].reshape(spread.shape[1], latent)
        query_ref[rows, :latent] = dot(spread, up, 1, 0).astype(bf16)
        latent_ref[rows, :] = total(
            *[dot(one_head(grad, head), value_up_ref[head], 1, 1) for head in range(HEADS)]
        ).astype(bf16)
        query = (iota((128, 128), 0) + step * 128) // HEADS
        pick = (iota((128, 128), 1) == query).astype(f32).astype(bf16)
        every = dot(pick, rope_ref[...], 1, 1)
        shape = every.shape
        mine = iota(shape, 1) // rope == lax.rem(iota(shape, 0), HEADS)
        fold = (lax.rem(iota((shape[1], rope), 0), rope) == iota((shape[1], rope), 1)).astype(f32).astype(bf16)
        query_ref[rows, latent:] = dot(jnp.where(mine, every, 0.0).astype(bf16), fold, 1, 0).astype(bf16)

    to_ahead.wait_recv()
    onward = copies.start(slot(behind), slot(behind), at(ahead, core))
    to_sibling.append(copies.start(slot(behind), slot(behind), sibling))
    to_behind.wait_recv()
    to_sibling.append(copies.start(slot(ahead), slot(ahead), sibling))
    onward.wait_recv()
    to_sibling.append(copies.start(slot(2), slot(2), sibling))
    for copy in to_sibling:
        copy.wait_recv()
    keep.wait()
    copies.finish()


def gather_and_project(own_rows, nope, grad, rope, key_up, value_up):
    rows, width = own_rows.shape
    latent = key_up.shape[2]
    vmem = pl.BlockSpec(memory_space=pltpu.VMEM)
    return pl.pallas_call(
        gather_kernel,
        out_shape=(
            jax.ShapeDtypeStruct((2 * NY, rows, width), bf16),
            jax.ShapeDtypeStruct((nope.shape[0], width), bf16),
            jax.ShapeDtypeStruct((nope.shape[0], latent), bf16),
        ),
        in_specs=[vmem] * 6,
        out_specs=(vmem,) * 3,
        scratch_shapes=[
            pltpu.SemaphoreType.DMA((7,)),
            pltpu.SemaphoreType.DMA((7,)),
            pltpu.SemaphoreType.DMA,
        ],
        compiler_params=pltpu.CompilerParams(collective_id=0, has_side_effects=True),
    )(own_rows, nope, grad, rope, key_up, value_up)


def main_kernel(
    table_ref, pos_ref, keys_ref, query_ref, latent_ref, nope_ref, grad_ref, key_up_ref,
    nope_out, rope_out, cache_ref, key_out, value_out,
    key_pos, scores, grad_probs, score_t, prob_t, query_grad, rope_parts, out_t,
    rows_out, pair_rows, acc, ring_half, ring_in, block, z_in, piece, piece_in, final, done,
    key_part, value_part,
    pair_key, pair_value, key_acc, value_acc, key_half, value_half, key_in, value_in,
    key_sum, value_sum, key_far, value_far,
    send_sems, recv_sems,
):
    ctx = lax.axis_index("ctx")
    head = lax.axis_index("head")
    dp = lax.axis_index("dp")
    y, core = ctx // 2, ctx % 2
    z = lax.rem(head, NZ)
    x_lo = head // NZ
    chips = [lax.rem(y + step, NY) for step in range(NY)]
    sibling = {"ctx": y * 2 + 1 - core}
    up = {"ctx": chips[1] * 2 + core}
    down = {"ctx": chips[3] * 2 + core}
    z_at = [lax.rem(z + step, NZ) for step in range(NZ)]
    z_device = [{"head": x_lo * NZ + place} for place in z_at]
    x_pair = {"head": (1 - x_lo) * NZ + z}
    dp_pair = {"dp": 1 - dp}
    far_first = sorted(range(1, NZ), key=lambda step: -min(step, NZ - step))
    friends = [z_device[step] for step in far_first] + [x_pair, dp_pair, up, down, sibling]
    barrier = pltpu.get_barrier_semaphore()
    for device in friends:
        pl.semaphore_signal(barrier, inc=1, device_id=device, device_id_type=MESH)

    blocks = table_ref.shape[1]
    page = keys_ref.shape[0] // blocks
    lanes = key_pos.shape[1]
    for slot in range(blocks):
        start = sum(jnp.where(table_ref[0, at] == slot, at * page, 0) for at in range(blocks))
        key_pos[slot * page:(slot + 1) * page, :] = (iota((page, lanes), 0) + start).astype(f32)
    count = query_ref.shape[0]
    spread = (iota((count // HEADS, count), 0) == iota((count // HEADS, count), 1) // HEADS).astype(f32).astype(bf16)
    pos = jnp.broadcast_to(pos_ref[...], (8, count // HEADS))
    pos_high, pos_low = pos // 32, lax.rem(pos, 32)
    query_pos = (
        dot(pos_high.astype(f32).astype(bf16), spread, 1, 0) * 32.0
        + dot(pos_low.astype(f32).astype(bf16), spread, 1, 0)
    )
    latent = latent_ref.shape[1]
    width = keys_ref.shape[1]
    n_keys = keys_ref.shape[0]
    chunk = 256
    n_chunks = n_keys // chunk

    for part in range(count // lanes):
        mine = slice(part * lanes, (part + 1) * lanes)
        at_pos = query_pos[0:1, mine]

        def score_step(step, row_max):
            rows = pl.ds(step * chunk, chunk)
            raw = dot(keys_ref[rows, :], query_ref[mine, :], 1, 1) * softmax_scale
            raw = jnp.where(key_pos[rows, :] <= at_pos, raw, -jnp.inf)
            scores[rows, :] = raw
            grad_probs[rows, :] = dot(keys_ref[rows, :latent], latent_ref[mine, :], 1, 1)
            return jnp.maximum(row_max, jnp.max(raw, axis=0, keepdims=True))

        row_max = lax.fori_loop(0, n_chunks, score_step, jnp.full((1, lanes), -jnp.inf, f32))

        def weight_step(step, sums):
            rows = pl.ds(step * chunk, chunk)
            weights = jnp.exp(scores[rows, :] - row_max)
            scores[rows, :] = weights
            return (
                sums[0] + jnp.sum(weights, axis=0, keepdims=True),
                sums[1] + jnp.sum(weights * grad_probs[rows, :], axis=0, keepdims=True),
            )

        zero = jnp.zeros((1, lanes), f32)
        denominator, weighted = lax.fori_loop(0, n_chunks, weight_step, (zero, zero))
        scale = 1.0 / denominator
        row_delta = weighted * scale

        def grad_step(step, carry):
            rows = pl.ds(step * chunk, chunk)
            probs = scores[rows, :] * scale
            prob_t[rows, mine] = probs.astype(bf16)
            score_t[rows, mine] = (probs * (grad_probs[rows, :] - row_delta) * softmax_scale).astype(bf16)
            return carry

        lax.fori_loop(0, n_chunks, grad_step, 0)

    pl.semaphore_wait(barrier, len(friends))
    copies = Copies(send_sems, recv_sems)

    def grad_rows(chip, which):
        rows = pl.ds(pl.multiple_of((chip * 2 + which) * 128, 128), 128)
        by_score = dot(score_t[rows, :], query_ref[...], 1, 0)
        by_prob = dot(prob_t[rows, :], latent_ref[...], 1, 0)
        return by_score[:, :latent] + by_prob, by_score[:, latent:]

    pair = {}
    for step in (2, 1, 3, 0):
        low, high = grad_rows(chips[step], 1 - core)
        rows_out[step, :, :, :latent] = low.astype(bf16).reshape(2, 64, latent)
        rows_out[step, :, :, latent:] = high.astype(bf16).reshape(2, 64, width - latent)
        pair[step] = copies.start(rows_out.at[step], pair_rows.at[step], sibling)

    def join(step):
        low, high = grad_rows(chips[step], core)
        pair[step].wait_recv()
        acc[step, :, :, :latent] = total(low.reshape(2, 64, latent), pair_rows[step, :, :, :latent]).astype(bf16)
        acc[step, :, :, latent:] = total(
            high.reshape(2, 64, width - latent), pair_rows[step, :, :, latent:]
        ).astype(bf16)

    join(2)
    up_far = copies.start(acc.at[2, 0], ring_half.at[0], up)
    down_far = copies.start(acc.at[2, 1], ring_half.at[1], down)
    join(1)
    up_own = copies.start(acc.at[1, 1], ring_in.at[0, 1], up)
    join(3)
    down_own = copies.start(acc.at[3, 0], ring_in.at[1, 0], down)
    join(0)
    up_far.wait_recv()
    acc[1, 0] = total(acc[1, 0], ring_half[0]).astype(bf16)
    up_both = copies.start(acc.at[1, 0], ring_in.at[0, 0], up)
    down_far.wait_recv()
    acc[3, 1] = total(acc[3, 1], ring_half[1]).astype(bf16)
    down_both = copies.start(acc.at[3, 1], ring_in.at[1, 1], down)

    @pl.loop(0, count // 128)
    def _(step):
        lane = pl.ds(pl.multiple_of(step * 128, 128), 128)
        grad = dot(score_t[:, lane], keys_ref[...], 0, 0)
        query_grad[lane, :] = grad[:, :latent].astype(bf16)
        rope_high = grad[:, latent:].astype(bf16)
        rope_parts[lane, :width - latent] = rope_high
        rope_parts[lane, width - latent:] = (grad[:, latent:] - rope_high.astype(f32)).astype(bf16)

    for copy in (up_own, down_own, up_both, down_both):
        copy.wait_recv()
    block[...] = total(acc[0], ring_in[0], ring_in[1]).astype(bf16).reshape(block.shape)
    scatter = [copies.start(block.at[z_at[step]], z_in.at[step], z_device[step]) for step in far_first]

    @pl.loop(0, HEADS)
    def _(at):
        part = dot(one_head(nope_ref[...], at), query_grad[...], 0, 0)
        key_part[at] = part.astype(bf16).reshape(key_part.shape[1:])

    pair_weights = [copies.start(key_part.at[:, :, 1 - core], pair_key, sibling)]

    @pl.loop(0, latent // 128)
    def _(step):
        lane = pl.ds(pl.multiple_of(step * 128, 128), 128)
        out_t[lane, :] = dot(keys_ref[:, lane], prob_t[...], 0, 0).astype(bf16)

    @pl.loop(0, HEADS)
    def _(at):
        part = dot(out_t[...], one_head(grad_ref[...], at), 1, 0)
        value_part[at] = part.astype(bf16).reshape(value_part.shape[1:])

    pair_weights.append(copies.start(value_part.at[:, :, 1 - core], pair_value, sibling))

    @pl.loop(0, count // 128)
    def _(step):
        rows = pl.ds(step * 128, 128)
        every = dot(query_grad[rows, :], key_up_ref[...].reshape(-1, latent), 1, 1)
        n = nope_out.shape[1]
        which = lax.rem(iota((128, n), 0), HEADS)
        nope_out[rows, :] = total(
            *[jnp.where(which == at, every[:, at * n:(at + 1) * n], 0.0) for at in range(HEADS)]
        )

    rope = width - latent
    queries = count // HEADS
    for at in range(HEADS):
        order = (iota((count, queries), 0) == iota((count, queries), 1) * HEADS + at).astype(f32).astype(bf16)
        turned = dot(rope_parts[...], order, 0, 0)
        rope_out[at * rope:(at + 1) * rope, :] = turned[:rope] + turned[rope:]

    for copy in pair_weights:
        copy.wait_recv()
    for step in range(NY):
        key_acc[step] = total(key_part[:, chips[step], core], pair_key[:, chips[step]]).astype(bf16)
        value_acc[step] = total(value_part[:, chips[step], core], pair_value[:, chips[step]]).astype(bf16)
    low, high = pl.ds(0, 2), pl.ds(2, 2)
    weights_far = [
        copies.start(key_acc.at[2, low], key_half.at[0], up),
        copies.start(value_acc.at[2, low], value_half.at[0], up),
        copies.start(key_acc.at[2, high], key_half.at[1], down),
        copies.start(value_acc.at[2, high], value_half.at[1], down),
    ]
    weights_in = [
        copies.start(key_acc.at[1, high], key_in.at[0, high], up),
        copies.start(value_acc.at[1, high], value_in.at[0, high], up),
        copies.start(key_acc.at[3, low], key_in.at[1, low], down),
        copies.start(value_acc.at[3, low], value_in.at[1, low], down),
    ]
    for copy in weights_far:
        copy.wait_recv()
    key_acc[1, low] = total(key_acc[1, low], key_half[0]).astype(bf16)
    value_acc[1, low] = total(value_acc[1, low], value_half[0]).astype(bf16)
    key_acc[3, high] = total(key_acc[3, high], key_half[1]).astype(bf16)
    value_acc[3, high] = total(value_acc[3, high], value_half[1]).astype(bf16)
    weights_in += [
        copies.start(key_acc.at[1, low], key_in.at[0, low], up),
        copies.start(value_acc.at[1, low], value_in.at[0, low], up),
        copies.start(key_acc.at[3, high], key_in.at[1, high], down),
        copies.start(value_acc.at[3, high], value_in.at[1, high], down),
    ]

    for copy in scatter:
        copy.wait_recv()
    piece[...] = total(block[z], *[z_in[step] for step in range(1, NZ)]).astype(bf16)
    across = copies.start(piece, piece_in, x_pair)
    across.wait_recv()
    done[...] = total(piece[...], piece_in[...]).astype(bf16)
    final[z] = done[...]
    gather = [copies.start(done, final.at[z], z_device[step]) for step in far_first]

    for copy in weights_in:
        copy.wait_recv()
    key_sum[...] = total(key_acc[0], key_in[0], key_in[1]).astype(bf16)
    value_sum[...] = total(value_acc[0], value_in[0], value_in[1]).astype(bf16)
    weights_pair = [
        copies.start(key_sum.at[:, 1 - dp], key_far, dp_pair),
        copies.start(value_sum.at[:, 1 - dp], value_far, dp_pair),
    ]
    for copy in weights_pair:
        copy.wait_recv()
    key_out[...] = total(key_sum[:, dp], key_far[...])
    value_out[...] = total(value_sum[:, dp], value_far[...])
    for copy in gather:
        copy.wait_recv()
    cache_ref[...] = final[...].astype(f32)
    copies.finish()


def attend_and_reduce(table, pos, keys, query_rows, grad_latent, nope, grad, key_up):
    n_keys, width = keys.shape
    count, n_nope = nope.shape
    heads, _, latent = key_up.shape
    values = grad.shape[1]
    key_piece = (heads, 2, n_nope // 16, latent)
    value_piece = (heads, 2, latent // 16, values)
    half_key = (heads // 2,) + key_piece[1:]
    half_value = (heads // 2,) + value_piece[1:]
    n_copies = 4 + 2 + 6 + 8 + 4 + 15 + 1 + 2 + 15
    vmem = pl.BlockSpec(memory_space=pltpu.VMEM)
    return pl.pallas_call(
        main_kernel,
        out_shape=(
            jax.ShapeDtypeStruct((count, n_nope), f32),
            jax.ShapeDtypeStruct((heads * (width - latent), count // heads), f32),
            jax.ShapeDtypeStruct((NZ, 8, width), f32),
            jax.ShapeDtypeStruct((heads, n_nope // 16, latent), f32),
            jax.ShapeDtypeStruct((heads, latent // 16, values), f32),
        ),
        in_specs=[pl.BlockSpec(memory_space=pltpu.SMEM)] + [vmem] * 7,
        out_specs=(vmem,) * 5,
        scratch_shapes=[
            pltpu.VMEM((n_keys, 256), f32),
            pltpu.VMEM((n_keys, 256), f32),
            pltpu.VMEM((n_keys, 256), f32),
            pltpu.VMEM((n_keys, count), bf16),
            pltpu.VMEM((n_keys, count), bf16),
            pltpu.VMEM((count, latent), bf16),
            pltpu.VMEM((count, 2 * (width - latent)), bf16),
            pltpu.VMEM((latent, count), bf16),
            pltpu.VMEM((NY, 2, 64, width), bf16),
            pltpu.VMEM((NY, 2, 64, width), bf16),
            pltpu.VMEM((NY, 2, 64, width), bf16),
            pltpu.VMEM((2, 64, width), bf16),
            pltpu.VMEM((2, 2, 64, width), bf16),
            pltpu.VMEM((NZ, 8, width), bf16),
            pltpu.VMEM((NZ, 8, width), bf16),
            pltpu.VMEM((8, width), bf16),
            pltpu.VMEM((8, width), bf16),
            pltpu.VMEM((NZ, 8, width), bf16),
            pltpu.VMEM((8, width), bf16),
            pltpu.VMEM((heads, NY, 2) + key_piece[1:], bf16),
            pltpu.VMEM((heads, NY, 2) + value_piece[1:], bf16),
            pltpu.VMEM((heads, NY) + key_piece[1:], bf16),
            pltpu.VMEM((heads, NY) + value_piece[1:], bf16),
            pltpu.VMEM((NY,) + key_piece, bf16),
            pltpu.VMEM((NY,) + value_piece, bf16),
            pltpu.VMEM((2,) + half_key, bf16),
            pltpu.VMEM((2,) + half_value, bf16),
            pltpu.VMEM((2,) + key_piece, bf16),
            pltpu.VMEM((2,) + value_piece, bf16),
            pltpu.VMEM(key_piece, bf16),
            pltpu.VMEM(value_piece, bf16),
            pltpu.VMEM((heads, n_nope // 16, latent), bf16),
            pltpu.VMEM((heads, latent // 16, values), bf16),
            pltpu.SemaphoreType.DMA((n_copies,)),
            pltpu.SemaphoreType.DMA((n_copies,)),
        ],
        compiler_params=pltpu.CompilerParams(collective_id=1, has_side_effects=True),
    )(table, pos, keys, query_rows, grad_latent, nope, grad, key_up)


def on_device(
    query_nope, query_rope, query_pos, latent_cache, block_table, key_up, value_up, grad_out
):
    row_width = latent_cache.shape[3]
    nope = query_nope.reshape(-1, query_nope.shape[3])
    grad = grad_out.reshape(-1, grad_out.shape[3])
    rope = jnp.transpose(query_rope[0], (1, 2, 0))
    heads, rope_width, queries = rope.shape
    own_rows = latent_cache.reshape(-1, row_width)
    keys, query_rows, grad_latent = gather_and_project(
        own_rows, nope, grad, rope.reshape(-1, queries), key_up, value_up
    )
    grad_nope, grad_rope, cache_grad, grad_key_map, grad_value_map = attend_and_reduce(
        block_table, query_pos, keys.reshape(-1, row_width), query_rows, grad_latent, nope, grad, key_up
    )
    return (
        grad_nope.reshape(query_nope.shape),
        jnp.transpose(grad_rope.reshape(heads, rope_width, queries), (2, 0, 1))[None],
        cache_grad.reshape(latent_cache.shape),
        grad_key_map,
        grad_value_map,
    )


def solution(mesh):
    placed = (
        P("dp", "ctx", "head", None),
        P("dp", "ctx", "head", None),
        P("dp", "ctx"),
        P("dp", "ctx", None, None),
        P("dp", None),
        P("head", None, None),
        P("head", None, None),
        P("dp", "ctx", "head", None),
    )
    return jax.shard_map(
        on_device,
        mesh=mesh,
        in_specs=placed,
        out_specs=(
            P("dp", "ctx", "head", None),
            P("dp", "ctx", "head", None),
            P("dp", "ctx", None, None),
            P("head", ("ctx", "dp"), None),
            P("head", ("ctx", "dp"), None),
        ),
        check_vma=False,
    )
```

```python
import jax
import jax.numpy as jnp
from jax import lax
from jax.experimental import pallas as pl
from jax.experimental.pallas import tpu as pltpu
from jax.sharding import PartitionSpec as P

softmax_scale = 192.0 ** (-0.5)
MESH = pl.DeviceIdType.MESH
NY = 4
NZ = 16
HEADS = 4
f32 = jnp.float32
bf16 = jnp.bfloat16


class Copies:
    def __init__(self, send_sems, recv_sems):
        self.send_sems, self.recv_sems, self.made = send_sems, recv_sems, []

    def start(self, src, dst, device):
        at = len(self.made)
        copy = pltpu.make_async_remote_copy(
            src_ref=src,
            dst_ref=dst,
            send_sem=self.send_sems.at[at],
            recv_sem=self.recv_sems.at[at],
            device_id=device,
            device_id_type=MESH,
        )
        copy.start()
        self.made.append(copy)
        return copy

    def finish(self):
        for copy in self.made:
            copy.wait_send()


def entry_barrier(devices):
    barrier = pltpu.get_barrier_semaphore()
    for device in devices:
        pl.semaphore_signal(barrier, inc=1, device_id=device, device_id_type=MESH)
    pl.semaphore_wait(barrier, len(devices))


def total(*terms):
    terms = [term.astype(f32) for term in terms]
    result = terms[0]
    for term in terms[1:]:
        result = result + term
    return result


def dot(a, b, a_dim, b_dim):
    return lax.dot_general(a, b, (((a_dim,), (b_dim,)), ((), ())), preferred_element_type=f32)


def iota(shape, dim):
    return lax.broadcasted_iota(jnp.int32, shape, dim)


def one_head(values, head):
    return jnp.where(lax.rem(iota(values.shape, 0), HEADS) == head, values.astype(f32), 0.0).astype(bf16)


def gather_kernel(
    own_ref, nope_ref, grad_ref, rope_ref, key_up_ref, value_up_ref,
    all_ref, query_ref, latent_ref,
    send_sems, recv_sems, own_sem,
):
    ctx = lax.axis_index("ctx")
    y, core = ctx // 2, ctx % 2
    rows_each = own_ref.shape[0]

    def at(step, which):
        return {"ctx": lax.rem(y + step, NY) * 2 + which}

    def slot(step):
        place = (lax.rem(y + step, NY) * 2 + core) * rows_each
        return all_ref.at[pl.ds(pl.multiple_of(place, rows_each), rows_each)]

    ahead = 1 + 2 * core
    behind = 3 - 2 * core
    sibling = at(0, 1 - core)
    entry_barrier([sibling, at(1, core), at(3, core)])
    copies = Copies(send_sems, recv_sems)
    to_ahead = copies.start(own_ref, slot(0), at(ahead, core))
    to_behind = copies.start(own_ref, slot(0), at(behind, core))
    to_sibling = [copies.start(own_ref, slot(0), sibling)]
    keep = pltpu.make_async_copy(own_ref, slot(0), own_sem)
    keep.start()

    latent = key_up_ref.shape[2]
    rope = rope_ref.shape[0] // HEADS

    @pl.loop(0, nope_ref.shape[0] // 128)
    def _(step):
        rows = pl.ds(step * 128, 128)
        nope, grad = nope_ref[rows, :], grad_ref[rows, :]
        spread = jnp.concatenate([one_head(nope, head) for head in range(HEADS)], axis=1)
        up = key_up_ref[...].reshape(spread.shape[1], latent)
        query_ref[rows, :latent] = dot(spread, up, 1, 0).astype(bf16)
        latent_ref[rows, :] = total(
            *[dot(one_head(grad, head), value_up_ref[head], 1, 1) for head in range(HEADS)]
        ).astype(bf16)
        query = (iota((128, 128), 0) + step * 128) // HEADS
        pick = (iota((128, 128), 1) == query).astype(f32).astype(bf16)
        every = dot(pick, rope_ref[...], 1, 1)
        shape = every.shape
        mine = iota(shape, 1) // rope == lax.rem(iota(shape, 0), HEADS)
        fold = (lax.rem(iota((shape[1], rope), 0), rope) == iota((shape[1], rope), 1)).astype(f32).astype(bf16)
        query_ref[rows, latent:] = dot(jnp.where(mine, every, 0.0).astype(bf16), fold, 1, 0).astype(bf16)

    to_ahead.wait_recv()
    onward = copies.start(slot(behind), slot(behind), at(ahead, core))
    to_sibling.append(copies.start(slot(behind), slot(behind), sibling))
    to_behind.wait_recv()
    to_sibling.append(copies.start(slot(ahead), slot(ahead), sibling))
    onward.wait_recv()
    to_sibling.append(copies.start(slot(2), slot(2), sibling))
    for copy in to_sibling:
        copy.wait_recv()
    keep.wait()
    copies.finish()


def gather_and_project(own_rows, nope, grad, rope, key_up, value_up):
    rows, width = own_rows.shape
    latent = key_up.shape[2]
    vmem = pl.BlockSpec(memory_space=pltpu.VMEM)
    return pl.pallas_call(
        gather_kernel,
        out_shape=(
            pltpu.VMEM((2 * NY * rows, width), bf16),
            pltpu.VMEM((nope.shape[0], width), bf16),
            pltpu.VMEM((nope.shape[0], latent), bf16),
        ),
        in_specs=[vmem] * 6,
        out_specs=(vmem,) * 3,
        scratch_shapes=[
            pltpu.SemaphoreType.DMA((7,)),
            pltpu.SemaphoreType.DMA((7,)),
            pltpu.SemaphoreType.DMA,
        ],
        compiler_params=pltpu.CompilerParams(collective_id=0, has_side_effects=True),
    )(own_rows, nope, grad, rope, key_up, value_up)


def main_kernel(
    table_ref, pos_ref, keys_ref, query_ref, latent_ref, nope_ref, grad_ref, key_up_ref,
    nope_out, rope_out, final, key_out, value_out,
    key_pos, scores, grad_probs, score_t, prob_t, query_grad, rope_parts, out_t,
    rows_out, pair_rows, acc, ring_half, ring_in, block, z_in, piece, piece_in, done,
    key_part, value_part,
    pair_key, pair_value, key_acc, value_acc, key_half, value_half, key_in, value_in,
    key_sum, value_sum, key_far, value_far,
    send_sems, recv_sems,
):
    ctx = lax.axis_index("ctx")
    head = lax.axis_index("head")
    dp = lax.axis_index("dp")
    y, core = ctx // 2, ctx % 2
    z = lax.rem(head, NZ)
    x_lo = head // NZ
    chips = [lax.rem(y + step, NY) for step in range(NY)]
    sibling = {"ctx": y * 2 + 1 - core}
    up = {"ctx": chips[1] * 2 + core}
    down = {"ctx": chips[3] * 2 + core}
    z_at = [lax.rem(z + step, NZ) for step in range(NZ)]
    z_device = [{"head": x_lo * NZ + place} for place in z_at]
    x_pair = {"head": (1 - x_lo) * NZ + z}
    dp_pair = {"dp": 1 - dp}
    far_first = sorted(range(1, NZ), key=lambda step: -min(step, NZ - step))
    friends = [z_device[step] for step in far_first] + [x_pair, dp_pair, up, down, sibling]
    barrier = pltpu.get_barrier_semaphore()
    for device in friends:
        pl.semaphore_signal(barrier, inc=1, device_id=device, device_id_type=MESH)

    blocks = table_ref.shape[1]
    page = keys_ref.shape[0] // blocks
    lanes = key_pos.shape[1]
    for slot in range(blocks):
        start = sum(jnp.where(table_ref[0, at] == slot, at * page, 0) for at in range(blocks))
        key_pos[slot * page:(slot + 1) * page, :] = (iota((page, lanes), 0) + start).astype(f32)
    count = query_ref.shape[0]
    spread = (iota((count // HEADS, count), 0) == iota((count // HEADS, count), 1) // HEADS).astype(f32).astype(bf16)
    pos = jnp.broadcast_to(pos_ref[...], (8, count // HEADS))
    pos_high, pos_low = pos // 32, lax.rem(pos, 32)
    query_pos = (
        dot(pos_high.astype(f32).astype(bf16), spread, 1, 0) * 32.0
        + dot(pos_low.astype(f32).astype(bf16), spread, 1, 0)
    )
    latent = latent_ref.shape[1]
    width = keys_ref.shape[1]
    n_keys = keys_ref.shape[0]
    chunk = 256
    n_chunks = n_keys // chunk

    for part in range(count // lanes):
        mine = slice(part * lanes, (part + 1) * lanes)
        at_pos = query_pos[0:1, mine]

        def score_step(step, row_max):
            rows = pl.ds(step * chunk, chunk)
            raw = dot(keys_ref[rows, :], query_ref[mine, :], 1, 1) * softmax_scale
            raw = jnp.where(key_pos[rows, :] <= at_pos, raw, -jnp.inf)
            scores[rows, :] = raw
            grad_probs[rows, :] = dot(keys_ref[rows, :latent], latent_ref[mine, :], 1, 1)
            return jnp.maximum(row_max, jnp.max(raw, axis=0, keepdims=True))

        row_max = lax.fori_loop(0, n_chunks, score_step, jnp.full((1, lanes), -jnp.inf, f32))

        def weight_step(step, sums):
            rows = pl.ds(step * chunk, chunk)
            weights = jnp.exp(scores[rows, :] - row_max)
            scores[rows, :] = weights
            return (
                sums[0] + jnp.sum(weights, axis=0, keepdims=True),
                sums[1] + jnp.sum(weights * grad_probs[rows, :], axis=0, keepdims=True),
            )

        zero = jnp.zeros((1, lanes), f32)
        denominator, weighted = lax.fori_loop(0, n_chunks, weight_step, (zero, zero))
        scale = 1.0 / denominator
        row_delta = weighted * scale

        def grad_step(step, carry):
            rows = pl.ds(step * chunk, chunk)
            probs = scores[rows, :] * scale
            prob_t[rows, mine] = probs.astype(bf16)
            score_t[rows, mine] = (probs * (grad_probs[rows, :] - row_delta) * softmax_scale).astype(bf16)
            return carry

        lax.fori_loop(0, n_chunks, grad_step, 0)

    pl.semaphore_wait(barrier, len(friends))
    copies = Copies(send_sems, recv_sems)

    def grad_rows(chip, which):
        rows = pl.ds(pl.multiple_of((chip * 2 + which) * 128, 128), 128)
        by_score = dot(score_t[rows, :], query_ref[...], 1, 0)
        by_prob = dot(prob_t[rows, :], latent_ref[...], 1, 0)
        return by_score[:, :latent] + by_prob, by_score[:, latent:]

    pair = {}
    for step in (2, 1, 3, 0):
        low, high = grad_rows(chips[step], 1 - core)
        rows_out[step, :, :, :latent] = low.astype(bf16).reshape(2, 64, latent)
        rows_out[step, :, :, latent:] = high.astype(bf16).reshape(2, 64, width - latent)
        pair[step] = copies.start(rows_out.at[step], pair_rows.at[step], sibling)

    def join(step):
        low, high = grad_rows(chips[step], core)
        pair[step].wait_recv()
        acc[step, :, :, :latent] = total(low.reshape(2, 64, latent), pair_rows[step, :, :, :latent]).astype(bf16)
        acc[step, :, :, latent:] = total(
            high.reshape(2, 64, width - latent), pair_rows[step, :, :, latent:]
        ).astype(bf16)

    join(2)
    up_far = copies.start(acc.at[2, 0], ring_half.at[0], up)
    down_far = copies.start(acc.at[2, 1], ring_half.at[1], down)
    join(1)
    up_own = copies.start(acc.at[1, 1], ring_in.at[0, 1], up)
    join(3)
    down_own = copies.start(acc.at[3, 0], ring_in.at[1, 0], down)
    join(0)
    up_far.wait_recv()
    acc[1, 0] = total(acc[1, 0], ring_half[0]).astype(bf16)
    up_both = copies.start(acc.at[1, 0], ring_in.at[0, 0], up)
    down_far.wait_recv()
    acc[3, 1] = total(acc[3, 1], ring_half[1]).astype(bf16)
    down_both = copies.start(acc.at[3, 1], ring_in.at[1, 1], down)

    @pl.loop(0, count // 128)
    def _(step):
        lane = pl.ds(pl.multiple_of(step * 128, 128), 128)
        grad = dot(score_t[:, lane], keys_ref[...], 0, 0)
        query_grad[lane, :] = grad[:, :latent].astype(bf16)
        rope_high = grad[:, latent:].astype(bf16)
        rope_parts[lane, :width - latent] = rope_high
        rope_parts[lane, width - latent:] = (grad[:, latent:] - rope_high.astype(f32)).astype(bf16)

    for copy in (up_own, down_own, up_both, down_both):
        copy.wait_recv()
    block[...] = total(acc[0], ring_in[0], ring_in[1]).astype(bf16).reshape(block.shape)
    scatter = [copies.start(block.at[z_at[step]], z_in.at[step], z_device[step]) for step in far_first]

    @pl.loop(0, HEADS)
    def _(at):
        part = dot(one_head(nope_ref[...], at), query_grad[...], 0, 0)
        key_part[at] = part.astype(bf16).reshape(key_part.shape[1:])

    pair_weights = [copies.start(key_part.at[:, :, 1 - core], pair_key, sibling)]

    @pl.loop(0, latent // 128)
    def _(step):
        lane = pl.ds(pl.multiple_of(step * 128, 128), 128)
        out_t[lane, :] = dot(keys_ref[:, lane], prob_t[...], 0, 0).astype(bf16)

    @pl.loop(0, HEADS)
    def _(at):
        part = dot(out_t[...], one_head(grad_ref[...], at), 1, 0)
        value_part[at] = part.astype(bf16).reshape(value_part.shape[1:])

    pair_weights.append(copies.start(value_part.at[:, :, 1 - core], pair_value, sibling))

    @pl.loop(0, count // 128)
    def _(step):
        rows = pl.ds(step * 128, 128)
        every = dot(query_grad[rows, :], key_up_ref[...].reshape(-1, latent), 1, 1)
        n = nope_out.shape[1]
        which = lax.rem(iota((128, n), 0), HEADS)
        nope_out[rows, :] = total(
            *[jnp.where(which == at, every[:, at * n:(at + 1) * n], 0.0) for at in range(HEADS)]
        )

    rope = width - latent
    queries = count // HEADS
    for at in range(HEADS):
        order = (iota((count, queries), 0) == iota((count, queries), 1) * HEADS + at).astype(f32).astype(bf16)
        turned = dot(rope_parts[...], order, 0, 0)
        rope_out[at * rope:(at + 1) * rope, :] = turned[:rope] + turned[rope:]

    for copy in pair_weights:
        copy.wait_recv()
    for step in range(NY):
        key_acc[step] = total(key_part[:, chips[step], core], pair_key[:, chips[step]]).astype(bf16)
        value_acc[step] = total(value_part[:, chips[step], core], pair_value[:, chips[step]]).astype(bf16)
    low, high = pl.ds(0, 2), pl.ds(2, 2)
    weights_far = [
        copies.start(key_acc.at[2, low], key_half.at[0], up),
        copies.start(value_acc.at[2, low], value_half.at[0], up),
        copies.start(key_acc.at[2, high], key_half.at[1], down),
        copies.start(value_acc.at[2, high], value_half.at[1], down),
    ]
    weights_in = [
        copies.start(key_acc.at[1, high], key_in.at[0, high], up),
        copies.start(value_acc.at[1, high], value_in.at[0, high], up),
        copies.start(key_acc.at[3, low], key_in.at[1, low], down),
        copies.start(value_acc.at[3, low], value_in.at[1, low], down),
    ]
    for copy in weights_far:
        copy.wait_recv()
    key_acc[1, low] = total(key_acc[1, low], key_half[0]).astype(bf16)
    value_acc[1, low] = total(value_acc[1, low], value_half[0]).astype(bf16)
    key_acc[3, high] = total(key_acc[3, high], key_half[1]).astype(bf16)
    value_acc[3, high] = total(value_acc[3, high], value_half[1]).astype(bf16)
    weights_in += [
        copies.start(key_acc.at[1, low], key_in.at[0, low], up),
        copies.start(value_acc.at[1, low], value_in.at[0, low], up),
        copies.start(key_acc.at[3, high], key_in.at[1, high], down),
        copies.start(value_acc.at[3, high], value_in.at[1, high], down),
    ]

    for copy in scatter:
        copy.wait_recv()
    piece[...] = total(block[z], *[z_in[step] for step in range(1, NZ)]).astype(bf16)
    across = copies.start(piece, piece_in, x_pair)
    across.wait_recv()
    done[...] = total(piece[...], piece_in[...]).astype(bf16)
    final[z] = done[...]
    gather = [copies.start(done, final.at[z], z_device[step]) for step in far_first]

    for copy in weights_in:
        copy.wait_recv()
    key_sum[...] = total(key_acc[0], key_in[0], key_in[1]).astype(bf16)
    value_sum[...] = total(value_acc[0], value_in[0], value_in[1]).astype(bf16)
    weights_pair = [
        copies.start(key_sum.at[:, 1 - dp], key_far, dp_pair),
        copies.start(value_sum.at[:, 1 - dp], value_far, dp_pair),
    ]
    for copy in weights_pair:
        copy.wait_recv()
    key_out[...] = total(key_sum[:, dp], key_far[...])
    value_out[...] = total(value_sum[:, dp], value_far[...])
    for copy in gather:
        copy.wait_recv()
    copies.finish()


def attend_and_reduce(table, pos, keys, query_rows, grad_latent, nope, grad, key_up):
    n_keys, width = keys.shape
    count, n_nope = nope.shape
    heads, _, latent = key_up.shape
    values = grad.shape[1]
    key_piece = (heads, 2, n_nope // 16, latent)
    value_piece = (heads, 2, latent // 16, values)
    half_key = (heads // 2,) + key_piece[1:]
    half_value = (heads // 2,) + value_piece[1:]
    n_copies = 4 + 2 + 6 + 8 + 4 + 15 + 1 + 2 + 15
    vmem = pl.BlockSpec(memory_space=pltpu.VMEM)
    return pl.pallas_call(
        main_kernel,
        out_shape=(
            pltpu.VMEM((count, n_nope), f32),
            pltpu.VMEM((heads * (width - latent), count // heads), f32),
            pltpu.VMEM((NZ, 8, width), bf16),
            pltpu.VMEM((heads, n_nope // 16, latent), f32),
            pltpu.VMEM((heads, latent // 16, values), f32),
        ),
        in_specs=[pl.BlockSpec(memory_space=pltpu.SMEM)] + [vmem] * 7,
        out_specs=(vmem,) * 5,
        scratch_shapes=[
            pltpu.VMEM((n_keys, 256), f32),
            pltpu.VMEM((n_keys, 256), f32),
            pltpu.VMEM((n_keys, 256), f32),
            pltpu.VMEM((n_keys, count), bf16),
            pltpu.VMEM((n_keys, count), bf16),
            pltpu.VMEM((count, latent), bf16),
            pltpu.VMEM((count, 2 * (width - latent)), bf16),
            pltpu.VMEM((latent, count), bf16),
            pltpu.VMEM((NY, 2, 64, width), bf16),
            pltpu.VMEM((NY, 2, 64, width), bf16),
            pltpu.VMEM((NY, 2, 64, width), bf16),
            pltpu.VMEM((2, 64, width), bf16),
            pltpu.VMEM((2, 2, 64, width), bf16),
            pltpu.VMEM((NZ, 8, width), bf16),
            pltpu.VMEM((NZ, 8, width), bf16),
            pltpu.VMEM((8, width), bf16),
            pltpu.VMEM((8, width), bf16),
            pltpu.VMEM((8, width), bf16),
            pltpu.VMEM((heads, NY, 2) + key_piece[1:], bf16),
            pltpu.VMEM((heads, NY, 2) + value_piece[1:], bf16),
            pltpu.VMEM((heads, NY) + key_piece[1:], bf16),
            pltpu.VMEM((heads, NY) + value_piece[1:], bf16),
            pltpu.VMEM((NY,) + key_piece, bf16),
            pltpu.VMEM((NY,) + value_piece, bf16),
            pltpu.VMEM((2,) + half_key, bf16),
            pltpu.VMEM((2,) + half_value, bf16),
            pltpu.VMEM((2,) + key_piece, bf16),
            pltpu.VMEM((2,) + value_piece, bf16),
            pltpu.VMEM(key_piece, bf16),
            pltpu.VMEM(value_piece, bf16),
            pltpu.VMEM((heads, n_nope // 16, latent), bf16),
            pltpu.VMEM((heads, latent // 16, values), bf16),
            pltpu.SemaphoreType.DMA((n_copies,)),
            pltpu.SemaphoreType.DMA((n_copies,)),
        ],
        compiler_params=pltpu.CompilerParams(collective_id=1, has_side_effects=True),
    )(table, pos, *in_vmem(keys, query_rows, grad_latent), nope, grad, key_up)


def in_vmem(*arrays):
    return [pltpu.with_memory_space_constraint(array, pltpu.VMEM) for array in arrays]


def store_kernel(*refs):
    for source, target in zip(refs[:5], refs[5:10]):
        target[...] = source[...].astype(f32)


def store_results(*results):
    vmem = pl.BlockSpec(memory_space=pltpu.VMEM)
    return pl.pallas_call(
        store_kernel,
        out_shape=tuple(jax.ShapeDtypeStruct(result.shape, f32) for result in results),
        in_specs=[vmem] * len(results),
        out_specs=(vmem,) * len(results),
    )(*in_vmem(*results))


def on_device(
    query_nope, query_rope, query_pos, latent_cache, block_table, key_up, value_up, grad_out
):
    row_width = latent_cache.shape[3]
    nope = query_nope.reshape(-1, query_nope.shape[3])
    grad = grad_out.reshape(-1, grad_out.shape[3])
    rope = jnp.transpose(query_rope[0], (1, 2, 0))
    heads, rope_width, queries = rope.shape
    own_rows = latent_cache.reshape(-1, row_width)
    keys, query_rows, grad_latent = gather_and_project(
        own_rows, nope, grad, rope.reshape(-1, queries), key_up, value_up
    )
    results = attend_and_reduce(
        block_table, query_pos, keys, query_rows, grad_latent, nope, grad, key_up
    )
    grad_nope, grad_rope, cache_grad, grad_key_map, grad_value_map = store_results(*results)
    return (
        grad_nope.reshape(query_nope.shape),
        jnp.transpose(grad_rope.reshape(heads, rope_width, queries), (2, 0, 1))[None],
        cache_grad.reshape(latent_cache.shape),
        grad_key_map,
        grad_value_map,
    )


def solution(mesh):
    placed = (
        P("dp", "ctx", "head", None),
        P("dp", "ctx", "head", None),
        P("dp", "ctx"),
        P("dp", "ctx", None, None),
        P("dp", None),
        P("head", None, None),
        P("head", None, None),
        P("dp", "ctx", "head", None),
    )
    return jax.shard_map(
        on_device,
        mesh=mesh,
        in_specs=placed,
        out_specs=(
            P("dp", "ctx", "head", None),
            P("dp", "ctx", "head", None),
            P("dp", "ctx", None, None),
            P("head", ("ctx", "dp"), None),
            P("head", ("ctx", "dp"), None),
        ),
        check_vma=False,
    )
```

```python
import jax
import jax.numpy as jnp
from jax import lax
from jax.experimental import pallas as pl
from jax.experimental.pallas import tpu as pltpu
from jax.sharding import PartitionSpec as P

softmax_scale = 192.0 ** (-0.5)
MESH = pl.DeviceIdType.MESH
NY = 4
NZ = 16
HEADS = 4
VMEM_LIMIT = 48 * 2**20
f32 = jnp.float32
bf16 = jnp.bfloat16


class Copies:
    def __init__(self, send_sems, recv_sems):
        self.send_sems, self.recv_sems, self.made = send_sems, recv_sems, []

    def start(self, src, dst, device):
        at = len(self.made)
        copy = pltpu.make_async_remote_copy(
            src_ref=src,
            dst_ref=dst,
            send_sem=self.send_sems.at[at],
            recv_sem=self.recv_sems.at[at],
            device_id=device,
            device_id_type=MESH,
        )
        copy.start()
        self.made.append(copy)
        return copy

    def finish(self):
        for copy in self.made:
            copy.wait_send()


def entry_barrier(devices):
    barrier = pltpu.get_barrier_semaphore()
    for device in devices:
        pl.semaphore_signal(barrier, inc=1, device_id=device, device_id_type=MESH)
    pl.semaphore_wait(barrier, len(devices))


def total(*terms):
    terms = [term.astype(f32) for term in terms]
    result = terms[0]
    for term in terms[1:]:
        result = result + term
    return result


def dot(a, b, a_dim, b_dim):
    return lax.dot_general(a, b, (((a_dim,), (b_dim,)), ((), ())), preferred_element_type=f32)


def iota(shape, dim):
    return lax.broadcasted_iota(jnp.int32, shape, dim)


def one_head(values, head):
    return jnp.where(lax.rem(iota(values.shape, 0), HEADS) == head, values.astype(f32), 0.0).astype(bf16)


def fetch(sources, targets, sems):
    copies = []
    for at, (source, target) in enumerate(zip(sources, targets)):
        copies.append(pltpu.make_async_copy(source, target, sems.at[at]))
        copies[-1].start()
    return copies


def gather_kernel(
    table_ref, pos_ref, own_ref, nope_hbm, grad_hbm, rope_hbm, key_up_hbm, value_up_hbm,
    all_ref, query_ref, latent_ref, scores, grad_probs, row_max,
    nope_ref, grad_ref, rope_ref, key_up_ref, value_up_ref,
    send_sems, recv_sems, own_sem, fetch_sems,
):
    fetches = fetch(
        [nope_hbm, key_up_hbm, rope_hbm, grad_hbm, value_up_hbm],
        [nope_ref, key_up_ref, rope_ref, grad_ref, value_up_ref],
        fetch_sems,
    )
    ctx = lax.axis_index("ctx")
    y, core = ctx // 2, ctx % 2
    rows_each = own_ref.shape[0]
    half = rows_each // 2

    def at(step, which):
        return {"ctx": lax.rem(y + step, NY) * 2 + which}

    def place(step, which):
        return pl.multiple_of((lax.rem(y + step, NY) * 2 + which) * rows_each, rows_each)

    def slot(step, part):
        return all_ref.at[pl.ds(pl.multiple_of(place(step, core) + part * half, half), half)]

    ahead = 1 + 2 * core
    behind = 3 - 2 * core
    sibling = at(0, 1 - core)
    entry_barrier([sibling, at(1, core), at(3, core)])
    copies = Copies(send_sems, recv_sems)
    halves = range(2)
    to_ahead, to_behind = [], []
    for part in halves:
        mine = own_ref.at[pl.ds(part * half, half)]
        to_ahead.append(copies.start(mine, slot(0, part), at(ahead, core)))
        to_behind.append(copies.start(mine, slot(0, part), at(behind, core)))
    own_slot = all_ref.at[pl.ds(place(0, core), rows_each)]
    pair_own = copies.start(own_ref, own_slot, sibling)
    keep = pltpu.make_async_copy(own_ref, own_slot, own_sem)
    keep.start()

    latent = key_up_ref.shape[2]
    rope = rope_ref.shape[0] // HEADS
    count = nope_ref.shape[0]

    def project(step):
        rows = slice(step * 128, (step + 1) * 128)
        nope, grad = nope_ref[rows, :], grad_ref[rows, :]
        spread = jnp.concatenate([one_head(nope, head) for head in range(HEADS)], axis=1)
        up = key_up_ref[...].reshape(spread.shape[1], latent)
        query_ref[rows, :latent] = dot(spread, up, 1, 0).astype(bf16)
        latent_ref[rows, :] = total(
            *[dot(one_head(grad, head), value_up_ref[head], 1, 1) for head in range(HEADS)]
        ).astype(bf16)
        query = (iota((128, 128), 0) + step * 128) // HEADS
        pick = (iota((128, 128), 1) == query).astype(f32).astype(bf16)
        every = dot(pick, rope_ref[...], 1, 1)
        shape = every.shape
        mine = iota(shape, 1) // rope == lax.rem(iota(shape, 0), HEADS)
        fold = (lax.rem(iota((shape[1], rope), 0), rope) == iota((shape[1], rope), 1)).astype(f32).astype(bf16)
        query_ref[rows, latent:] = dot(jnp.where(mine, every, 0.0).astype(bf16), fold, 1, 0).astype(bf16)

    for copy in fetches:
        copy.wait()
    project(0)
    project(1)
    project(2)
    onward, from_behind, from_ahead = [], [], []
    for part in halves:
        to_ahead[part].wait_recv()
        onward.append(copies.start(slot(behind, part), slot(behind, part), at(ahead, core)))
        from_behind.append(copies.start(slot(behind, part), slot(behind, part), sibling))
        to_behind[part].wait_recv()
        from_ahead.append(copies.start(slot(ahead, part), slot(ahead, part), sibling))
        if part == 0:
            project(3)

    blocks = table_ref.shape[1]
    page = all_ref.shape[0] // blocks
    spread = (iota((count // HEADS, count), 0) == iota((count // HEADS, count), 1) // HEADS).astype(f32).astype(bf16)
    pos = jnp.broadcast_to(pos_ref[...], (8, count // HEADS))
    query_pos = (
        dot((pos // 32).astype(f32).astype(bf16), spread, 1, 0) * 32.0
        + dot(lax.rem(pos, 32).astype(f32).astype(bf16), spread, 1, 0)
    )
    row_max[...] = jnp.full(row_max.shape, -jnp.inf, f32)

    def score(source, first, start):
        rows = pl.ds(start, rows_each)
        keys = source[pl.ds(first, rows_each), :]
        raw = dot(keys, query_ref[...], 1, 1) * softmax_scale
        index = iota((rows_each, 1), 0)
        key_pos = lax.rem(index, page)
        for part in range(rows_each // page):
            here = start // page + part
            base = sum(jnp.where(table_ref[0, b] == here, b * page, 0) for b in range(blocks))
            key_pos = key_pos + jnp.where(index // page == part, base, 0)
        raw = jnp.where(key_pos.astype(f32) <= query_pos[0:1, :], raw, -jnp.inf)
        scores[rows, :] = raw
        grad_probs[rows, :] = dot(keys[:, :latent], latent_ref[...], 1, 1)
        row_max[...] = jnp.maximum(row_max[...], jnp.max(raw, axis=0, keepdims=True))

    keep.wait()
    score(all_ref, place(0, core), place(0, core))
    pair_own.wait_recv()
    score(all_ref, place(0, 1 - core), place(0, 1 - core))
    score(all_ref, place(behind, core), place(behind, core))
    onward[0].wait_recv()
    far = [copies.start(slot(2, 0), slot(2, 0), sibling)]
    score(all_ref, place(ahead, core), place(ahead, core))
    onward[1].wait_recv()
    far.append(copies.start(slot(2, 1), slot(2, 1), sibling))
    for copy in from_behind:
        copy.wait_recv()
    score(all_ref, place(ahead, 1 - core), place(ahead, 1 - core))
    for copy in from_ahead:
        copy.wait_recv()
    score(all_ref, place(behind, 1 - core), place(behind, 1 - core))
    score(all_ref, place(2, core), place(2, core))
    for copy in far:
        copy.wait_recv()
    score(all_ref, place(2, 1 - core), place(2, 1 - core))
    copies.finish()


def gather_and_score(table, pos, own_rows, nope, grad, rope, key_up, value_up):
    rows, width = own_rows.shape
    latent = key_up.shape[2]
    count = nope.shape[0]
    n_keys = 2 * NY * rows
    vmem = pl.BlockSpec(memory_space=pltpu.VMEM)
    hbm = pl.BlockSpec(memory_space=pltpu.HBM)
    return pl.pallas_call(
        gather_kernel,
        out_shape=(
            pltpu.VMEM((n_keys, width), bf16),
            pltpu.VMEM((count, width), bf16),
            pltpu.VMEM((count, latent), bf16),
            pltpu.VMEM((n_keys, count), f32),
            pltpu.VMEM((n_keys, count), f32),
            pltpu.VMEM((1, count), f32),
        ),
        in_specs=[pl.BlockSpec(memory_space=pltpu.SMEM), vmem] + [hbm] * 6,
        out_specs=(vmem,) * 6,
        scratch_shapes=[pltpu.VMEM(array.shape, bf16) for array in (nope, grad, rope, key_up, value_up)]
        + [
            pltpu.SemaphoreType.DMA((13,)),
            pltpu.SemaphoreType.DMA((13,)),
            pltpu.SemaphoreType.DMA,
            pltpu.SemaphoreType.DMA((5,)),
        ],
        compiler_params=pltpu.CompilerParams(
            collective_id=0, has_side_effects=True, vmem_limit_bytes=VMEM_LIMIT
        ),
    )(table, pos, own_rows, nope, grad, rope, key_up, value_up)


def main_kernel(
    keys_ref, query_ref, latent_ref, scores, grad_probs, row_max_ref, nope_hbm, grad_hbm, key_up_hbm,
    nope_out, rope_out, final, key_out, value_out,
    score_t, prob_t, query_grad, rope_parts, out_t,
    rows_out, pair_rows, acc, ring_half, ring_in, block, z_in, piece, piece_in, done,
    key_part, value_part,
    pair_key, pair_value, key_acc, value_acc, key_half, value_half, key_in, value_in,
    key_sum, value_sum, key_far, value_far,
    nope_ref, grad_ref, key_up_ref,
    send_sems, recv_sems, fetch_sems,
):
    ctx = lax.axis_index("ctx")
    head = lax.axis_index("head")
    dp = lax.axis_index("dp")
    y, core = ctx // 2, ctx % 2
    z = lax.rem(head, NZ)
    x_lo = head // NZ
    chips = [lax.rem(y + step, NY) for step in range(NY)]
    sibling = {"ctx": y * 2 + 1 - core}
    up = {"ctx": chips[1] * 2 + core}
    down = {"ctx": chips[3] * 2 + core}
    z_at = [lax.rem(z + step, NZ) for step in range(NZ)]
    z_device = [{"head": x_lo * NZ + place} for place in z_at]
    x_pair = {"head": (1 - x_lo) * NZ + z}
    dp_pair = {"dp": 1 - dp}
    far_first = sorted(range(1, NZ), key=lambda step: -min(step, NZ - step))
    friends = [z_device[step] for step in far_first] + [x_pair, dp_pair, up, down, sibling]
    barrier = pltpu.get_barrier_semaphore()
    for device in friends:
        pl.semaphore_signal(barrier, inc=1, device_id=device, device_id_type=MESH)

    fetches = fetch([nope_hbm, grad_hbm, key_up_hbm], [nope_ref, grad_ref, key_up_ref], fetch_sems)
    count = query_ref.shape[0]
    latent = latent_ref.shape[1]
    width = keys_ref.shape[1]
    n_keys = keys_ref.shape[0]
    chunk = 64
    n_chunks = n_keys // chunk
    row_max = row_max_ref[...]

    def weight_step(step, sums):
        rows = pl.ds(step * chunk, chunk)
        weights = jnp.exp(scores[rows, :] - row_max)
        pair = weights * grad_probs[rows, :]
        return sums[0] + by_eight(weights), sums[1] + by_eight(pair)

    def by_eight(values):
        return jnp.sum(values.reshape(-1, 8, values.shape[1]), axis=0)

    zero = jnp.zeros((8, count), f32)
    sums = lax.fori_loop(0, n_chunks, weight_step, (zero, zero))
    denominator, weighted = [jnp.sum(part, axis=0, keepdims=True) for part in sums]
    scale = 1.0 / denominator
    row_delta = weighted * scale

    def grad_step(step, carry):
        rows = pl.ds(step * chunk, chunk)
        probs = jnp.exp(scores[rows, :] - row_max) * scale
        prob_t[rows, :] = probs.astype(bf16)
        score_t[rows, :] = (probs * (grad_probs[rows, :] - row_delta) * softmax_scale).astype(bf16)
        return carry

    lax.fori_loop(0, n_chunks, grad_step, 0)

    pl.semaphore_wait(barrier, len(friends))
    copies = Copies(send_sems, recv_sems)

    def grad_rows(chip, which):
        rows = pl.ds(pl.multiple_of((chip * 2 + which) * 128, 128), 128)
        by_score = dot(score_t[rows, :], query_ref[...], 1, 0)
        by_prob = dot(prob_t[rows, :], latent_ref[...], 1, 0)
        return by_score[:, :latent] + by_prob, by_score[:, latent:]

    pair = {}
    for step in (2, 1, 3, 0):
        low, high = grad_rows(chips[step], 1 - core)
        rows_out[step, :, :, :latent] = low.astype(bf16).reshape(2, 64, latent)
        rows_out[step, :, :, latent:] = high.astype(bf16).reshape(2, 64, width - latent)
        pair[step] = copies.start(rows_out.at[step], pair_rows.at[step], sibling)

    def join(step):
        low, high = grad_rows(chips[step], core)
        pair[step].wait_recv()
        acc[step, :, :, :latent] = total(low.reshape(2, 64, latent), pair_rows[step, :, :, :latent]).astype(bf16)
        acc[step, :, :, latent:] = total(
            high.reshape(2, 64, width - latent), pair_rows[step, :, :, latent:]
        ).astype(bf16)

    join(2)
    up_far = copies.start(acc.at[2, 0], ring_half.at[0], up)
    down_far = copies.start(acc.at[2, 1], ring_half.at[1], down)
    join(1)
    up_own = copies.start(acc.at[1, 1], ring_in.at[0, 1], up)
    join(3)
    down_own = copies.start(acc.at[3, 0], ring_in.at[1, 0], down)
    join(0)
    up_far.wait_recv()
    acc[1, 0] = total(acc[1, 0], ring_half[0]).astype(bf16)
    up_both = copies.start(acc.at[1, 0], ring_in.at[0, 0], up)
    down_far.wait_recv()
    acc[3, 1] = total(acc[3, 1], ring_half[1]).astype(bf16)
    down_both = copies.start(acc.at[3, 1], ring_in.at[1, 1], down)

    @pl.loop(0, count // 128)
    def _(step):
        lane = pl.ds(pl.multiple_of(step * 128, 128), 128)
        grad = dot(score_t[:, lane], keys_ref[...], 0, 0)
        query_grad[lane, :] = grad[:, :latent].astype(bf16)
        rope_high = grad[:, latent:].astype(bf16)
        rope_parts[lane, :width - latent] = rope_high
        rope_parts[lane, width - latent:] = (grad[:, latent:] - rope_high.astype(f32)).astype(bf16)

    for copy in (up_own, down_own, up_both, down_both):
        copy.wait_recv()
    block[...] = total(acc[0], ring_in[0], ring_in[1]).astype(bf16).reshape(block.shape)
    scatter = [copies.start(block.at[z_at[step]], z_in.at[step], z_device[step]) for step in far_first]

    for copy in fetches:
        copy.wait()

    @pl.loop(0, HEADS)
    def _(at):
        part = dot(one_head(nope_ref[...], at), query_grad[...], 0, 0)
        key_part[at] = part.astype(bf16).reshape(key_part.shape[1:])

    pair_weights = [copies.start(key_part.at[:, :, 1 - core], pair_key, sibling)]

    @pl.loop(0, latent // 128)
    def _(step):
        lane = pl.ds(pl.multiple_of(step * 128, 128), 128)
        out_t[lane, :] = dot(keys_ref[:, lane], prob_t[...], 0, 0).astype(bf16)

    @pl.loop(0, HEADS)
    def _(at):
        part = dot(out_t[...], one_head(grad_ref[...], at), 1, 0)
        value_part[at] = part.astype(bf16).reshape(value_part.shape[1:])

    pair_weights.append(copies.start(value_part.at[:, :, 1 - core], pair_value, sibling))

    @pl.loop(0, count // 128)
    def _(step):
        rows = pl.ds(step * 128, 128)
        every = dot(query_grad[rows, :], key_up_ref[...].reshape(-1, latent), 1, 1)
        n = nope_out.shape[1]
        which = lax.rem(iota((128, n), 0), HEADS)
        nope_out[rows, :] = total(
            *[jnp.where(which == at, every[:, at * n:(at + 1) * n], 0.0) for at in range(HEADS)]
        )

    rope = width - latent
    queries = count // HEADS
    for at in range(HEADS):
        order = (iota((count, queries), 0) == iota((count, queries), 1) * HEADS + at).astype(f32).astype(bf16)
        turned = dot(rope_parts[...], order, 0, 0)
        rope_out[at * rope:(at + 1) * rope, :] = turned[:rope] + turned[rope:]

    for copy in pair_weights:
        copy.wait_recv()
    for step in range(NY):
        key_acc[step] = total(key_part[:, chips[step], core], pair_key[:, chips[step]]).astype(bf16)
        value_acc[step] = total(value_part[:, chips[step], core], pair_value[:, chips[step]]).astype(bf16)
    low, high = pl.ds(0, 2), pl.ds(2, 2)
    weights_far = [
        copies.start(key_acc.at[2, low], key_half.at[0], up),
        copies.start(value_acc.at[2, low], value_half.at[0], up),
        copies.start(key_acc.at[2, high], key_half.at[1], down),
        copies.start(value_acc.at[2, high], value_half.at[1], down),
    ]
    weights_in = [
        copies.start(key_acc.at[1, high], key_in.at[0, high], up),
        copies.start(value_acc.at[1, high], value_in.at[0, high], up),
        copies.start(key_acc.at[3, low], key_in.at[1, low], down),
        copies.start(value_acc.at[3, low], value_in.at[1, low], down),
    ]
    for copy in scatter:
        copy.wait_recv()
    piece[...] = total(block[z], *[z_in[step] for step in range(1, NZ)]).astype(bf16)
    across = copies.start(piece, piece_in, x_pair)
    for copy in weights_far:
        copy.wait_recv()
    key_acc[1, low] = total(key_acc[1, low], key_half[0]).astype(bf16)
    value_acc[1, low] = total(value_acc[1, low], value_half[0]).astype(bf16)
    key_acc[3, high] = total(key_acc[3, high], key_half[1]).astype(bf16)
    value_acc[3, high] = total(value_acc[3, high], value_half[1]).astype(bf16)
    weights_in += [
        copies.start(key_acc.at[1, low], key_in.at[0, low], up),
        copies.start(value_acc.at[1, low], value_in.at[0, low], up),
        copies.start(key_acc.at[3, high], key_in.at[1, high], down),
        copies.start(value_acc.at[3, high], value_in.at[1, high], down),
    ]

    across.wait_recv()
    done[...] = total(piece[...], piece_in[...]).astype(bf16)
    final[z] = done[...]
    gather = [copies.start(done, final.at[z], z_device[step]) for step in far_first]

    for copy in weights_in:
        copy.wait_recv()
    key_sum[...] = total(key_acc[0], key_in[0], key_in[1]).astype(bf16)
    value_sum[...] = total(value_acc[0], value_in[0], value_in[1]).astype(bf16)
    weights_pair = [
        copies.start(key_sum.at[:, 1 - dp], key_far, dp_pair),
        copies.start(value_sum.at[:, 1 - dp], value_far, dp_pair),
    ]
    for copy in weights_pair:
        copy.wait_recv()
    key_out[...] = total(key_sum[:, dp], key_far[...])
    value_out[...] = total(value_sum[:, dp], value_far[...])
    for copy in gather:
        copy.wait_recv()
    copies.finish()


def attend_and_reduce(keys, query_rows, grad_latent, scores, grad_probs, row_max, nope, grad, key_up):
    n_keys, width = keys.shape
    count, n_nope = nope.shape
    heads, _, latent = key_up.shape
    values = grad.shape[1]
    key_piece = (heads, 2, n_nope // 16, latent)
    value_piece = (heads, 2, latent // 16, values)
    half_key = (heads // 2,) + key_piece[1:]
    half_value = (heads // 2,) + value_piece[1:]
    n_copies = 4 + 2 + 6 + 8 + 4 + 15 + 1 + 2 + 15
    vmem = pl.BlockSpec(memory_space=pltpu.VMEM)
    hbm = pl.BlockSpec(memory_space=pltpu.HBM)
    return pl.pallas_call(
        main_kernel,
        out_shape=(
            pltpu.VMEM((count, n_nope), f32),
            pltpu.VMEM((heads * (width - latent), count // heads), f32),
            pltpu.VMEM((NZ, 8, width), bf16),
            pltpu.VMEM((heads, n_nope // 16, latent), f32),
            pltpu.VMEM((heads, latent // 16, values), f32),
        ),
        in_specs=[vmem] * 6 + [hbm] * 3,
        out_specs=(vmem,) * 5,
        scratch_shapes=[
            pltpu.VMEM((n_keys, count), bf16),
            pltpu.VMEM((n_keys, count), bf16),
            pltpu.VMEM((count, latent), bf16),
            pltpu.VMEM((count, 2 * (width - latent)), bf16),
            pltpu.VMEM((latent, count), bf16),
            pltpu.VMEM((NY, 2, 64, width), bf16),
            pltpu.VMEM((NY, 2, 64, width), bf16),
            pltpu.VMEM((NY, 2, 64, width), bf16),
            pltpu.VMEM((2, 64, width), bf16),
            pltpu.VMEM((2, 2, 64, width), bf16),
            pltpu.VMEM((NZ, 8, width), bf16),
            pltpu.VMEM((NZ, 8, width), bf16),
            pltpu.VMEM((8, width), bf16),
            pltpu.VMEM((8, width), bf16),
            pltpu.VMEM((8, width), bf16),
            pltpu.VMEM((heads, NY, 2) + key_piece[1:], bf16),
            pltpu.VMEM((heads, NY, 2) + value_piece[1:], bf16),
            pltpu.VMEM((heads, NY) + key_piece[1:], bf16),
            pltpu.VMEM((heads, NY) + value_piece[1:], bf16),
            pltpu.VMEM((NY,) + key_piece, bf16),
            pltpu.VMEM((NY,) + value_piece, bf16),
            pltpu.VMEM((2,) + half_key, bf16),
            pltpu.VMEM((2,) + half_value, bf16),
            pltpu.VMEM((2,) + key_piece, bf16),
            pltpu.VMEM((2,) + value_piece, bf16),
            pltpu.VMEM(key_piece, bf16),
            pltpu.VMEM(value_piece, bf16),
            pltpu.VMEM((heads, n_nope // 16, latent), bf16),
            pltpu.VMEM((heads, latent // 16, values), bf16),
            pltpu.VMEM(nope.shape, bf16),
            pltpu.VMEM(grad.shape, bf16),
            pltpu.VMEM(key_up.shape, bf16),
            pltpu.SemaphoreType.DMA((n_copies,)),
            pltpu.SemaphoreType.DMA((n_copies,)),
            pltpu.SemaphoreType.DMA((3,)),
        ],
        compiler_params=pltpu.CompilerParams(
            collective_id=1, has_side_effects=True, vmem_limit_bytes=VMEM_LIMIT
        ),
    )(*in_vmem(keys, query_rows, grad_latent, scores, grad_probs, row_max), nope, grad, key_up)


def in_vmem(*arrays):
    return [pltpu.with_memory_space_constraint(array, pltpu.VMEM) for array in arrays]


def store_kernel(*refs):
    for source, target in zip(refs[:5], refs[5:10]):
        target[...] = source[...].astype(f32)


def store_results(*results):
    vmem = pl.BlockSpec(memory_space=pltpu.VMEM)
    return pl.pallas_call(
        store_kernel,
        out_shape=tuple(jax.ShapeDtypeStruct(result.shape, f32) for result in results),
        in_specs=[vmem] * len(results),
        out_specs=(vmem,) * len(results),
        compiler_params=pltpu.CompilerParams(vmem_limit_bytes=VMEM_LIMIT),
    )(*in_vmem(*results))


def on_device(
    query_nope, query_rope, query_pos, latent_cache, block_table, key_up, value_up, grad_out
):
    row_width = latent_cache.shape[3]
    nope = query_nope.reshape(-1, query_nope.shape[3])
    grad = grad_out.reshape(-1, grad_out.shape[3])
    rope = jnp.transpose(query_rope[0], (1, 2, 0))
    heads, rope_width, queries = rope.shape
    own_rows = latent_cache.reshape(-1, row_width)
    shared = gather_and_score(
        block_table, query_pos, own_rows, nope, grad, rope.reshape(-1, queries), key_up, value_up
    )
    results = attend_and_reduce(*shared, nope, grad, key_up)
    grad_nope, grad_rope, cache_grad, grad_key_map, grad_value_map = store_results(*results)
    return (
        grad_nope.reshape(query_nope.shape),
        jnp.transpose(grad_rope.reshape(heads, rope_width, queries), (2, 0, 1))[None],
        cache_grad.reshape(latent_cache.shape),
        grad_key_map,
        grad_value_map,
    )


def solution(mesh):
    placed = (
        P("dp", "ctx", "head", None),
        P("dp", "ctx", "head", None),
        P("dp", "ctx"),
        P("dp", "ctx", None, None),
        P("dp", None),
        P("head", None, None),
        P("head", None, None),
        P("dp", "ctx", "head", None),
    )
    return jax.shard_map(
        on_device,
        mesh=mesh,
        in_specs=placed,
        out_specs=(
            P("dp", "ctx", "head", None),
            P("dp", "ctx", "head", None),
            P("dp", "ctx", None, None),
            P("head", ("ctx", "dp"), None),
            P("head", ("ctx", "dp"), None),
        ),
        check_vma=False,
    )
```

```python
import jax
import jax.numpy as jnp
from jax import lax
from jax.experimental import pallas as pl
from jax.experimental.pallas import tpu as pltpu
from jax.sharding import PartitionSpec as P

softmax_scale = 192.0 ** (-0.5)
MESH = pl.DeviceIdType.MESH
NY = 4
NZ = 16
HEADS = 4
VMEM_LIMIT = 48 * 2**20
f32 = jnp.float32
bf16 = jnp.bfloat16


class Copies:
    def __init__(self, send_sems, recv_sems):
        self.send_sems, self.recv_sems, self.made = send_sems, recv_sems, []

    def start(self, src, dst, device, recv_sem=None):
        at = len(self.made)
        copy = pltpu.make_async_remote_copy(
            src_ref=src,
            dst_ref=dst,
            send_sem=self.send_sems.at[at],
            recv_sem=self.recv_sems.at[at] if recv_sem is None else recv_sem,
            device_id=device,
            device_id_type=MESH,
        )
        copy.start()
        self.made.append(copy)
        return copy

    def finish(self):
        for copy in self.made:
            copy.wait_send()


def entry_barrier(devices):
    barrier = pltpu.get_barrier_semaphore()
    for device in devices:
        pl.semaphore_signal(barrier, inc=1, device_id=device, device_id_type=MESH)
    pl.semaphore_wait(barrier, len(devices))


def total(*terms):
    terms = [term.astype(f32) for term in terms]
    result = terms[0]
    for term in terms[1:]:
        result = result + term
    return result


def dot(a, b, a_dim, b_dim):
    return lax.dot_general(a, b, (((a_dim,), (b_dim,)), ((), ())), preferred_element_type=f32)


def iota(shape, dim):
    return lax.broadcasted_iota(jnp.int32, shape, dim)


def one_head(values, head):
    return jnp.where(lax.rem(iota(values.shape, 0), HEADS) == head, values.astype(f32), 0.0).astype(bf16)


def fetch(sources, targets, sems):
    copies = []
    for at, (source, target) in enumerate(zip(sources, targets)):
        copies.append(pltpu.make_async_copy(source, target, sems.at[at]))
        copies[-1].start()
    return copies


def gather_kernel(
    table_ref, pos_ref, own_ref, nope_hbm, grad_hbm, rope_hbm, key_up_hbm, value_up_hbm,
    all_ref, query_ref, latent_ref, scores, grad_probs, row_max,
    nope_ref, grad_ref, rope_ref, key_up_ref, value_up_ref,
    send_sems, recv_sems, own_sem, fetch_sems,
):
    fetches = fetch(
        [nope_hbm, key_up_hbm, rope_hbm, grad_hbm, value_up_hbm],
        [nope_ref, key_up_ref, rope_ref, grad_ref, value_up_ref],
        fetch_sems,
    )
    ctx = lax.axis_index("ctx")
    y, core = ctx // 2, ctx % 2
    rows_each = own_ref.shape[0]
    half = rows_each // 2

    def at(step, which):
        return {"ctx": lax.rem(y + step, NY) * 2 + which}

    def place(step, which):
        return pl.multiple_of((lax.rem(y + step, NY) * 2 + which) * rows_each, rows_each)

    def slot(step, part):
        return all_ref.at[pl.ds(pl.multiple_of(place(step, core) + part * half, half), half)]

    ahead = 1 + 2 * core
    behind = 3 - 2 * core
    sibling = at(0, 1 - core)
    entry_barrier([sibling, at(1, core), at(3, core)])
    copies = Copies(send_sems, recv_sems)
    halves = range(2)
    own_half = [own_ref.at[pl.ds(part * half, half)] for part in halves]
    to_ahead = [copies.start(own_half[part], slot(0, part), at(ahead, core)) for part in halves]
    own_slot = all_ref.at[pl.ds(place(0, core), rows_each)]
    pair_own = copies.start(own_ref, own_slot, sibling)
    keep = pltpu.make_async_copy(own_ref, own_slot, own_sem)
    keep.start()

    latent = key_up_ref.shape[2]
    rope = rope_ref.shape[0] // HEADS
    count = nope_ref.shape[0]

    def project(step):
        rows = slice(step * 128, (step + 1) * 128)
        nope, grad = nope_ref[rows, :], grad_ref[rows, :]
        spread = jnp.concatenate([one_head(nope, head) for head in range(HEADS)], axis=1)
        up = key_up_ref[...].reshape(spread.shape[1], latent)
        query_ref[rows, :latent] = dot(spread, up, 1, 0).astype(bf16)
        latent_ref[rows, :] = total(
            *[dot(one_head(grad, head), value_up_ref[head], 1, 1) for head in range(HEADS)]
        ).astype(bf16)
        query = (iota((128, 128), 0) + step * 128) // HEADS
        pick = (iota((128, 128), 1) == query).astype(f32).astype(bf16)
        every = dot(pick, rope_ref[...], 1, 1)
        shape = every.shape
        mine = iota(shape, 1) // rope == lax.rem(iota(shape, 0), HEADS)
        fold = (lax.rem(iota((shape[1], rope), 0), rope) == iota((shape[1], rope), 1)).astype(f32).astype(bf16)
        query_ref[rows, latent:] = dot(jnp.where(mine, every, 0.0).astype(bf16), fold, 1, 0).astype(bf16)

    for copy in fetches:
        copy.wait()
    project(0)
    project(1)
    to_behind = [copies.start(own_half[part], slot(0, part), at(behind, core)) for part in halves]
    project(2)
    onward, from_behind = [], []
    for part in halves:
        to_ahead[part].wait_recv()
        onward.append(copies.start(slot(behind, part), slot(behind, part), at(ahead, core)))
        from_behind.append(copies.start(slot(behind, part), slot(behind, part), sibling))
        if part == 0:
            project(3)

    blocks = table_ref.shape[1]
    page = all_ref.shape[0] // blocks
    spread = (iota((count // HEADS, count), 0) == iota((count // HEADS, count), 1) // HEADS).astype(f32).astype(bf16)
    pos = jnp.broadcast_to(pos_ref[...], (8, count // HEADS))
    query_pos = (
        dot((pos // 32).astype(f32).astype(bf16), spread, 1, 0) * 32.0
        + dot(lax.rem(pos, 32).astype(f32).astype(bf16), spread, 1, 0)
    )
    row_max[...] = jnp.full(row_max.shape, -jnp.inf, f32)

    def score(source, first, start):
        rows = pl.ds(start, rows_each)
        keys = source[pl.ds(first, rows_each), :]
        raw = dot(keys, query_ref[...], 1, 1) * softmax_scale
        index = iota((rows_each, 1), 0)
        key_pos = lax.rem(index, page)
        for part in range(rows_each // page):
            here = start // page + part
            base = sum(jnp.where(table_ref[0, b] == here, b * page, 0) for b in range(blocks))
            key_pos = key_pos + jnp.where(index // page == part, base, 0)
        raw = jnp.where(key_pos.astype(f32) <= query_pos[0:1, :], raw, -jnp.inf)
        scores[rows, :] = raw
        grad_probs[rows, :] = dot(keys[:, :latent], latent_ref[...], 1, 1)
        row_max[...] = jnp.maximum(row_max[...], jnp.max(raw, axis=0, keepdims=True))

    keep.wait()
    score(all_ref, place(0, core), place(0, core))
    pair_own.wait_recv()
    score(all_ref, place(0, 1 - core), place(0, 1 - core))
    from_ahead = []
    for part in halves:
        to_behind[part].wait_recv()
        from_ahead.append(copies.start(slot(ahead, part), slot(ahead, part), sibling))
    score(all_ref, place(behind, core), place(behind, core))
    far = []
    for part in halves:
        onward[part].wait_recv()
        far.append(copies.start(slot(2, part), slot(2, part), sibling))
    score(all_ref, place(ahead, core), place(ahead, core))
    for copy in from_behind:
        copy.wait_recv()
    score(all_ref, place(ahead, 1 - core), place(ahead, 1 - core))
    for copy in from_ahead:
        copy.wait_recv()
    score(all_ref, place(behind, 1 - core), place(behind, 1 - core))
    score(all_ref, place(2, core), place(2, core))
    for copy in far:
        copy.wait_recv()
    score(all_ref, place(2, 1 - core), place(2, 1 - core))
    copies.finish()


def gather_and_score(table, pos, own_rows, nope, grad, rope, key_up, value_up):
    rows, width = own_rows.shape
    latent = key_up.shape[2]
    count = nope.shape[0]
    n_keys = 2 * NY * rows
    vmem = pl.BlockSpec(memory_space=pltpu.VMEM)
    hbm = pl.BlockSpec(memory_space=pltpu.HBM)
    return pl.pallas_call(
        gather_kernel,
        out_shape=(
            pltpu.VMEM((n_keys, width), bf16),
            pltpu.VMEM((count, width), bf16),
            pltpu.VMEM((count, latent), bf16),
            pltpu.VMEM((n_keys, count), f32),
            pltpu.VMEM((n_keys, count), f32),
            pltpu.VMEM((1, count), f32),
        ),
        in_specs=[pl.BlockSpec(memory_space=pltpu.SMEM), vmem] + [hbm] * 6,
        out_specs=(vmem,) * 6,
        scratch_shapes=[pltpu.VMEM(array.shape, bf16) for array in (nope, grad, rope, key_up, value_up)]
        + [
            pltpu.SemaphoreType.DMA((13,)),
            pltpu.SemaphoreType.DMA((13,)),
            pltpu.SemaphoreType.DMA,
            pltpu.SemaphoreType.DMA((5,)),
        ],
        compiler_params=pltpu.CompilerParams(
            collective_id=0, has_side_effects=True, vmem_limit_bytes=VMEM_LIMIT
        ),
    )(table, pos, own_rows, nope, grad, rope, key_up, value_up)


def main_kernel(
    keys_ref, query_ref, latent_ref, scores, grad_probs, row_max_ref, nope_hbm, grad_hbm, key_up_hbm,
    nope_out, rope_out, final, key_out, value_out,
    score_t, prob_t, query_grad, rope_parts, out_t,
    rows_out, pair_rows, acc, ring_half, ring_in, own_in, block, z_in, done,
    key_part, value_part,
    pair_key, pair_value, key_acc, value_acc, key_half, value_half, key_in, value_in,
    key_sum, value_sum, key_far, value_far,
    nope_ref, grad_ref, key_up_ref,
    send_sems, recv_sems, fetch_sems, ring_sems, cross_sems,
):
    ctx = lax.axis_index("ctx")
    head = lax.axis_index("head")
    dp = lax.axis_index("dp")
    y, core = ctx // 2, ctx % 2
    z = lax.rem(head, NZ)
    x_lo = head // NZ
    chips = [lax.rem(y + step, NY) for step in range(NY)]
    sibling = {"ctx": y * 2 + 1 - core}
    up = {"ctx": chips[1] * 2 + core}
    down = {"ctx": chips[3] * 2 + core}
    z_at = [lax.rem(z + step, NZ) for step in range(NZ)]
    z_device = [{"head": x_lo * NZ + place} for place in z_at]
    x_pair = {"head": (1 - x_lo) * NZ + z}
    x_device = [{"head": (1 - x_lo) * NZ + place} for place in z_at]
    up_to = [{"ctx": chips[1] * 2 + core, "head": x * NZ + z} for x in range(2)]
    down_to = [{"ctx": chips[3] * 2 + core, "head": x * NZ + z} for x in range(2)]
    up_across = {"ctx": chips[1] * 2 + core, "head": (1 - x_lo) * NZ + z}
    down_across = {"ctx": chips[3] * 2 + core, "head": (1 - x_lo) * NZ + z}
    dp_pair = {"dp": 1 - dp}
    far_first = sorted(range(1, NZ), key=lambda step: -min(step, NZ - step))
    direct = far_first[:5]
    friends = [z_device[step] for step in far_first] + [x_device[step] for step in direct]
    friends += [x_pair, dp_pair, up_across, down_across, up, down, sibling]
    barrier = pltpu.get_barrier_semaphore()
    for device in friends:
        pl.semaphore_signal(barrier, inc=1, device_id=device, device_id_type=MESH)

    fetches = fetch([nope_hbm, grad_hbm, key_up_hbm], [nope_ref, grad_ref, key_up_ref], fetch_sems)
    count = query_ref.shape[0]
    latent = latent_ref.shape[1]
    width = keys_ref.shape[1]
    n_keys = keys_ref.shape[0]
    chunk = 64
    n_chunks = n_keys // chunk
    row_max = row_max_ref[...]

    def weight_step(step, sums):
        rows = pl.ds(step * chunk, chunk)
        weights = jnp.exp(scores[rows, :] - row_max)
        pair = weights * grad_probs[rows, :]
        return sums[0] + by_eight(weights), sums[1] + by_eight(pair)

    def by_eight(values):
        return jnp.sum(values.reshape(-1, 8, values.shape[1]), axis=0)

    zero = jnp.zeros((8, count), f32)
    sums = lax.fori_loop(0, n_chunks, weight_step, (zero, zero))
    denominator, weighted = [jnp.sum(part, axis=0, keepdims=True) for part in sums]
    scale = 1.0 / denominator
    row_delta = weighted * scale

    def grad_step(step, carry):
        rows = pl.ds(step * chunk, chunk)
        probs = jnp.exp(scores[rows, :] - row_max) * scale
        prob_t[rows, :] = probs.astype(bf16)
        score_t[rows, :] = (probs * (grad_probs[rows, :] - row_delta) * softmax_scale).astype(bf16)
        return carry

    lax.fori_loop(0, n_chunks, grad_step, 0)

    pl.semaphore_wait(barrier, len(friends))
    copies = Copies(send_sems, recv_sems)

    def grad_rows(chip, which):
        rows = pl.ds(pl.multiple_of((chip * 2 + which) * 128, 128), 128)
        by_score = dot(score_t[rows, :], query_ref[...], 1, 0)
        by_prob = dot(prob_t[rows, :], latent_ref[...], 1, 0)
        return by_score[:, :latent] + by_prob, by_score[:, latent:]

    pair = {}
    for step in (2, 1, 3, 0):
        low, high = grad_rows(chips[step], 1 - core)
        rows_out[step, :, :, :latent] = low.astype(bf16).reshape(2, 64, latent)
        rows_out[step, :, :, latent:] = high.astype(bf16).reshape(2, 64, width - latent)
        pair[step] = copies.start(rows_out.at[step], pair_rows.at[step], sibling)

    def join(step):
        low, high = grad_rows(chips[step], core)
        pair[step].wait_recv()
        acc[step, :, :, :latent] = total(low.reshape(2, 64, latent), pair_rows[step, :, :, :latent]).astype(bf16)
        acc[step, :, :, latent:] = total(
            high.reshape(2, 64, width - latent), pair_rows[step, :, :, latent:]
        ).astype(bf16)

    join(2)
    up_far = copies.start(acc.at[2, 0], ring_half.at[0], up)
    down_far = copies.start(acc.at[2, 1], ring_half.at[1], down)
    join(1)
    copies.start(acc.at[1, 1], ring_in.at[0, x_lo], up_to[1], ring_sems.at[x_lo])
    join(3)
    copies.start(acc.at[3, 0], ring_in.at[1, x_lo], down_to[0], ring_sems.at[2 + x_lo])
    join(0)
    across = copies.start(acc.at[0, 1 - x_lo], own_in, x_pair)
    up_far.wait_recv()
    acc[1, 0] = total(acc[1, 0], ring_half[0]).astype(bf16)
    copies.start(acc.at[1, 0], ring_in.at[0, x_lo], up_to[0], ring_sems.at[x_lo])
    down_far.wait_recv()
    acc[3, 1] = total(acc[3, 1], ring_half[1]).astype(bf16)
    copies.start(acc.at[3, 1], ring_in.at[1, x_lo], down_to[1], ring_sems.at[2 + x_lo])

    @pl.loop(0, count // 128)
    def _(step):
        lane = pl.ds(pl.multiple_of(step * 128, 128), 128)
        grad = dot(score_t[:, lane], keys_ref[...], 0, 0)
        query_grad[lane, :] = grad[:, :latent].astype(bf16)
        rope_high = grad[:, latent:].astype(bf16)
        rope_parts[lane, :width - latent] = rope_high
        rope_parts[lane, width - latent:] = (grad[:, latent:] - rope_high.astype(f32)).astype(bf16)

    across.wait_recv()
    for way in range(2):
        for x in range(2):
            pltpu.make_async_remote_copy(
                src_ref=ring_in.at[way, x],
                dst_ref=ring_in.at[way, x],
                send_sem=send_sems.at[0],
                recv_sem=ring_sems.at[way * 2 + x],
                device_id=x_pair,
                device_id_type=MESH,
            ).wait_recv()
    mine = total(acc[0, x_lo], own_in[...], ring_in[0, 0], ring_in[0, 1], ring_in[1, 0], ring_in[1, 1])
    piece_rows = block.shape[1]
    for at in range(NZ):
        block[at] = mine[at * piece_rows:(at + 1) * piece_rows].astype(bf16)
    scatter = [copies.start(block.at[z_at[step]], z_in.at[step], z_device[step]) for step in far_first]

    for copy in fetches:
        copy.wait()

    @pl.loop(0, HEADS)
    def _(at):
        part = dot(one_head(nope_ref[...], at), query_grad[...], 0, 0)
        key_part[at] = part.astype(bf16).reshape(key_part.shape[1:])

    pair_weights = [copies.start(key_part.at[:, :, 1 - core], pair_key, sibling)]

    @pl.loop(0, latent // 128)
    def _(step):
        lane = pl.ds(pl.multiple_of(step * 128, 128), 128)
        out_t[lane, :] = dot(keys_ref[:, lane], prob_t[...], 0, 0).astype(bf16)

    @pl.loop(0, HEADS)
    def _(at):
        part = dot(out_t[...], one_head(grad_ref[...], at), 1, 0)
        value_part[at] = part.astype(bf16).reshape(value_part.shape[1:])

    pair_weights.append(copies.start(value_part.at[:, :, 1 - core], pair_value, sibling))

    @pl.loop(0, count // 128)
    def _(step):
        rows = pl.ds(step * 128, 128)
        every = dot(query_grad[rows, :], key_up_ref[...].reshape(-1, latent), 1, 1)
        n = nope_out.shape[1]
        which = lax.rem(iota((128, n), 0), HEADS)
        nope_out[rows, :] = total(
            *[jnp.where(which == at, every[:, at * n:(at + 1) * n], 0.0) for at in range(HEADS)]
        )

    rope = width - latent
    queries = count // HEADS
    for at in range(HEADS):
        order = (iota((count, queries), 0) == iota((count, queries), 1) * HEADS + at).astype(f32).astype(bf16)
        turned = dot(rope_parts[...], order, 0, 0)
        rope_out[at * rope:(at + 1) * rope, :] = turned[:rope] + turned[rope:]

    for copy in pair_weights:
        copy.wait_recv()
    for step in range(NY):
        key_acc[step] = total(key_part[:, chips[step], core], pair_key[:, chips[step]]).astype(bf16)
        value_acc[step] = total(value_part[:, chips[step], core], pair_value[:, chips[step]]).astype(bf16)
    low, high = pl.ds(0, 2), pl.ds(2, 2)
    weights_far = [
        copies.start(key_acc.at[2, low], key_half.at[0], up),
        copies.start(value_acc.at[2, low], value_half.at[0], up),
        copies.start(key_acc.at[2, high], key_half.at[1], down),
        copies.start(value_acc.at[2, high], value_half.at[1], down),
    ]
    weights_in = [
        copies.start(key_acc.at[1, high], key_in.at[0, high], up),
        copies.start(value_acc.at[1, high], value_in.at[0, high], up),
        copies.start(key_acc.at[3, low], key_in.at[1, low], down),
        copies.start(value_acc.at[3, low], value_in.at[1, low], down),
    ]
    for copy in scatter:
        copy.wait_recv()
    done[...] = total(block[z], *[z_in[step] for step in range(1, NZ)]).astype(bf16)
    final[x_lo, z] = done[...]
    gather = {}
    crossed = []
    for step in far_first:
        gather[step] = copies.start(done, final.at[x_lo, z], z_device[step])
        if step in direct:
            crossed.append(copies.start(done, final.at[x_lo, z], x_device[step], cross_sems.at[step]))
    crossed.append(copies.start(done, final.at[x_lo, z], x_pair, cross_sems.at[0]))
    for copy in weights_far:
        copy.wait_recv()
    key_acc[1, low] = total(key_acc[1, low], key_half[0]).astype(bf16)
    value_acc[1, low] = total(value_acc[1, low], value_half[0]).astype(bf16)
    key_acc[3, high] = total(key_acc[3, high], key_half[1]).astype(bf16)
    value_acc[3, high] = total(value_acc[3, high], value_half[1]).astype(bf16)
    weights_in += [
        copies.start(key_acc.at[1, low], key_in.at[0, low], up),
        copies.start(value_acc.at[1, low], value_in.at[0, low], up),
        copies.start(key_acc.at[3, high], key_in.at[1, high], down),
        copies.start(value_acc.at[3, high], value_in.at[1, high], down),
    ]

    def pass_on(steps):
        for step in steps:
            gather[step].wait_recv()
            if step not in direct:
                come = final.at[x_lo, z_at[NZ - step]]
                crossed.append(copies.start(come, come, x_pair, cross_sems.at[step]))

    near_first = far_first[::-1]
    pass_on(near_first[:6])

    for copy in weights_in:
        copy.wait_recv()
    key_sum[...] = total(key_acc[0], key_in[0], key_in[1]).astype(bf16)
    value_sum[...] = total(value_acc[0], value_in[0], value_in[1]).astype(bf16)
    weights_pair = [
        copies.start(key_sum.at[:, 1 - dp], key_far, dp_pair),
        copies.start(value_sum.at[:, 1 - dp], value_far, dp_pair),
    ]
    pass_on(near_first[6:])
    for copy in weights_pair:
        copy.wait_recv()
    key_out[...] = total(key_sum[:, dp], key_far[...])
    value_out[...] = total(value_sum[:, dp], value_far[...])
    for copy in crossed:
        copy.wait_recv()
    copies.finish()


def attend_and_reduce(keys, query_rows, grad_latent, scores, grad_probs, row_max, nope, grad, key_up):
    n_keys, width = keys.shape
    count, n_nope = nope.shape
    heads, _, latent = key_up.shape
    values = grad.shape[1]
    key_piece = (heads, 2, n_nope // 16, latent)
    value_piece = (heads, 2, latent // 16, values)
    half_key = (heads // 2,) + key_piece[1:]
    half_value = (heads // 2,) + value_piece[1:]
    n_copies = 4 + 2 + 4 + 1 + 15 + 31 + 16
    vmem = pl.BlockSpec(memory_space=pltpu.VMEM)
    hbm = pl.BlockSpec(memory_space=pltpu.HBM)
    return pl.pallas_call(
        main_kernel,
        out_shape=(
            pltpu.VMEM((count, n_nope), f32),
            pltpu.VMEM((heads * (width - latent), count // heads), f32),
            pltpu.VMEM((2, NZ, 4, width), bf16),
            pltpu.VMEM((heads, n_nope // 16, latent), f32),
            pltpu.VMEM((heads, latent // 16, values), f32),
        ),
        in_specs=[vmem] * 6 + [hbm] * 3,
        out_specs=(vmem,) * 5,
        scratch_shapes=[
            pltpu.VMEM((n_keys, count), bf16),
            pltpu.VMEM((n_keys, count), bf16),
            pltpu.VMEM((count, latent), bf16),
            pltpu.VMEM((count, 2 * (width - latent)), bf16),
            pltpu.VMEM((latent, count), bf16),
            pltpu.VMEM((NY, 2, 64, width), bf16),
            pltpu.VMEM((NY, 2, 64, width), bf16),
            pltpu.VMEM((NY, 2, 64, width), bf16),
            pltpu.VMEM((2, 64, width), bf16),
            pltpu.VMEM((2, 2, 64, width), bf16),
            pltpu.VMEM((64, width), bf16),
            pltpu.VMEM((NZ, 4, width), bf16),
            pltpu.VMEM((NZ, 4, width), bf16),
            pltpu.VMEM((4, width), bf16),
            pltpu.VMEM((heads, NY, 2) + key_piece[1:], bf16),
            pltpu.VMEM((heads, NY, 2) + value_piece[1:], bf16),
            pltpu.VMEM((heads, NY) + key_piece[1:], bf16),
            pltpu.VMEM((heads, NY) + value_piece[1:], bf16),
            pltpu.VMEM((NY,) + key_piece, bf16),
            pltpu.VMEM((NY,) + value_piece, bf16),
            pltpu.VMEM((2,) + half_key, bf16),
            pltpu.VMEM((2,) + half_value, bf16),
            pltpu.VMEM((2,) + key_piece, bf16),
            pltpu.VMEM((2,) + value_piece, bf16),
            pltpu.VMEM(key_piece, bf16),
            pltpu.VMEM(value_piece, bf16),
            pltpu.VMEM((heads, n_nope // 16, latent), bf16),
            pltpu.VMEM((heads, latent // 16, values), bf16),
            pltpu.VMEM(nope.shape, bf16),
            pltpu.VMEM(grad.shape, bf16),
            pltpu.VMEM(key_up.shape, bf16),
            pltpu.SemaphoreType.DMA((n_copies,)),
            pltpu.SemaphoreType.DMA((n_copies,)),
            pltpu.SemaphoreType.DMA((3,)),
            pltpu.SemaphoreType.DMA((4,)),
            pltpu.SemaphoreType.DMA((NZ,)),
        ],
        compiler_params=pltpu.CompilerParams(
            collective_id=1, has_side_effects=True, vmem_limit_bytes=VMEM_LIMIT
        ),
    )(*in_vmem(keys, query_rows, grad_latent, scores, grad_probs, row_max), nope, grad, key_up)


def in_vmem(*arrays):
    return [pltpu.with_memory_space_constraint(array, pltpu.VMEM) for array in arrays]


def store_kernel(*refs):
    for source, target in zip(refs[:5], refs[5:10]):
        if source.dtype == bf16:
            for half in range(source.shape[0]):
                for at in range(source.shape[1]):
                    rows = source.shape[2]
                    first = (half * source.shape[1] + at) * rows
                    target[first:first + rows, :] = source[half, at].astype(f32)
        else:
            target[...] = source[...]


def store_results(*results):
    vmem = pl.BlockSpec(memory_space=pltpu.VMEM)
    return pl.pallas_call(
        store_kernel,
        out_shape=tuple(
            jax.ShapeDtypeStruct(result.shape, f32)
            if result.dtype != bf16
            else jax.ShapeDtypeStruct((result.size // result.shape[3], result.shape[3]), f32)
            for result in results
        ),
        in_specs=[vmem] * len(results),
        out_specs=(vmem,) * len(results),
        compiler_params=pltpu.CompilerParams(vmem_limit_bytes=VMEM_LIMIT),
    )(*in_vmem(*results))


def on_device(
    query_nope, query_rope, query_pos, latent_cache, block_table, key_up, value_up, grad_out
):
    row_width = latent_cache.shape[3]
    nope = query_nope.reshape(-1, query_nope.shape[3])
    grad = grad_out.reshape(-1, grad_out.shape[3])
    rope = jnp.transpose(query_rope[0], (1, 2, 0))
    heads, rope_width, queries = rope.shape
    own_rows = latent_cache.reshape(-1, row_width)
    shared = gather_and_score(
        block_table, query_pos, own_rows, nope, grad, rope.reshape(-1, queries), key_up, value_up
    )
    results = attend_and_reduce(*shared, nope, grad, key_up)
    grad_nope, grad_rope, cache_grad, grad_key_map, grad_value_map = store_results(*results)
    return (
        grad_nope.reshape(query_nope.shape),
        jnp.transpose(grad_rope.reshape(heads, rope_width, queries), (2, 0, 1))[None],
        cache_grad.reshape(latent_cache.shape),
        grad_key_map,
        grad_value_map,
    )


def solution(mesh):
    placed = (
        P("dp", "ctx", "head", None),
        P("dp", "ctx", "head", None),
        P("dp", "ctx"),
        P("dp", "ctx", None, None),
        P("dp", None),
        P("head", None, None),
        P("head", None, None),
        P("dp", "ctx", "head", None),
    )
    return jax.shard_map(
        on_device,
        mesh=mesh,
        in_specs=placed,
        out_specs=(
            P("dp", "ctx", "head", None),
            P("dp", "ctx", "head", None),
            P("dp", "ctx", None, None),
            P("head", ("ctx", "dp"), None),
            P("head", ("ctx", "dp"), None),
        ),
        check_vma=False,
    )
```

```python
import jax
import jax.numpy as jnp
from jax import lax
from jax.experimental import pallas as pl
from jax.experimental.pallas import tpu as pltpu
from jax.sharding import PartitionSpec as P

softmax_scale = 192.0 ** (-0.5)
MESH = pl.DeviceIdType.MESH
NY = 4
NZ = 16
HEADS = 4
VMEM_LIMIT = 48 * 2**20
f32 = jnp.float32
bf16 = jnp.bfloat16


class Copies:
    def __init__(self, send_sems, recv_sems):
        self.send_sems, self.recv_sems, self.made = send_sems, recv_sems, []

    def start(self, src, dst, device, recv_sem=None):
        at = len(self.made)
        copy = pltpu.make_async_remote_copy(
            src_ref=src,
            dst_ref=dst,
            send_sem=self.send_sems.at[at],
            recv_sem=self.recv_sems.at[at] if recv_sem is None else recv_sem,
            device_id=device,
            device_id_type=MESH,
        )
        copy.start()
        self.made.append(copy)
        return copy

    def finish(self):
        for copy in self.made:
            copy.wait_send()


def entry_barrier(devices):
    barrier = pltpu.get_barrier_semaphore()
    for device in devices:
        pl.semaphore_signal(barrier, inc=1, device_id=device, device_id_type=MESH)
    pl.semaphore_wait(barrier, len(devices))


def total(*terms):
    terms = [term.astype(f32) for term in terms]
    result = terms[0]
    for term in terms[1:]:
        result = result + term
    return result


def dot(a, b, a_dim, b_dim):
    return lax.dot_general(a, b, (((a_dim,), (b_dim,)), ((), ())), preferred_element_type=f32)


def iota(shape, dim):
    return lax.broadcasted_iota(jnp.int32, shape, dim)


def one_head(values, head):
    return jnp.where(lax.rem(iota(values.shape, 0), HEADS) == head, values.astype(f32), 0.0).astype(bf16)


def fetch(sources, targets, sems):
    copies = []
    for at, (source, target) in enumerate(zip(sources, targets)):
        copies.append(pltpu.make_async_copy(source, target, sems.at[at]))
        copies[-1].start()
    return copies


def gather_kernel(
    table_hbm, pos_hbm, own_ref, nope_hbm, grad_hbm, rope_hbm, key_up_hbm, value_up_hbm,
    all_ref, query_ref, latent_ref, scores, grad_probs, row_max,
    table_ref, pos_ref, nope_ref, grad_ref, rope_ref, key_up_ref, value_up_ref,
    send_sems, recv_sems, own_sem, fetch_sems,
):
    fetches = fetch(
        [nope_hbm, key_up_hbm, rope_hbm, grad_hbm, value_up_hbm, table_hbm, pos_hbm],
        [nope_ref, key_up_ref, rope_ref, grad_ref, value_up_ref, table_ref, pos_ref],
        fetch_sems,
    )
    ctx = lax.axis_index("ctx")
    y, core = ctx // 2, ctx % 2
    rows_each = own_ref.shape[0]
    half = rows_each // 2

    def at(step, which):
        return {"ctx": lax.rem(y + step, NY) * 2 + which}

    def place(step, which):
        return pl.multiple_of((lax.rem(y + step, NY) * 2 + which) * rows_each, rows_each)

    def slot(step, part):
        return all_ref.at[pl.ds(pl.multiple_of(place(step, core) + part * half, half), half)]

    ahead = 1 + 2 * core
    behind = 3 - 2 * core
    sibling = at(0, 1 - core)
    entry_barrier([sibling, at(1, core), at(3, core)])
    copies = Copies(send_sems, recv_sems)
    halves = range(2)
    own_half = [own_ref.at[pl.ds(part * half, half)] for part in halves]
    to_ahead = [copies.start(own_half[part], slot(0, part), at(ahead, core)) for part in halves]
    own_slot = all_ref.at[pl.ds(place(0, core), rows_each)]
    pair_own = copies.start(own_ref, own_slot, sibling)
    keep = pltpu.make_async_copy(own_ref, own_slot, own_sem)
    keep.start()

    latent = key_up_ref.shape[2]
    rope = rope_ref.shape[0] // HEADS
    count = nope_ref.shape[0]

    def project(step):
        rows = slice(step * 128, (step + 1) * 128)
        nope, grad = nope_ref[rows, :], grad_ref[rows, :]
        spread = jnp.concatenate([one_head(nope, head) for head in range(HEADS)], axis=1)
        up = key_up_ref[...].reshape(spread.shape[1], latent)
        query_ref[rows, :latent] = dot(spread, up, 1, 0).astype(bf16)
        latent_ref[rows, :] = total(
            *[dot(one_head(grad, head), value_up_ref[head], 1, 1) for head in range(HEADS)]
        ).astype(bf16)
        query = (iota((128, 128), 0) + step * 128) // HEADS
        pick = (iota((128, 128), 1) == query).astype(f32).astype(bf16)
        every = dot(pick, rope_ref[...], 1, 1)
        shape = every.shape
        mine = iota(shape, 1) // rope == lax.rem(iota(shape, 0), HEADS)
        fold = (lax.rem(iota((shape[1], rope), 0), rope) == iota((shape[1], rope), 1)).astype(f32).astype(bf16)
        query_ref[rows, latent:] = dot(jnp.where(mine, every, 0.0).astype(bf16), fold, 1, 0).astype(bf16)

    for copy in fetches:
        copy.wait()
    project(0)
    project(1)
    to_behind = [copies.start(own_half[part], slot(0, part), at(behind, core)) for part in halves]
    project(2)
    onward, from_behind = [], []
    for part in halves:
        to_ahead[part].wait_recv()
        onward.append(copies.start(slot(behind, part), slot(behind, part), at(ahead, core)))
        from_behind.append(copies.start(slot(behind, part), slot(behind, part), sibling))
        if part == 0:
            project(3)

    blocks = table_ref.shape[1]
    page = all_ref.shape[0] // blocks
    spread = (iota((count // HEADS, count), 0) == iota((count // HEADS, count), 1) // HEADS).astype(f32).astype(bf16)
    pos = jnp.broadcast_to(pos_ref[...], (8, count // HEADS))
    query_pos = (
        dot((pos // 32).astype(f32).astype(bf16), spread, 1, 0) * 32.0
        + dot(lax.rem(pos, 32).astype(f32).astype(bf16), spread, 1, 0)
    )
    row_max[...] = jnp.full(row_max.shape, -jnp.inf, f32)

    def score(source, first, start):
        rows = pl.ds(start, rows_each)
        keys = source[pl.ds(first, rows_each), :]
        raw = dot(keys, query_ref[...], 1, 1) * softmax_scale
        index = iota((rows_each, 1), 0)
        key_pos = lax.rem(index, page)
        for part in range(rows_each // page):
            here = start // page + part
            base = sum(jnp.where(table_ref[0, b] == here, b * page, 0) for b in range(blocks))
            key_pos = key_pos + jnp.where(index // page == part, base, 0)
        raw = jnp.where(key_pos.astype(f32) <= query_pos[0:1, :], raw, -jnp.inf)
        scores[rows, :] = raw
        grad_probs[rows, :] = dot(keys[:, :latent], latent_ref[...], 1, 1)
        row_max[...] = jnp.maximum(row_max[...], jnp.max(raw, axis=0, keepdims=True))

    keep.wait()
    score(all_ref, place(0, core), place(0, core))
    pair_own.wait_recv()
    score(all_ref, place(0, 1 - core), place(0, 1 - core))
    from_ahead = []
    for part in halves:
        to_behind[part].wait_recv()
        from_ahead.append(copies.start(slot(ahead, part), slot(ahead, part), sibling))
    score(all_ref, place(behind, core), place(behind, core))
    far = []
    for part in halves:
        onward[part].wait_recv()
        far.append(copies.start(slot(2, part), slot(2, part), sibling))
    score(all_ref, place(ahead, core), place(ahead, core))
    for copy in from_behind:
        copy.wait_recv()
    score(all_ref, place(ahead, 1 - core), place(ahead, 1 - core))
    for copy in from_ahead:
        copy.wait_recv()
    score(all_ref, place(behind, 1 - core), place(behind, 1 - core))
    score(all_ref, place(2, core), place(2, core))
    for copy in far:
        copy.wait_recv()
    score(all_ref, place(2, 1 - core), place(2, 1 - core))
    copies.finish()


def gather_and_score(table, pos, own_rows, nope, grad, rope, key_up, value_up):
    rows, width = own_rows.shape
    latent = key_up.shape[2]
    count = nope.shape[0]
    n_keys = 2 * NY * rows
    vmem = pl.BlockSpec(memory_space=pltpu.VMEM)
    hbm = pl.BlockSpec(memory_space=pltpu.HBM)
    return pl.pallas_call(
        gather_kernel,
        out_shape=(
            pltpu.VMEM((n_keys, width), bf16),
            pltpu.VMEM((count, width), bf16),
            pltpu.VMEM((count, latent), bf16),
            pltpu.VMEM((n_keys, count), f32),
            pltpu.VMEM((n_keys, count), f32),
            pltpu.VMEM((1, count), f32),
        ),
        in_specs=[hbm] * 8,
        out_specs=(vmem,) * 6,
        scratch_shapes=[pltpu.SMEM(table.shape, jnp.int32), pltpu.VMEM(pos.shape, jnp.int32)]
        + [pltpu.VMEM(array.shape, bf16) for array in (nope, grad, rope, key_up, value_up)]
        + [
            pltpu.SemaphoreType.DMA((13,)),
            pltpu.SemaphoreType.DMA((13,)),
            pltpu.SemaphoreType.DMA,
            pltpu.SemaphoreType.DMA((7,)),
        ],
        compiler_params=pltpu.CompilerParams(
            collective_id=0, has_side_effects=True, vmem_limit_bytes=VMEM_LIMIT
        ),
    )(table, pos, own_rows, nope, grad, rope, key_up, value_up)


def main_kernel(
    keys_ref, query_ref, latent_ref, scores, grad_probs, row_max_ref, nope_hbm, grad_hbm, key_up_hbm,
    nope_out, rope_out, final, key_out, value_out,
    score_t, prob_t, query_grad, rope_parts, out_t,
    rows_out, pair_rows, acc, ring_half, ring_in, block, z_in, done,
    key_part, value_part,
    pair_key, pair_value, key_acc, value_acc, key_half, value_half, key_in, value_in,
    key_sum, value_sum, key_far, value_far,
    nope_ref, grad_ref, key_up_ref,
    send_sems, recv_sems, fetch_sems, cross_sems,
):
    ctx = lax.axis_index("ctx")
    head = lax.axis_index("head")
    dp = lax.axis_index("dp")
    y, core = ctx // 2, ctx % 2
    z = lax.rem(head, NZ)
    x_lo = head // NZ
    chips = [lax.rem(y + step, NY) for step in range(NY)]
    sibling = {"ctx": y * 2 + 1 - core}
    up = {"ctx": chips[1] * 2 + core}
    down = {"ctx": chips[3] * 2 + core}
    z_at = [lax.rem(z + step, NZ) for step in range(NZ)]
    z_device = [{"head": x_lo * NZ + place} for place in z_at]
    x_pair = {"head": (1 - x_lo) * NZ + z}
    x_device = [{"head": (1 - x_lo) * NZ + place} for place in z_at]
    dp_pair = {"dp": 1 - dp}
    far_first = sorted(range(1, NZ), key=lambda step: -min(step, NZ - step))
    direct = far_first[:5]
    friends = [z_device[step] for step in far_first] + [x_device[step] for step in far_first]
    friends += [x_pair, dp_pair, up, down, sibling]
    barrier = pltpu.get_barrier_semaphore()
    for device in friends:
        pl.semaphore_signal(barrier, inc=1, device_id=device, device_id_type=MESH)

    fetches = fetch([nope_hbm, grad_hbm, key_up_hbm], [nope_ref, grad_ref, key_up_ref], fetch_sems)
    count = query_ref.shape[0]
    latent = latent_ref.shape[1]
    width = keys_ref.shape[1]
    n_keys = keys_ref.shape[0]
    chunk = 64
    n_chunks = n_keys // chunk
    row_max = row_max_ref[...]

    def weight_step(step, sums):
        rows = pl.ds(step * chunk, chunk)
        weights = jnp.exp(scores[rows, :] - row_max)
        pair = weights * grad_probs[rows, :]
        return sums[0] + by_eight(weights), sums[1] + by_eight(pair)

    def by_eight(values):
        return jnp.sum(values.reshape(-1, 8, values.shape[1]), axis=0)

    zero = jnp.zeros((8, count), f32)
    sums = lax.fori_loop(0, n_chunks, weight_step, (zero, zero))
    denominator, weighted = [jnp.sum(part, axis=0, keepdims=True) for part in sums]
    scale = 1.0 / denominator
    row_delta = weighted * scale

    def grad_step(step, carry):
        rows = pl.ds(step * chunk, chunk)
        probs = jnp.exp(scores[rows, :] - row_max) * scale
        prob_t[rows, :] = probs.astype(bf16)
        score_t[rows, :] = (probs * (grad_probs[rows, :] - row_delta) * softmax_scale).astype(bf16)
        return carry

    lax.fori_loop(0, n_chunks, grad_step, 0)

    pl.semaphore_wait(barrier, len(friends))
    copies = Copies(send_sems, recv_sems)

    def grad_rows(chip, which):
        rows = pl.ds(pl.multiple_of((chip * 2 + which) * 128, 128), 128)
        by_score = dot(score_t[rows, :], query_ref[...], 1, 0)
        by_prob = dot(prob_t[rows, :], latent_ref[...], 1, 0)
        return by_score[:, :latent] + by_prob, by_score[:, latent:]

    pair = {}
    for step in (2, 1, 3, 0):
        low, high = grad_rows(chips[step], 1 - core)
        rows_out[step, :, :, :latent] = low.astype(bf16).reshape(2, 64, latent)
        rows_out[step, :, :, latent:] = high.astype(bf16).reshape(2, 64, width - latent)
        pair[step] = copies.start(rows_out.at[step], pair_rows.at[step], sibling)

    def join(step):
        low, high = grad_rows(chips[step], core)
        pair[step].wait_recv()
        acc[step, :, :, :latent] = total(low.reshape(2, 64, latent), pair_rows[step, :, :, :latent]).astype(bf16)
        acc[step, :, :, latent:] = total(
            high.reshape(2, 64, width - latent), pair_rows[step, :, :, latent:]
        ).astype(bf16)

    join(2)
    up_far = copies.start(acc.at[2, 0], ring_half.at[0], up)
    down_far = copies.start(acc.at[2, 1], ring_half.at[1], down)
    join(1)
    up_own = copies.start(acc.at[1, 1], ring_in.at[0, 1], up)
    join(3)
    down_own = copies.start(acc.at[3, 0], ring_in.at[1, 0], down)
    join(0)

    @pl.loop(0, count // 128)
    def _(step):
        lane = pl.ds(pl.multiple_of(step * 128, 128), 128)
        grad = dot(score_t[:, lane], keys_ref[...], 0, 0)
        query_grad[lane, :] = grad[:, :latent].astype(bf16)
        rope_high = grad[:, latent:].astype(bf16)
        rope_parts[lane, :width - latent] = rope_high
        rope_parts[lane, width - latent:] = (grad[:, latent:] - rope_high.astype(f32)).astype(bf16)

    for copy in fetches:
        copy.wait()

    @pl.loop(0, HEADS)
    def _(at):
        part = dot(one_head(nope_ref[...], at), query_grad[...], 0, 0)
        key_part[at] = part.astype(bf16).reshape(key_part.shape[1:])

    pair_weights = [copies.start(key_part.at[:, :, 1 - core], pair_key, sibling)]

    up_far.wait_recv()
    acc[1, 0] = total(acc[1, 0], ring_half[0]).astype(bf16)
    up_both = copies.start(acc.at[1, 0], ring_in.at[0, 0], up)
    down_far.wait_recv()
    acc[3, 1] = total(acc[3, 1], ring_half[1]).astype(bf16)
    down_both = copies.start(acc.at[3, 1], ring_in.at[1, 1], down)

    @pl.loop(0, latent // 128)
    def _(step):
        lane = pl.ds(pl.multiple_of(step * 128, 128), 128)
        out_t[lane, :] = dot(keys_ref[:, lane], prob_t[...], 0, 0).astype(bf16)

    @pl.loop(0, HEADS)
    def _(at):
        part = dot(out_t[...], one_head(grad_ref[...], at), 1, 0)
        value_part[at] = part.astype(bf16).reshape(value_part.shape[1:])

    pair_weights.append(copies.start(value_part.at[:, :, 1 - core], pair_value, sibling))

    for copy in (up_own, down_own, up_both, down_both):
        copy.wait_recv()
    piece_rows = block.shape[2]
    for half in range(2):
        mine = total(acc[0, half], ring_in[0, half], ring_in[1, half])
        for at in range(NZ):
            block[half, at] = mine[at * piece_rows:(at + 1) * piece_rows].astype(bf16)
    scatter = []
    for step in far_first + [0]:
        if step:
            scatter.append(copies.start(block.at[x_lo, z_at[step]], z_in.at[0, step], z_device[step]))
        scatter.append(copies.start(block.at[1 - x_lo, z_at[step]], z_in.at[1, step], x_device[step]))

    for copy in pair_weights:
        copy.wait_recv()
    for step in range(NY):
        key_acc[step] = total(key_part[:, chips[step], core], pair_key[:, chips[step]]).astype(bf16)
        value_acc[step] = total(value_part[:, chips[step], core], pair_value[:, chips[step]]).astype(bf16)
    low, high = pl.ds(0, 2), pl.ds(2, 2)
    weights_far = [
        copies.start(key_acc.at[2, low], key_half.at[0], up),
        copies.start(value_acc.at[2, low], value_half.at[0], up),
        copies.start(key_acc.at[2, high], key_half.at[1], down),
        copies.start(value_acc.at[2, high], value_half.at[1], down),
    ]
    weights_in = [
        copies.start(key_acc.at[1, high], key_in.at[0, high], up),
        copies.start(value_acc.at[1, high], value_in.at[0, high], up),
        copies.start(key_acc.at[3, low], key_in.at[1, low], down),
        copies.start(value_acc.at[3, low], value_in.at[1, low], down),
    ]
    @pl.loop(0, count // 128)
    def _(step):
        rows = pl.ds(step * 128, 128)
        every = dot(query_grad[rows, :], key_up_ref[...].reshape(-1, latent), 1, 1)
        n = nope_out.shape[1]
        which = lax.rem(iota((128, n), 0), HEADS)
        nope_out[rows, :] = total(
            *[jnp.where(which == at, every[:, at * n:(at + 1) * n], 0.0) for at in range(HEADS)]
        )

    rope = width - latent
    queries = count // HEADS
    for at in range(HEADS):
        order = (iota((count, queries), 0) == iota((count, queries), 1) * HEADS + at).astype(f32).astype(bf16)
        turned = dot(rope_parts[...], order, 0, 0)
        rope_out[at * rope:(at + 1) * rope, :] = turned[:rope] + turned[rope:]

    for copy in weights_far:
        copy.wait_recv()
    key_acc[1, low] = total(key_acc[1, low], key_half[0]).astype(bf16)
    value_acc[1, low] = total(value_acc[1, low], value_half[0]).astype(bf16)
    key_acc[3, high] = total(key_acc[3, high], key_half[1]).astype(bf16)
    value_acc[3, high] = total(value_acc[3, high], value_half[1]).astype(bf16)
    weights_in += [
        copies.start(key_acc.at[1, low], key_in.at[0, low], up),
        copies.start(value_acc.at[1, low], value_in.at[0, low], up),
        copies.start(key_acc.at[3, high], key_in.at[1, high], down),
        copies.start(value_acc.at[3, high], value_in.at[1, high], down),
    ]

    for copy in scatter:
        copy.wait_recv()
    parts = [z_in[0, step] for step in range(1, NZ)] + [z_in[1, step] for step in range(NZ)]
    done[...] = total(block[x_lo, z], *parts).astype(bf16)
    final[x_lo, z] = done[...]
    gather = {}
    crossed = []
    for step in far_first:
        gather[step] = copies.start(done, final.at[x_lo, z], z_device[step])
        if step in direct:
            crossed.append(copies.start(done, final.at[x_lo, z], x_device[step], cross_sems.at[step]))
    crossed.append(copies.start(done, final.at[x_lo, z], x_pair, cross_sems.at[0]))
    def pass_on(steps):
        for step in steps:
            gather[step].wait_recv()
            if step not in direct:
                come = final.at[x_lo, z_at[NZ - step]]
                crossed.append(copies.start(come, come, x_pair, cross_sems.at[step]))

    near_first = far_first[::-1]
    pass_on(near_first[:6])

    for copy in weights_in:
        copy.wait_recv()
    key_sum[...] = total(key_acc[0], key_in[0], key_in[1]).astype(bf16)
    value_sum[...] = total(value_acc[0], value_in[0], value_in[1]).astype(bf16)
    weights_pair = [
        copies.start(key_sum.at[:, 1 - dp], key_far, dp_pair),
        copies.start(value_sum.at[:, 1 - dp], value_far, dp_pair),
    ]
    pass_on(near_first[6:])
    for copy in weights_pair:
        copy.wait_recv()
    key_out[...] = total(key_sum[:, dp], key_far[...])
    value_out[...] = total(value_sum[:, dp], value_far[...])
    for copy in crossed:
        copy.wait_recv()
    copies.finish()


def attend_and_reduce(keys, query_rows, grad_latent, scores, grad_probs, row_max, nope, grad, key_up):
    n_keys, width = keys.shape
    count, n_nope = nope.shape
    heads, _, latent = key_up.shape
    values = grad.shape[1]
    key_piece = (heads, 2, n_nope // 16, latent)
    value_piece = (heads, 2, latent // 16, values)
    half_key = (heads // 2,) + key_piece[1:]
    half_value = (heads // 2,) + value_piece[1:]
    n_copies = 4 + 6 + 31 + 31 + 16
    vmem = pl.BlockSpec(memory_space=pltpu.VMEM)
    hbm = pl.BlockSpec(memory_space=pltpu.HBM)
    return pl.pallas_call(
        main_kernel,
        out_shape=(
            pltpu.VMEM((count, n_nope), f32),
            pltpu.VMEM((heads * (width - latent), count // heads), f32),
            pltpu.VMEM((2, NZ, 4, width), bf16),
            pltpu.VMEM((heads, n_nope // 16, latent), f32),
            pltpu.VMEM((heads, latent // 16, values), f32),
        ),
        in_specs=[vmem] * 6 + [hbm] * 3,
        out_specs=(vmem,) * 5,
        scratch_shapes=[
            pltpu.VMEM((n_keys, count), bf16),
            pltpu.VMEM((n_keys, count), bf16),
            pltpu.VMEM((count, latent), bf16),
            pltpu.VMEM((count, 2 * (width - latent)), bf16),
            pltpu.VMEM((latent, count), bf16),
            pltpu.VMEM((NY, 2, 64, width), bf16),
            pltpu.VMEM((NY, 2, 64, width), bf16),
            pltpu.VMEM((NY, 2, 64, width), bf16),
            pltpu.VMEM((2, 64, width), bf16),
            pltpu.VMEM((2, 2, 64, width), bf16),
            pltpu.VMEM((2, NZ, 4, width), bf16),
            pltpu.VMEM((2, NZ, 4, width), bf16),
            pltpu.VMEM((4, width), bf16),
            pltpu.VMEM((heads, NY, 2) + key_piece[1:], bf16),
            pltpu.VMEM((heads, NY, 2) + value_piece[1:], bf16),
            pltpu.VMEM((heads, NY) + key_piece[1:], bf16),
            pltpu.VMEM((heads, NY) + value_piece[1:], bf16),
            pltpu.VMEM((NY,) + key_piece, bf16),
            pltpu.VMEM((NY,) + value_piece, bf16),
            pltpu.VMEM((2,) + half_key, bf16),
            pltpu.VMEM((2,) + half_value, bf16),
            pltpu.VMEM((2,) + key_piece, bf16),
            pltpu.VMEM((2,) + value_piece, bf16),
            pltpu.VMEM(key_piece, bf16),
            pltpu.VMEM(value_piece, bf16),
            pltpu.VMEM((heads, n_nope // 16, latent), bf16),
            pltpu.VMEM((heads, latent // 16, values), bf16),
            pltpu.VMEM(nope.shape, bf16),
            pltpu.VMEM(grad.shape, bf16),
            pltpu.VMEM(key_up.shape, bf16),
            pltpu.SemaphoreType.DMA((n_copies,)),
            pltpu.SemaphoreType.DMA((n_copies,)),
            pltpu.SemaphoreType.DMA((3,)),
            pltpu.SemaphoreType.DMA((NZ,)),
        ],
        compiler_params=pltpu.CompilerParams(
            collective_id=1, has_side_effects=True, vmem_limit_bytes=VMEM_LIMIT
        ),
    )(*in_vmem(keys, query_rows, grad_latent, scores, grad_probs, row_max), nope, grad, key_up)


def in_vmem(*arrays):
    return [pltpu.with_memory_space_constraint(array, pltpu.VMEM) for array in arrays]


def store_kernel(*refs):
    for source, target in zip(refs[:5], refs[5:10]):
        if source.dtype == bf16:
            for half in range(source.shape[0]):
                for at in range(source.shape[1]):
                    rows = source.shape[2]
                    first = (half * source.shape[1] + at) * rows
                    target[first:first + rows, :] = source[half, at].astype(f32)
        else:
            target[...] = source[...]


def store_results(*results):
    vmem = pl.BlockSpec(memory_space=pltpu.VMEM)
    return pl.pallas_call(
        store_kernel,
        out_shape=tuple(
            jax.ShapeDtypeStruct(result.shape, f32)
            if result.dtype != bf16
            else jax.ShapeDtypeStruct((result.size // result.shape[3], result.shape[3]), f32)
            for result in results
        ),
        in_specs=[vmem] * len(results),
        out_specs=(vmem,) * len(results),
        compiler_params=pltpu.CompilerParams(vmem_limit_bytes=VMEM_LIMIT),
    )(*in_vmem(*results))


def on_device(
    query_nope, query_rope, query_pos, latent_cache, block_table, key_up, value_up, grad_out
):
    row_width = latent_cache.shape[3]
    nope = query_nope.reshape(-1, query_nope.shape[3])
    grad = grad_out.reshape(-1, grad_out.shape[3])
    rope = jnp.transpose(query_rope[0], (1, 2, 0))
    heads, rope_width, queries = rope.shape
    own_rows = latent_cache.reshape(-1, row_width)
    shared = gather_and_score(
        block_table, query_pos, own_rows, nope, grad, rope.reshape(-1, queries), key_up, value_up
    )
    results = attend_and_reduce(*shared, nope, grad, key_up)
    grad_nope, grad_rope, cache_grad, grad_key_map, grad_value_map = store_results(*results)
    return (
        grad_nope.reshape(query_nope.shape),
        jnp.transpose(grad_rope.reshape(heads, rope_width, queries), (2, 0, 1))[None],
        cache_grad.reshape(latent_cache.shape),
        grad_key_map,
        grad_value_map,
    )


def solution(mesh):
    placed = (
        P("dp", "ctx", "head", None),
        P("dp", "ctx", "head", None),
        P("dp", "ctx"),
        P("dp", "ctx", None, None),
        P("dp", None),
        P("head", None, None),
        P("head", None, None),
        P("dp", "ctx", "head", None),
    )
    return jax.shard_map(
        on_device,
        mesh=mesh,
        in_specs=placed,
        out_specs=(
            P("dp", "ctx", "head", None),
            P("dp", "ctx", "head", None),
            P("dp", "ctx", None, None),
            P("head", ("ctx", "dp"), None),
            P("head", ("ctx", "dp"), None),
        ),
        check_vma=False,
    )
```

```python
import jax
import jax.numpy as jnp
from jax import lax
from jax.experimental import pallas as pl
from jax.experimental.pallas import tpu as pltpu
from jax.sharding import PartitionSpec as P

softmax_scale = 192.0 ** (-0.5)
MESH = pl.DeviceIdType.MESH
NY = 4
NZ = 16
HEADS = 4
VMEM_LIMIT = 48 * 2**20
f32 = jnp.float32
bf16 = jnp.bfloat16


class Copies:
    def __init__(self, send_sems, recv_sems):
        self.send_sems, self.recv_sems, self.made = send_sems, recv_sems, []

    def start(self, src, dst, device, recv_sem=None):
        at = len(self.made)
        copy = pltpu.make_async_remote_copy(
            src_ref=src,
            dst_ref=dst,
            send_sem=self.send_sems.at[at],
            recv_sem=self.recv_sems.at[at] if recv_sem is None else recv_sem,
            device_id=device,
            device_id_type=MESH,
        )
        copy.start()
        self.made.append(copy)
        return copy

    def finish(self):
        for copy in self.made:
            copy.wait_send()


def entry_barrier(devices):
    barrier = pltpu.get_barrier_semaphore()
    for device in devices:
        pl.semaphore_signal(barrier, inc=1, device_id=device, device_id_type=MESH)
    pl.semaphore_wait(barrier, len(devices))


def total(*terms):
    terms = [term.astype(f32) for term in terms]
    result = terms[0]
    for term in terms[1:]:
        result = result + term
    return result


def dot(a, b, a_dim, b_dim):
    return lax.dot_general(a, b, (((a_dim,), (b_dim,)), ((), ())), preferred_element_type=f32)


def iota(shape, dim):
    return lax.broadcasted_iota(jnp.int32, shape, dim)


def one_head(values, head):
    return jnp.where(lax.rem(iota(values.shape, 0), HEADS) == head, values.astype(f32), 0.0).astype(bf16)


def fetch(sources, targets, sems):
    copies = []
    for at, (source, target) in enumerate(zip(sources, targets)):
        copies.append(pltpu.make_async_copy(source, target, sems.at[at]))
        copies[-1].start()
    return copies


def gather_kernel(
    table_hbm, pos_hbm, own_ref, nope_hbm, grad_hbm, rope_hbm, key_up_hbm, value_up_hbm,
    all_ref, query_ref, latent_ref, scores, grad_probs, row_max,
    table_ref, pos_ref, nope_ref, grad_ref, rope_ref, key_up_ref, value_up_ref,
    send_sems, recv_sems, own_sem, fetch_sems,
):
    fetches = fetch(
        [nope_hbm, key_up_hbm, rope_hbm, grad_hbm, value_up_hbm, table_hbm, pos_hbm],
        [nope_ref, key_up_ref, rope_ref, grad_ref, value_up_ref, table_ref, pos_ref],
        fetch_sems,
    )
    ctx = lax.axis_index("ctx")
    y, core = ctx // 2, ctx % 2
    rows_each = own_ref.shape[0]
    half = rows_each // 2

    def at(step, which):
        return {"ctx": lax.rem(y + step, NY) * 2 + which}

    def place(step, which):
        return pl.multiple_of((lax.rem(y + step, NY) * 2 + which) * rows_each, rows_each)

    def slot(step, part):
        return all_ref.at[pl.ds(pl.multiple_of(place(step, core) + part * half, half), half)]

    ahead = 1 + 2 * core
    behind = 3 - 2 * core
    sibling = at(0, 1 - core)
    entry_barrier([sibling, at(1, core), at(3, core)])
    copies = Copies(send_sems, recv_sems)
    halves = range(2)
    own_half = [own_ref.at[pl.ds(part * half, half)] for part in halves]
    to_ahead = [copies.start(own_half[part], slot(0, part), at(ahead, core)) for part in halves]
    own_slot = all_ref.at[pl.ds(place(0, core), rows_each)]
    pair_own = copies.start(own_ref, own_slot, sibling)
    keep = pltpu.make_async_copy(own_ref, own_slot, own_sem)
    keep.start()

    latent = key_up_ref.shape[2]
    rope = rope_ref.shape[0] // HEADS
    count = nope_ref.shape[0]

    def project(step):
        rows = slice(step * 128, (step + 1) * 128)
        nope, grad = nope_ref[rows, :], grad_ref[rows, :]
        spread = jnp.concatenate([one_head(nope, head) for head in range(HEADS)], axis=1)
        up = key_up_ref[...].reshape(spread.shape[1], latent)
        query_ref[rows, :latent] = dot(spread, up, 1, 0).astype(bf16)
        latent_ref[rows, :] = total(
            *[dot(one_head(grad, head), value_up_ref[head], 1, 1) for head in range(HEADS)]
        ).astype(bf16)
        query = (iota((128, 128), 0) + step * 128) // HEADS
        pick = (iota((128, 128), 1) == query).astype(f32).astype(bf16)
        every = dot(pick, rope_ref[...], 1, 1)
        shape = every.shape
        mine = iota(shape, 1) // rope == lax.rem(iota(shape, 0), HEADS)
        fold = (lax.rem(iota((shape[1], rope), 0), rope) == iota((shape[1], rope), 1)).astype(f32).astype(bf16)
        query_ref[rows, latent:] = dot(jnp.where(mine, every, 0.0).astype(bf16), fold, 1, 0).astype(bf16)

    for copy in fetches:
        copy.wait()
    project(0)
    project(1)
    to_behind = [copies.start(own_half[part], slot(0, part), at(behind, core)) for part in halves]
    project(2)
    onward, from_behind = [], []
    for part in halves:
        to_ahead[part].wait_recv()
        onward.append(copies.start(slot(behind, part), slot(behind, part), at(ahead, core)))
        from_behind.append(copies.start(slot(behind, part), slot(behind, part), sibling))
        if part == 0:
            project(3)

    blocks = table_ref.shape[1]
    page = all_ref.shape[0] // blocks
    spread = (iota((count // HEADS, count), 0) == iota((count // HEADS, count), 1) // HEADS).astype(f32).astype(bf16)
    pos = jnp.broadcast_to(pos_ref[...], (8, count // HEADS))
    query_pos = (
        dot((pos // 32).astype(f32).astype(bf16), spread, 1, 0) * 32.0
        + dot(lax.rem(pos, 32).astype(f32).astype(bf16), spread, 1, 0)
    )
    row_max[...] = jnp.full(row_max.shape, -jnp.inf, f32)

    def score(source, first, start):
        rows = pl.ds(start, rows_each)
        keys = source[pl.ds(first, rows_each), :]
        raw = dot(keys, query_ref[...], 1, 1) * softmax_scale
        index = iota((rows_each, 1), 0)
        key_pos = lax.rem(index, page)
        for part in range(rows_each // page):
            here = start // page + part
            base = sum(jnp.where(table_ref[0, b] == here, b * page, 0) for b in range(blocks))
            key_pos = key_pos + jnp.where(index // page == part, base, 0)
        raw = jnp.where(key_pos.astype(f32) <= query_pos[0:1, :], raw, -jnp.inf)
        scores[rows, :] = raw
        grad_probs[rows, :] = dot(keys[:, :latent], latent_ref[...], 1, 1)
        row_max[...] = jnp.maximum(row_max[...], jnp.max(raw, axis=0, keepdims=True))

    keep.wait()
    score(all_ref, place(0, core), place(0, core))
    pair_own.wait_recv()
    score(all_ref, place(0, 1 - core), place(0, 1 - core))
    from_ahead = []
    for part in halves:
        to_behind[part].wait_recv()
        from_ahead.append(copies.start(slot(ahead, part), slot(ahead, part), sibling))
    score(all_ref, place(behind, core), place(behind, core))
    far = []
    for part in halves:
        onward[part].wait_recv()
        far.append(copies.start(slot(2, part), slot(2, part), sibling))
    score(all_ref, place(ahead, core), place(ahead, core))
    for copy in from_behind:
        copy.wait_recv()
    score(all_ref, place(ahead, 1 - core), place(ahead, 1 - core))
    for copy in from_ahead:
        copy.wait_recv()
    score(all_ref, place(behind, 1 - core), place(behind, 1 - core))
    score(all_ref, place(2, core), place(2, core))
    for copy in far:
        copy.wait_recv()
    score(all_ref, place(2, 1 - core), place(2, 1 - core))
    copies.finish()


def gather_and_score(table, pos, own_rows, nope, grad, rope, key_up, value_up):
    rows, width = own_rows.shape
    latent = key_up.shape[2]
    count = nope.shape[0]
    n_keys = 2 * NY * rows
    vmem = pl.BlockSpec(memory_space=pltpu.VMEM)
    hbm = pl.BlockSpec(memory_space=pltpu.HBM)
    return pl.pallas_call(
        gather_kernel,
        out_shape=(
            pltpu.VMEM((n_keys, width), bf16),
            pltpu.VMEM((count, width), bf16),
            pltpu.VMEM((count, latent), bf16),
            pltpu.VMEM((n_keys, count), f32),
            pltpu.VMEM((n_keys, count), f32),
            pltpu.VMEM((1, count), f32),
        ),
        in_specs=[hbm] * 8,
        out_specs=(vmem,) * 6,
        scratch_shapes=[pltpu.SMEM(table.shape, jnp.int32), pltpu.VMEM(pos.shape, jnp.int32)]
        + [pltpu.VMEM(array.shape, bf16) for array in (nope, grad, rope, key_up, value_up)]
        + [
            pltpu.SemaphoreType.DMA((13,)),
            pltpu.SemaphoreType.DMA((13,)),
            pltpu.SemaphoreType.DMA,
            pltpu.SemaphoreType.DMA((7,)),
        ],
        compiler_params=pltpu.CompilerParams(
            collective_id=0, has_side_effects=True, vmem_limit_bytes=VMEM_LIMIT
        ),
    )(table, pos, own_rows, nope, grad, rope, key_up, value_up)


def main_kernel(
    keys_ref, query_ref, latent_ref, scores, grad_probs, row_max_ref, nope_hbm, grad_hbm, key_up_hbm,
    nope_out, rope_out, final, key_out, value_out,
    score_t, prob_t, query_grad, rope_parts, out_t,
    rows_out, pair_rows, acc, ring_half, ring_in, block, z_in, done,
    key_part, value_part,
    pair_key, pair_value, key_acc, value_acc, key_half, value_half, key_in, value_in,
    key_sum, value_sum, key_far, value_far,
    nope_ref, grad_ref, key_up_ref,
    send_sems, recv_sems, fetch_sems,
):
    ctx = lax.axis_index("ctx")
    head = lax.axis_index("head")
    dp = lax.axis_index("dp")
    y, core = ctx // 2, ctx % 2
    z = lax.rem(head, NZ)
    x_lo = head // NZ
    chips = [lax.rem(y + step, NY) for step in range(NY)]
    sibling = {"ctx": y * 2 + 1 - core}
    up = {"ctx": chips[1] * 2 + core}
    down = {"ctx": chips[3] * 2 + core}
    z_at = [lax.rem(z + step, NZ) for step in range(NZ)]
    z_device = [{"head": x_lo * NZ + place} for place in z_at]
    x_pair = {"head": (1 - x_lo) * NZ + z}
    x_device = [{"head": (1 - x_lo) * NZ + place} for place in z_at]
    dp_pair = {"dp": 1 - dp}
    far_first = sorted(range(1, NZ), key=lambda step: -min(step, NZ - step))
    friends = [z_device[step] for step in far_first] + [x_device[step] for step in far_first]
    friends += [x_pair, dp_pair, up, down, sibling]
    barrier = pltpu.get_barrier_semaphore()
    for device in friends:
        pl.semaphore_signal(barrier, inc=1, device_id=device, device_id_type=MESH)

    fetches = fetch([nope_hbm, grad_hbm, key_up_hbm], [nope_ref, grad_ref, key_up_ref], fetch_sems)
    count = query_ref.shape[0]
    latent = latent_ref.shape[1]
    width = keys_ref.shape[1]
    n_keys = keys_ref.shape[0]
    chunk = 64
    n_chunks = n_keys // chunk
    row_max = row_max_ref[...]

    def weight_step(step, sums):
        rows = pl.ds(step * chunk, chunk)
        weights = jnp.exp(scores[rows, :] - row_max)
        pair = weights * grad_probs[rows, :]
        return sums[0] + by_eight(weights), sums[1] + by_eight(pair)

    def by_eight(values):
        return jnp.sum(values.reshape(-1, 8, values.shape[1]), axis=0)

    zero = jnp.zeros((8, count), f32)
    sums = lax.fori_loop(0, n_chunks, weight_step, (zero, zero))
    denominator, weighted = [jnp.sum(part, axis=0, keepdims=True) for part in sums]
    scale = 1.0 / denominator
    row_delta = weighted * scale

    def grad_step(step, carry):
        rows = pl.ds(step * chunk, chunk)
        probs = jnp.exp(scores[rows, :] - row_max) * scale
        prob_t[rows, :] = probs.astype(bf16)
        score_t[rows, :] = (probs * (grad_probs[rows, :] - row_delta) * softmax_scale).astype(bf16)
        return carry

    lax.fori_loop(0, n_chunks, grad_step, 0)

    pl.semaphore_wait(barrier, len(friends))
    copies = Copies(send_sems, recv_sems)

    def grad_rows(chip, which):
        rows = pl.ds(pl.multiple_of((chip * 2 + which) * 128, 128), 128)
        by_score = dot(score_t[rows, :], query_ref[...], 1, 0)
        by_prob = dot(prob_t[rows, :], latent_ref[...], 1, 0)
        return by_score[:, :latent] + by_prob, by_score[:, latent:]

    pair = {}
    for step in (2, 1, 3, 0):
        low, high = grad_rows(chips[step], 1 - core)
        rows_out[step, :, :, :latent] = low.astype(bf16).reshape(2, 64, latent)
        rows_out[step, :, :, latent:] = high.astype(bf16).reshape(2, 64, width - latent)
        pair[step] = copies.start(rows_out.at[step], pair_rows.at[step], sibling)

    def join(step):
        low, high = grad_rows(chips[step], core)
        pair[step].wait_recv()
        acc[step, :, :, :latent] = total(low.reshape(2, 64, latent), pair_rows[step, :, :, :latent]).astype(bf16)
        acc[step, :, :, latent:] = total(
            high.reshape(2, 64, width - latent), pair_rows[step, :, :, latent:]
        ).astype(bf16)

    join(2)
    up_far = copies.start(acc.at[2, 0], ring_half.at[0], up)
    down_far = copies.start(acc.at[2, 1], ring_half.at[1], down)
    join(1)
    up_own = copies.start(acc.at[1, 1], ring_in.at[0, 1], up)
    join(3)
    down_own = copies.start(acc.at[3, 0], ring_in.at[1, 0], down)
    join(0)

    up_far.wait_recv()
    acc[1, 0] = total(acc[1, 0], ring_half[0]).astype(bf16)
    up_both = copies.start(acc.at[1, 0], ring_in.at[0, 0], up)
    down_far.wait_recv()
    acc[3, 1] = total(acc[3, 1], ring_half[1]).astype(bf16)
    down_both = copies.start(acc.at[3, 1], ring_in.at[1, 1], down)

    @pl.loop(0, count // 128)
    def _(step):
        lane = pl.ds(pl.multiple_of(step * 128, 128), 128)
        grad = dot(score_t[:, lane], keys_ref[...], 0, 0)
        query_grad[lane, :] = grad[:, :latent].astype(bf16)
        rope_high = grad[:, latent:].astype(bf16)
        rope_parts[lane, :width - latent] = rope_high
        rope_parts[lane, width - latent:] = (grad[:, latent:] - rope_high.astype(f32)).astype(bf16)

    for copy in (up_own, down_own, up_both, down_both):
        copy.wait_recv()
    piece_rows = block.shape[2]
    for half in range(2):
        mine = total(acc[0, half], ring_in[0, half], ring_in[1, half])
        for at in range(NZ):
            block[half, at] = mine[at * piece_rows:(at + 1) * piece_rows].astype(bf16)
    scatter = []
    for step in far_first + [0]:
        if step:
            scatter.append(copies.start(block.at[x_lo, z_at[step]], z_in.at[0, step], z_device[step]))
        scatter.append(copies.start(block.at[1 - x_lo, z_at[step]], z_in.at[1, step], x_device[step]))

    for copy in fetches:
        copy.wait()

    @pl.loop(0, HEADS)
    def _(at):
        part = dot(one_head(nope_ref[...], at), query_grad[...], 0, 0)
        key_part[at] = part.astype(bf16).reshape(key_part.shape[1:])

    pair_weights = [copies.start(key_part.at[:, :, 1 - core], pair_key, sibling)]

    @pl.loop(0, latent // 128)
    def _(step):
        lane = pl.ds(pl.multiple_of(step * 128, 128), 128)
        out_t[lane, :] = dot(keys_ref[:, lane], prob_t[...], 0, 0).astype(bf16)

    @pl.loop(0, HEADS)
    def _(at):
        part = dot(out_t[...], one_head(grad_ref[...], at), 1, 0)
        value_part[at] = part.astype(bf16).reshape(value_part.shape[1:])

    pair_weights.append(copies.start(value_part.at[:, :, 1 - core], pair_value, sibling))

    weights_far, weights_in = [], []
    low, high = pl.ds(0, 2), pl.ds(2, 2)
    weights = (
        (pair_weights[0], key_part, pair_key, key_acc, key_half, key_in),
        (pair_weights[1], value_part, pair_value, value_acc, value_half, value_in),
    )
    for copy, part, paired, joined, half_in, ring_to in weights:
        copy.wait_recv()
        for step in (2, 1, 3, 0):
            joined[step] = total(part[:, chips[step], core], paired[:, chips[step]]).astype(bf16)
            if step == 2:
                weights_far.append(copies.start(joined.at[2, low], half_in.at[0], up))
                weights_far.append(copies.start(joined.at[2, high], half_in.at[1], down))
            if step == 1:
                weights_in.append(copies.start(joined.at[1, high], ring_to.at[0, high], up))
            if step == 3:
                weights_in.append(copies.start(joined.at[3, low], ring_to.at[1, low], down))

    @pl.loop(0, count // 128)
    def _(step):
        rows = pl.ds(step * 128, 128)
        every = dot(query_grad[rows, :], key_up_ref[...].reshape(-1, latent), 1, 1)
        n = nope_out.shape[1]
        which = lax.rem(iota((128, n), 0), HEADS)
        nope_out[rows, :] = total(
            *[jnp.where(which == at, every[:, at * n:(at + 1) * n], 0.0) for at in range(HEADS)]
        )

    rope = width - latent
    queries = count // HEADS
    for at in range(HEADS):
        order = (iota((count, queries), 0) == iota((count, queries), 1) * HEADS + at).astype(f32).astype(bf16)
        turned = dot(rope_parts[...], order, 0, 0)
        rope_out[at * rope:(at + 1) * rope, :] = turned[:rope] + turned[rope:]

    for copy in scatter:
        copy.wait_recv()
    parts = [z_in[0, step] for step in range(1, NZ)] + [z_in[1, step] for step in range(NZ)]
    done[...] = total(block[x_lo, z], *parts).astype(bf16)
    final[x_lo, z] = done[...]
    gather = []
    for step in far_first + [0]:
        if step:
            gather.append(copies.start(done, final.at[x_lo, z], z_device[step]))
        gather.append(copies.start(done, final.at[x_lo, z], x_device[step]))

    for copy in weights_far:
        copy.wait_recv()
    key_acc[1, low] = total(key_acc[1, low], key_half[0]).astype(bf16)
    value_acc[1, low] = total(value_acc[1, low], value_half[0]).astype(bf16)
    key_acc[3, high] = total(key_acc[3, high], key_half[1]).astype(bf16)
    value_acc[3, high] = total(value_acc[3, high], value_half[1]).astype(bf16)
    weights_in += [
        copies.start(key_acc.at[1, low], key_in.at[0, low], up),
        copies.start(value_acc.at[1, low], value_in.at[0, low], up),
        copies.start(key_acc.at[3, high], key_in.at[1, high], down),
        copies.start(value_acc.at[3, high], value_in.at[1, high], down),
    ]

    for copy in weights_in:
        copy.wait_recv()
    key_sum[...] = total(key_acc[0], key_in[0], key_in[1]).astype(bf16)
    value_sum[...] = total(value_acc[0], value_in[0], value_in[1]).astype(bf16)
    weights_pair = [
        copies.start(key_sum.at[:, 1 - dp], key_far, dp_pair),
        copies.start(value_sum.at[:, 1 - dp], value_far, dp_pair),
    ]
    for copy in weights_pair:
        copy.wait_recv()
    key_out[...] = total(key_sum[:, dp], key_far[...])
    value_out[...] = total(value_sum[:, dp], value_far[...])
    for copy in gather:
        copy.wait_recv()
    copies.finish()


def attend_and_reduce(keys, query_rows, grad_latent, scores, grad_probs, row_max, nope, grad, key_up):
    n_keys, width = keys.shape
    count, n_nope = nope.shape
    heads, _, latent = key_up.shape
    values = grad.shape[1]
    key_piece = (heads, 2, n_nope // 16, latent)
    value_piece = (heads, 2, latent // 16, values)
    half_key = (heads // 2,) + key_piece[1:]
    half_value = (heads // 2,) + value_piece[1:]
    n_copies = 4 + 6 + 31 + 31 + 16
    vmem = pl.BlockSpec(memory_space=pltpu.VMEM)
    hbm = pl.BlockSpec(memory_space=pltpu.HBM)
    return pl.pallas_call(
        main_kernel,
        out_shape=(
            pltpu.VMEM((count, n_nope), f32),
            pltpu.VMEM((heads * (width - latent), count // heads), f32),
            pltpu.VMEM((2, NZ, 4, width), bf16),
            pltpu.VMEM((heads, n_nope // 16, latent), f32),
            pltpu.VMEM((heads, latent // 16, values), f32),
        ),
        in_specs=[vmem] * 6 + [hbm] * 3,
        out_specs=(vmem,) * 5,
        scratch_shapes=[
            pltpu.VMEM((n_keys, count), bf16),
            pltpu.VMEM((n_keys, count), bf16),
            pltpu.VMEM((count, latent), bf16),
            pltpu.VMEM((count, 2 * (width - latent)), bf16),
            pltpu.VMEM((latent, count), bf16),
            pltpu.VMEM((NY, 2, 64, width), bf16),
            pltpu.VMEM((NY, 2, 64, width), bf16),
            pltpu.VMEM((NY, 2, 64, width), bf16),
            pltpu.VMEM((2, 64, width), bf16),
            pltpu.VMEM((2, 2, 64, width), bf16),
            pltpu.VMEM((2, NZ, 4, width), bf16),
            pltpu.VMEM((2, NZ, 4, width), bf16),
            pltpu.VMEM((4, width), bf16),
            pltpu.VMEM((heads, NY, 2) + key_piece[1:], bf16),
            pltpu.VMEM((heads, NY, 2) + value_piece[1:], bf16),
            pltpu.VMEM((heads, NY) + key_piece[1:], bf16),
            pltpu.VMEM((heads, NY) + value_piece[1:], bf16),
            pltpu.VMEM((NY,) + key_piece, bf16),
            pltpu.VMEM((NY,) + value_piece, bf16),
            pltpu.VMEM((2,) + half_key, bf16),
            pltpu.VMEM((2,) + half_value, bf16),
            pltpu.VMEM((2,) + key_piece, bf16),
            pltpu.VMEM((2,) + value_piece, bf16),
            pltpu.VMEM(key_piece, bf16),
            pltpu.VMEM(value_piece, bf16),
            pltpu.VMEM((heads, n_nope // 16, latent), bf16),
            pltpu.VMEM((heads, latent // 16, values), bf16),
            pltpu.VMEM(nope.shape, bf16),
            pltpu.VMEM(grad.shape, bf16),
            pltpu.VMEM(key_up.shape, bf16),
            pltpu.SemaphoreType.DMA((n_copies,)),
            pltpu.SemaphoreType.DMA((n_copies,)),
            pltpu.SemaphoreType.DMA((3,)),
        ],
        compiler_params=pltpu.CompilerParams(
            collective_id=1, has_side_effects=True, vmem_limit_bytes=VMEM_LIMIT
        ),
    )(*in_vmem(keys, query_rows, grad_latent, scores, grad_probs, row_max), nope, grad, key_up)


def in_vmem(*arrays):
    return [pltpu.with_memory_space_constraint(array, pltpu.VMEM) for array in arrays]


def store_kernel(*refs):
    for source, target in zip(refs[:5], refs[5:10]):
        if source.dtype == bf16:
            for half in range(source.shape[0]):
                for at in range(source.shape[1]):
                    rows = source.shape[2]
                    first = (half * source.shape[1] + at) * rows
                    target[first:first + rows, :] = source[half, at].astype(f32)
        else:
            target[...] = source[...]


def store_results(*results):
    vmem = pl.BlockSpec(memory_space=pltpu.VMEM)
    return pl.pallas_call(
        store_kernel,
        out_shape=tuple(
            jax.ShapeDtypeStruct(result.shape, f32)
            if result.dtype != bf16
            else jax.ShapeDtypeStruct((result.size // result.shape[3], result.shape[3]), f32)
            for result in results
        ),
        in_specs=[vmem] * len(results),
        out_specs=(vmem,) * len(results),
        compiler_params=pltpu.CompilerParams(vmem_limit_bytes=VMEM_LIMIT),
    )(*in_vmem(*results))


def on_device(
    query_nope, query_rope, query_pos, latent_cache, block_table, key_up, value_up, grad_out
):
    row_width = latent_cache.shape[3]
    nope = query_nope.reshape(-1, query_nope.shape[3])
    grad = grad_out.reshape(-1, grad_out.shape[3])
    rope = jnp.transpose(query_rope[0], (1, 2, 0))
    heads, rope_width, queries = rope.shape
    own_rows = latent_cache.reshape(-1, row_width)
    shared = gather_and_score(
        block_table, query_pos, own_rows, nope, grad, rope.reshape(-1, queries), key_up, value_up
    )
    results = attend_and_reduce(*shared, nope, grad, key_up)
    grad_nope, grad_rope, cache_grad, grad_key_map, grad_value_map = store_results(*results)
    return (
        grad_nope.reshape(query_nope.shape),
        jnp.transpose(grad_rope.reshape(heads, rope_width, queries), (2, 0, 1))[None],
        cache_grad.reshape(latent_cache.shape),
        grad_key_map,
        grad_value_map,
    )


def solution(mesh):
    placed = (
        P("dp", "ctx", "head", None),
        P("dp", "ctx", "head", None),
        P("dp", "ctx"),
        P("dp", "ctx", None, None),
        P("dp", None),
        P("head", None, None),
        P("head", None, None),
        P("dp", "ctx", "head", None),
    )
    return jax.shard_map(
        on_device,
        mesh=mesh,
        in_specs=placed,
        out_specs=(
            P("dp", "ctx", "head", None),
            P("dp", "ctx", "head", None),
            P("dp", "ctx", None, None),
            P("head", ("ctx", "dp"), None),
            P("head", ("ctx", "dp"), None),
        ),
        check_vma=False,
    )
```

```python
import jax
import jax.numpy as jnp
from jax import lax
from jax.experimental import pallas as pl
from jax.experimental.pallas import tpu as pltpu
from jax.sharding import PartitionSpec as P

softmax_scale = 192.0 ** (-0.5)
MESH = pl.DeviceIdType.MESH
NY = 4
NZ = 16
HEADS = 4
VMEM_LIMIT = 48 * 2**20
f32 = jnp.float32
bf16 = jnp.bfloat16


class Copies:
    def __init__(self, send_sems, recv_sems):
        self.send_sems, self.recv_sems, self.made = send_sems, recv_sems, []

    def start(self, src, dst, device):
        at = len(self.made)
        copy = pltpu.make_async_remote_copy(
            src_ref=src,
            dst_ref=dst,
            send_sem=self.send_sems.at[at],
            recv_sem=self.recv_sems.at[at],
            device_id=device,
            device_id_type=MESH,
        )
        copy.start()
        self.made.append(copy)
        return copy

    def finish(self):
        for copy in self.made:
            copy.wait_send()


def entry_barrier(devices):
    barrier = pltpu.get_barrier_semaphore()
    for device in devices:
        pl.semaphore_signal(barrier, inc=1, device_id=device, device_id_type=MESH)
    pl.semaphore_wait(barrier, len(devices))


def total(*terms):
    terms = [term.astype(f32) for term in terms]
    result = terms[0]
    for term in terms[1:]:
        result = result + term
    return result


def dot(a, b, a_dim, b_dim):
    return lax.dot_general(a, b, (((a_dim,), (b_dim,)), ((), ())), preferred_element_type=f32)


def iota(shape, dim):
    return lax.broadcasted_iota(jnp.int32, shape, dim)


def one_head(values, head):
    return jnp.where(lax.rem(iota(values.shape, 0), HEADS) == head, values.astype(f32), 0.0).astype(bf16)


def fetch(sources, targets, sems):
    copies = []
    for at, (source, target) in enumerate(zip(sources, targets)):
        copies.append(pltpu.make_async_copy(source, target, sems.at[at]))
        copies[-1].start()
    return copies


def gather_kernel(
    table_hbm, pos_hbm, own_ref, nope_hbm, grad_hbm, rope_hbm, key_up_hbm, value_up_hbm,
    all_ref, query_ref, latent_ref, scores, grad_probs, row_max,
    table_ref, pos_ref, nope_ref, grad_ref, rope_ref, key_up_ref, value_up_ref,
    send_sems, recv_sems, own_sem, fetch_sems,
):
    fetches = fetch(
        [nope_hbm, key_up_hbm, rope_hbm, grad_hbm, value_up_hbm, table_hbm, pos_hbm],
        [nope_ref, key_up_ref, rope_ref, grad_ref, value_up_ref, table_ref, pos_ref],
        fetch_sems,
    )
    ctx = lax.axis_index("ctx")
    y, core = ctx // 2, ctx % 2
    rows_each = own_ref.shape[0]
    half = rows_each // 2

    def at(step, which):
        return {"ctx": lax.rem(y + step, NY) * 2 + which}

    def place(step, which):
        return pl.multiple_of((lax.rem(y + step, NY) * 2 + which) * rows_each, rows_each)

    def slot(step, part):
        return all_ref.at[pl.ds(pl.multiple_of(place(step, core) + part * half, half), half)]

    ahead = 1 + 2 * core
    behind = 3 - 2 * core
    sibling = at(0, 1 - core)
    entry_barrier([sibling, at(1, core), at(3, core)])
    copies = Copies(send_sems, recv_sems)
    halves = range(2)
    own_half = [own_ref.at[pl.ds(part * half, half)] for part in halves]
    to_ahead = [copies.start(own_half[part], slot(0, part), at(ahead, core)) for part in halves]
    own_slot = all_ref.at[pl.ds(place(0, core), rows_each)]
    pair_own = copies.start(own_ref, own_slot, sibling)
    keep = pltpu.make_async_copy(own_ref, own_slot, own_sem)
    keep.start()

    latent = key_up_ref.shape[2]
    rope = rope_ref.shape[0] // HEADS
    count = nope_ref.shape[0]

    def project(step):
        rows = slice(step * 128, (step + 1) * 128)
        nope, grad = nope_ref[rows, :], grad_ref[rows, :]
        spread = jnp.concatenate([one_head(nope, head) for head in range(HEADS)], axis=1)
        up = key_up_ref[...].reshape(spread.shape[1], latent)
        query_ref[rows, :latent] = dot(spread, up, 1, 0).astype(bf16)
        latent_ref[rows, :] = total(
            *[dot(one_head(grad, head), value_up_ref[head], 1, 1) for head in range(HEADS)]
        ).astype(bf16)
        query = (iota((128, 128), 0) + step * 128) // HEADS
        pick = (iota((128, 128), 1) == query).astype(f32).astype(bf16)
        every = dot(pick, rope_ref[...], 1, 1)
        shape = every.shape
        mine = iota(shape, 1) // rope == lax.rem(iota(shape, 0), HEADS)
        fold = (lax.rem(iota((shape[1], rope), 0), rope) == iota((shape[1], rope), 1)).astype(f32).astype(bf16)
        query_ref[rows, latent:] = dot(jnp.where(mine, every, 0.0).astype(bf16), fold, 1, 0).astype(bf16)

    for copy in fetches:
        copy.wait()
    project(0)
    project(1)
    to_behind = [copies.start(own_half[part], slot(0, part), at(behind, core)) for part in halves]
    project(2)
    onward, from_behind = [], []
    for part in halves:
        to_ahead[part].wait_recv()
        onward.append(copies.start(slot(behind, part), slot(behind, part), at(ahead, core)))
        from_behind.append(copies.start(slot(behind, part), slot(behind, part), sibling))
        if part == 0:
            project(3)

    blocks = table_ref.shape[1]
    page = all_ref.shape[0] // blocks
    spread = (iota((count // HEADS, count), 0) == iota((count // HEADS, count), 1) // HEADS).astype(f32).astype(bf16)
    pos = jnp.broadcast_to(pos_ref[...], (8, count // HEADS))
    query_pos = (
        dot((pos // 32).astype(f32).astype(bf16), spread, 1, 0) * 32.0
        + dot(lax.rem(pos, 32).astype(f32).astype(bf16), spread, 1, 0)
    )
    row_max[...] = jnp.full(row_max.shape, -jnp.inf, f32)

    def score(source, first, start):
        rows = pl.ds(start, rows_each)
        keys = source[pl.ds(first, rows_each), :]
        raw = dot(keys, query_ref[...], 1, 1) * softmax_scale
        index = iota((rows_each, 1), 0)
        key_pos = lax.rem(index, page)
        for part in range(rows_each // page):
            here = start // page + part
            base = sum(jnp.where(table_ref[0, b] == here, b * page, 0) for b in range(blocks))
            key_pos = key_pos + jnp.where(index // page == part, base, 0)
        raw = jnp.where(key_pos.astype(f32) <= query_pos[0:1, :], raw, -jnp.inf)
        scores[rows, :] = raw
        grad_probs[rows, :] = dot(keys[:, :latent], latent_ref[...], 1, 1)
        row_max[...] = jnp.maximum(row_max[...], jnp.max(raw, axis=0, keepdims=True))

    keep.wait()
    score(all_ref, place(0, core), place(0, core))
    pair_own.wait_recv()
    score(all_ref, place(0, 1 - core), place(0, 1 - core))
    from_ahead = []
    for part in halves:
        to_behind[part].wait_recv()
        from_ahead.append(copies.start(slot(ahead, part), slot(ahead, part), sibling))
    score(all_ref, place(behind, core), place(behind, core))
    far = []
    for part in halves:
        onward[part].wait_recv()
        far.append(copies.start(slot(2, part), slot(2, part), sibling))
    score(all_ref, place(ahead, core), place(ahead, core))
    for copy in from_behind:
        copy.wait_recv()
    score(all_ref, place(ahead, 1 - core), place(ahead, 1 - core))
    for copy in from_ahead:
        copy.wait_recv()
    score(all_ref, place(behind, 1 - core), place(behind, 1 - core))
    score(all_ref, place(2, core), place(2, core))
    for copy in far:
        copy.wait_recv()
    score(all_ref, place(2, 1 - core), place(2, 1 - core))
    copies.finish()


def gather_and_score(table, pos, own_rows, nope, grad, rope, key_up, value_up):
    rows, width = own_rows.shape
    latent = key_up.shape[2]
    count = nope.shape[0]
    n_keys = 2 * NY * rows
    vmem = pl.BlockSpec(memory_space=pltpu.VMEM)
    hbm = pl.BlockSpec(memory_space=pltpu.HBM)
    return pl.pallas_call(
        gather_kernel,
        out_shape=(
            pltpu.VMEM((n_keys, width), bf16),
            pltpu.VMEM((count, width), bf16),
            pltpu.VMEM((count, latent), bf16),
            pltpu.VMEM((n_keys, count), f32),
            pltpu.VMEM((n_keys, count), f32),
            pltpu.VMEM((1, count), f32),
        ),
        in_specs=[hbm] * 8,
        out_specs=(vmem,) * 6,
        scratch_shapes=[pltpu.SMEM(table.shape, jnp.int32), pltpu.VMEM(pos.shape, jnp.int32)]
        + [pltpu.VMEM(array.shape, bf16) for array in (nope, grad, rope, key_up, value_up)]
        + [
            pltpu.SemaphoreType.DMA((13,)),
            pltpu.SemaphoreType.DMA((13,)),
            pltpu.SemaphoreType.DMA,
            pltpu.SemaphoreType.DMA((7,)),
        ],
        compiler_params=pltpu.CompilerParams(
            collective_id=0, has_side_effects=True, vmem_limit_bytes=VMEM_LIMIT
        ),
    )(table, pos, own_rows, nope, grad, rope, key_up, value_up)


def main_kernel(
    keys_ref, query_ref, latent_ref, scores, grad_probs, row_max_ref, nope_hbm, grad_hbm, key_up_hbm,
    nope_out, rope_out, final, key_out, value_out,
    score_t, prob_t, query_grad, rope_parts, out_t,
    rows_out, pair_rows, acc, ring_half, ring_in, block, z_in, piece, piece_in, done,
    key_part, value_part,
    pair_key, pair_value, key_acc, value_acc, key_half, value_half, key_in, value_in,
    key_sum, value_sum, key_far, value_far,
    nope_ref, grad_ref, key_up_ref,
    send_sems, recv_sems, fetch_sems,
):
    ctx = lax.axis_index("ctx")
    head = lax.axis_index("head")
    dp = lax.axis_index("dp")
    y, core = ctx // 2, ctx % 2
    z = lax.rem(head, NZ)
    x_lo = head // NZ
    chips = [lax.rem(y + step, NY) for step in range(NY)]
    sibling = {"ctx": y * 2 + 1 - core}
    up = {"ctx": chips[1] * 2 + core}
    down = {"ctx": chips[3] * 2 + core}
    z_at = [lax.rem(z + step, NZ) for step in range(NZ)]
    z_device = [{"head": x_lo * NZ + place} for place in z_at]
    x_pair = {"head": (1 - x_lo) * NZ + z}
    dp_pair = {"dp": 1 - dp}
    far_first = sorted(range(1, NZ), key=lambda step: -min(step, NZ - step))
    friends = [z_device[step] for step in far_first] + [x_pair, dp_pair, up, down, sibling]
    barrier = pltpu.get_barrier_semaphore()
    for device in friends:
        pl.semaphore_signal(barrier, inc=1, device_id=device, device_id_type=MESH)

    fetches = fetch([nope_hbm, grad_hbm, key_up_hbm], [nope_ref, grad_ref, key_up_ref], fetch_sems)
    count = query_ref.shape[0]
    latent = latent_ref.shape[1]
    width = keys_ref.shape[1]
    n_keys = keys_ref.shape[0]
    chunk = 64
    n_chunks = n_keys // chunk
    row_max = row_max_ref[...]

    def weight_step(step, sums):
        rows = pl.ds(step * chunk, chunk)
        weights = jnp.exp(scores[rows, :] - row_max)
        pair = weights * grad_probs[rows, :]
        return sums[0] + by_eight(weights), sums[1] + by_eight(pair)

    def by_eight(values):
        return jnp.sum(values.reshape(-1, 8, values.shape[1]), axis=0)

    zero = jnp.zeros((8, count), f32)
    sums = lax.fori_loop(0, n_chunks, weight_step, (zero, zero))
    denominator, weighted = [jnp.sum(part, axis=0, keepdims=True) for part in sums]
    scale = 1.0 / denominator
    row_delta = weighted * scale

    def grad_step(step, carry):
        rows = pl.ds(step * chunk, chunk)
        probs = jnp.exp(scores[rows, :] - row_max) * scale
        prob_t[rows, :] = probs.astype(bf16)
        score_t[rows, :] = (probs * (grad_probs[rows, :] - row_delta) * softmax_scale).astype(bf16)
        return carry

    lax.fori_loop(0, n_chunks, grad_step, 0)

    pl.semaphore_wait(barrier, len(friends))
    copies = Copies(send_sems, recv_sems)

    def grad_rows(chip, which):
        rows = pl.ds(pl.multiple_of((chip * 2 + which) * 128, 128), 128)
        by_score = dot(score_t[rows, :], query_ref[...], 1, 0)
        by_prob = dot(prob_t[rows, :], latent_ref[...], 1, 0)
        return by_score[:, :latent] + by_prob, by_score[:, latent:]

    pair = {}
    for step in (2, 1, 3, 0):
        low, high = grad_rows(chips[step], 1 - core)
        rows_out[step, :, :, :latent] = low.astype(bf16).reshape(2, 64, latent)
        rows_out[step, :, :, latent:] = high.astype(bf16).reshape(2, 64, width - latent)
        pair[step] = copies.start(rows_out.at[step], pair_rows.at[step], sibling)

    def join(step):
        low, high = grad_rows(chips[step], core)
        pair[step].wait_recv()
        acc[step, :, :, :latent] = total(low.reshape(2, 64, latent), pair_rows[step, :, :, :latent]).astype(bf16)
        acc[step, :, :, latent:] = total(
            high.reshape(2, 64, width - latent), pair_rows[step, :, :, latent:]
        ).astype(bf16)

    join(2)
    up_far = copies.start(acc.at[2, 0], ring_half.at[0], up)
    down_far = copies.start(acc.at[2, 1], ring_half.at[1], down)
    join(1)
    up_own = copies.start(acc.at[1, 1], ring_in.at[0, 1], up)
    join(3)
    down_own = copies.start(acc.at[3, 0], ring_in.at[1, 0], down)
    join(0)
    up_far.wait_recv()
    acc[1, 0] = total(acc[1, 0], ring_half[0]).astype(bf16)
    up_both = copies.start(acc.at[1, 0], ring_in.at[0, 0], up)
    down_far.wait_recv()
    acc[3, 1] = total(acc[3, 1], ring_half[1]).astype(bf16)
    down_both = copies.start(acc.at[3, 1], ring_in.at[1, 1], down)

    @pl.loop(0, count // 128)
    def _(step):
        lane = pl.ds(pl.multiple_of(step * 128, 128), 128)
        grad = dot(score_t[:, lane], keys_ref[...], 0, 0)
        query_grad[lane, :] = grad[:, :latent].astype(bf16)
        rope_high = grad[:, latent:].astype(bf16)
        rope_parts[lane, :width - latent] = rope_high
        rope_parts[lane, width - latent:] = (grad[:, latent:] - rope_high.astype(f32)).astype(bf16)

    for copy in (up_own, down_own, up_both, down_both):
        copy.wait_recv()
    block[...] = total(acc[0], ring_in[0], ring_in[1]).astype(bf16).reshape(block.shape)
    scatter = [copies.start(block.at[z_at[step]], z_in.at[step], z_device[step]) for step in far_first]

    for copy in fetches:
        copy.wait()

    @pl.loop(0, HEADS)
    def _(at):
        part = dot(one_head(nope_ref[...], at), query_grad[...], 0, 0)
        key_part[at] = part.astype(bf16).reshape(key_part.shape[1:])

    pair_weights = [copies.start(key_part.at[:, :, 1 - core], pair_key, sibling)]

    @pl.loop(0, latent // 128)
    def _(step):
        lane = pl.ds(pl.multiple_of(step * 128, 128), 128)
        out_t[lane, :] = dot(keys_ref[:, lane], prob_t[...], 0, 0).astype(bf16)

    @pl.loop(0, HEADS)
    def _(at):
        part = dot(out_t[...], one_head(grad_ref[...], at), 1, 0)
        value_part[at] = part.astype(bf16).reshape(value_part.shape[1:])

    pair_weights.append(copies.start(value_part.at[:, :, 1 - core], pair_value, sibling))

    for copy in pair_weights:
        copy.wait_recv()
    for step in range(NY):
        key_acc[step] = total(key_part[:, chips[step], core], pair_key[:, chips[step]]).astype(bf16)
        value_acc[step] = total(value_part[:, chips[step], core], pair_value[:, chips[step]]).astype(bf16)
    low, high = pl.ds(0, 2), pl.ds(2, 2)
    weights_far = [
        copies.start(key_acc.at[2, low], key_half.at[0], up),
        copies.start(value_acc.at[2, low], value_half.at[0], up),
        copies.start(key_acc.at[2, high], key_half.at[1], down),
        copies.start(value_acc.at[2, high], value_half.at[1], down),
    ]
    weights_in = [
        copies.start(key_acc.at[1, high], key_in.at[0, high], up),
        copies.start(value_acc.at[1, high], value_in.at[0, high], up),
        copies.start(key_acc.at[3, low], key_in.at[1, low], down),
        copies.start(value_acc.at[3, low], value_in.at[1, low], down),
    ]
    @pl.loop(0, count // 128)
    def _(step):
        rows = pl.ds(step * 128, 128)
        every = dot(query_grad[rows, :], key_up_ref[...].reshape(-1, latent), 1, 1)
        n = nope_out.shape[1]
        which = lax.rem(iota((128, n), 0), HEADS)
        nope_out[rows, :] = total(
            *[jnp.where(which == at, every[:, at * n:(at + 1) * n], 0.0) for at in range(HEADS)]
        )

    rope = width - latent
    queries = count // HEADS
    for at in range(HEADS):
        order = (iota((count, queries), 0) == iota((count, queries), 1) * HEADS + at).astype(f32).astype(bf16)
        turned = dot(rope_parts[...], order, 0, 0)
        rope_out[at * rope:(at + 1) * rope, :] = turned[:rope] + turned[rope:]

    for copy in scatter:
        copy.wait_recv()
    piece[...] = total(block[z], *[z_in[step] for step in range(1, NZ)]).astype(bf16)
    across = copies.start(piece, piece_in, x_pair)
    for copy in weights_far:
        copy.wait_recv()
    key_acc[1, low] = total(key_acc[1, low], key_half[0]).astype(bf16)
    value_acc[1, low] = total(value_acc[1, low], value_half[0]).astype(bf16)
    key_acc[3, high] = total(key_acc[3, high], key_half[1]).astype(bf16)
    value_acc[3, high] = total(value_acc[3, high], value_half[1]).astype(bf16)
    weights_in += [
        copies.start(key_acc.at[1, low], key_in.at[0, low], up),
        copies.start(value_acc.at[1, low], value_in.at[0, low], up),
        copies.start(key_acc.at[3, high], key_in.at[1, high], down),
        copies.start(value_acc.at[3, high], value_in.at[1, high], down),
    ]

    across.wait_recv()
    done[...] = total(piece[...], piece_in[...]).astype(bf16)
    final[z] = done[...]
    gather = [copies.start(done, final.at[z], z_device[step]) for step in far_first]

    for copy in weights_in:
        copy.wait_recv()
    key_sum[...] = total(key_acc[0], key_in[0], key_in[1]).astype(bf16)
    value_sum[...] = total(value_acc[0], value_in[0], value_in[1]).astype(bf16)
    weights_pair = [
        copies.start(key_sum.at[:, 1 - dp], key_far, dp_pair),
        copies.start(value_sum.at[:, 1 - dp], value_far, dp_pair),
    ]
    for copy in weights_pair:
        copy.wait_recv()
    key_out[...] = total(key_sum[:, dp], key_far[...])
    value_out[...] = total(value_sum[:, dp], value_far[...])
    for copy in gather:
        copy.wait_recv()
    copies.finish()


def attend_and_reduce(keys, query_rows, grad_latent, scores, grad_probs, row_max, nope, grad, key_up):
    n_keys, width = keys.shape
    count, n_nope = nope.shape
    heads, _, latent = key_up.shape
    values = grad.shape[1]
    key_piece = (heads, 2, n_nope // 16, latent)
    value_piece = (heads, 2, latent // 16, values)
    half_key = (heads // 2,) + key_piece[1:]
    half_value = (heads // 2,) + value_piece[1:]
    n_copies = 4 + 2 + 6 + 8 + 4 + 15 + 1 + 2 + 15
    vmem = pl.BlockSpec(memory_space=pltpu.VMEM)
    hbm = pl.BlockSpec(memory_space=pltpu.HBM)
    return pl.pallas_call(
        main_kernel,
        out_shape=(
            pltpu.VMEM((count, n_nope), f32),
            pltpu.VMEM((heads * (width - latent), count // heads), f32),
            pltpu.VMEM((NZ, 8, width), bf16),
            pltpu.VMEM((heads, n_nope // 16, latent), f32),
            pltpu.VMEM((heads, latent // 16, values), f32),
        ),
        in_specs=[vmem] * 6 + [hbm] * 3,
        out_specs=(vmem,) * 5,
        scratch_shapes=[
            pltpu.VMEM((n_keys, count), bf16),
            pltpu.VMEM((n_keys, count), bf16),
            pltpu.VMEM((count, latent), bf16),
            pltpu.VMEM((count, 2 * (width - latent)), bf16),
            pltpu.VMEM((latent, count), bf16),
            pltpu.VMEM((NY, 2, 64, width), bf16),
            pltpu.VMEM((NY, 2, 64, width), bf16),
            pltpu.VMEM((NY, 2, 64, width), bf16),
            pltpu.VMEM((2, 64, width), bf16),
            pltpu.VMEM((2, 2, 64, width), bf16),
            pltpu.VMEM((NZ, 8, width), bf16),
            pltpu.VMEM((NZ, 8, width), bf16),
            pltpu.VMEM((8, width), bf16),
            pltpu.VMEM((8, width), bf16),
            pltpu.VMEM((8, width), bf16),
            pltpu.VMEM((heads, NY, 2) + key_piece[1:], bf16),
            pltpu.VMEM((heads, NY, 2) + value_piece[1:], bf16),
            pltpu.VMEM((heads, NY) + key_piece[1:], bf16),
            pltpu.VMEM((heads, NY) + value_piece[1:], bf16),
            pltpu.VMEM((NY,) + key_piece, bf16),
            pltpu.VMEM((NY,) + value_piece, bf16),
            pltpu.VMEM((2,) + half_key, bf16),
            pltpu.VMEM((2,) + half_value, bf16),
            pltpu.VMEM((2,) + key_piece, bf16),
            pltpu.VMEM((2,) + value_piece, bf16),
            pltpu.VMEM(key_piece, bf16),
            pltpu.VMEM(value_piece, bf16),
            pltpu.VMEM((heads, n_nope // 16, latent), bf16),
            pltpu.VMEM((heads, latent // 16, values), bf16),
            pltpu.VMEM(nope.shape, bf16),
            pltpu.VMEM(grad.shape, bf16),
            pltpu.VMEM(key_up.shape, bf16),
            pltpu.SemaphoreType.DMA((n_copies,)),
            pltpu.SemaphoreType.DMA((n_copies,)),
            pltpu.SemaphoreType.DMA((3,)),
        ],
        compiler_params=pltpu.CompilerParams(
            collective_id=1, has_side_effects=True, vmem_limit_bytes=VMEM_LIMIT
        ),
    )(*in_vmem(keys, query_rows, grad_latent, scores, grad_probs, row_max), nope, grad, key_up)


def in_vmem(*arrays):
    return [pltpu.with_memory_space_constraint(array, pltpu.VMEM) for array in arrays]


def store_kernel(*refs):
    for source, target in zip(refs[:5], refs[5:10]):
        target[...] = source[...].astype(f32)


def store_results(*results):
    vmem = pl.BlockSpec(memory_space=pltpu.VMEM)
    return pl.pallas_call(
        store_kernel,
        out_shape=tuple(jax.ShapeDtypeStruct(result.shape, f32) for result in results),
        in_specs=[vmem] * len(results),
        out_specs=(vmem,) * len(results),
        compiler_params=pltpu.CompilerParams(vmem_limit_bytes=VMEM_LIMIT),
    )(*in_vmem(*results))


def on_device(
    query_nope, query_rope, query_pos, latent_cache, block_table, key_up, value_up, grad_out
):
    row_width = latent_cache.shape[3]
    nope = query_nope.reshape(-1, query_nope.shape[3])
    grad = grad_out.reshape(-1, grad_out.shape[3])
    rope = jnp.transpose(query_rope[0], (1, 2, 0))
    heads, rope_width, queries = rope.shape
    own_rows = latent_cache.reshape(-1, row_width)
    shared = gather_and_score(
        block_table, query_pos, own_rows, nope, grad, rope.reshape(-1, queries), key_up, value_up
    )
    results = attend_and_reduce(*shared, nope, grad, key_up)
    grad_nope, grad_rope, cache_grad, grad_key_map, grad_value_map = store_results(*results)
    return (
        grad_nope.reshape(query_nope.shape),
        jnp.transpose(grad_rope.reshape(heads, rope_width, queries), (2, 0, 1))[None],
        cache_grad.reshape(latent_cache.shape),
        grad_key_map,
        grad_value_map,
    )


def solution(mesh):
    placed = (
        P("dp", "ctx", "head", None),
        P("dp", "ctx", "head", None),
        P("dp", "ctx"),
        P("dp", "ctx", None, None),
        P("dp", None),
        P("head", None, None),
        P("head", None, None),
        P("dp", "ctx", "head", None),
    )
    return jax.shard_map(
        on_device,
        mesh=mesh,
        in_specs=placed,
        out_specs=(
            P("dp", "ctx", "head", None),
            P("dp", "ctx", "head", None),
            P("dp", "ctx", None, None),
            P("head", ("ctx", "dp"), None),
            P("head", ("ctx", "dp"), None),
        ),
        check_vma=False,
    )
```

```python
import jax
import jax.numpy as jnp
from jax import lax
from jax.experimental import pallas as pl
from jax.experimental.pallas import tpu as pltpu
from jax.sharding import PartitionSpec as P

softmax_scale = 192.0 ** (-0.5)
MESH = pl.DeviceIdType.MESH
NY = 4
NZ = 16
HEADS = 4
VMEM_LIMIT = 48 * 2**20
f32 = jnp.float32
bf16 = jnp.bfloat16


class Copies:
    def __init__(self, send_sems, recv_sems):
        self.send_sems, self.recv_sems, self.made = send_sems, recv_sems, []

    def start(self, src, dst, device):
        at = len(self.made)
        copy = pltpu.make_async_remote_copy(
            src_ref=src,
            dst_ref=dst,
            send_sem=self.send_sems.at[at],
            recv_sem=self.recv_sems.at[at],
            device_id=device,
            device_id_type=MESH,
        )
        copy.start()
        self.made.append(copy)
        return copy

    def finish(self):
        for copy in self.made:
            copy.wait_send()


def entry_barrier(devices):
    barrier = pltpu.get_barrier_semaphore()
    for device in devices:
        pl.semaphore_signal(barrier, inc=1, device_id=device, device_id_type=MESH)
    pl.semaphore_wait(barrier, len(devices))


def total(*terms):
    terms = [term.astype(f32) for term in terms]
    result = terms[0]
    for term in terms[1:]:
        result = result + term
    return result


def dot(a, b, a_dim, b_dim):
    return lax.dot_general(a, b, (((a_dim,), (b_dim,)), ((), ())), preferred_element_type=f32)


def iota(shape, dim):
    return lax.broadcasted_iota(jnp.int32, shape, dim)


def one_head(values, head):
    return jnp.where(lax.rem(iota(values.shape, 0), HEADS) == head, values.astype(f32), 0.0).astype(bf16)


def fetch(sources, targets, sems):
    copies = []
    for at, (source, target) in enumerate(zip(sources, targets)):
        copies.append(pltpu.make_async_copy(source, target, sems.at[at]))
        copies[-1].start()
    return copies


def gather_kernel(
    table_hbm, pos_hbm, own_ref, nope_hbm, grad_hbm, rope_hbm, key_up_hbm, value_up_hbm,
    all_ref, query_ref, latent_ref, scores, grad_probs, row_max,
    table_ref, pos_ref, nope_ref, grad_ref, rope_ref, key_up_ref, value_up_ref,
    send_sems, recv_sems, own_sem, fetch_sems,
):
    fetches = fetch(
        [nope_hbm, key_up_hbm, rope_hbm, grad_hbm, value_up_hbm, table_hbm, pos_hbm],
        [nope_ref, key_up_ref, rope_ref, grad_ref, value_up_ref, table_ref, pos_ref],
        fetch_sems,
    )
    ctx = lax.axis_index("ctx")
    y, core = ctx // 2, ctx % 2
    rows_each = own_ref.shape[0]
    half = rows_each // 2

    def at(step, which):
        return {"ctx": lax.rem(y + step, NY) * 2 + which}

    def place(step, which):
        return pl.multiple_of((lax.rem(y + step, NY) * 2 + which) * rows_each, rows_each)

    def slot(step, part):
        return all_ref.at[pl.ds(pl.multiple_of(place(step, core) + part * half, half), half)]

    ahead = 1 + 2 * core
    behind = 3 - 2 * core
    sibling = at(0, 1 - core)
    entry_barrier([sibling, at(1, core), at(3, core)])
    copies = Copies(send_sems, recv_sems)
    halves = range(2)
    own_half = [own_ref.at[pl.ds(part * half, half)] for part in halves]
    to_ahead = [copies.start(own_half[part], slot(0, part), at(ahead, core)) for part in halves]
    own_slot = all_ref.at[pl.ds(place(0, core), rows_each)]
    pair_own = copies.start(own_ref, own_slot, sibling)
    keep = pltpu.make_async_copy(own_ref, own_slot, own_sem)
    keep.start()

    latent = key_up_ref.shape[2]
    rope = rope_ref.shape[0] // HEADS
    count = nope_ref.shape[0]

    def project(step):
        rows = slice(step * 128, (step + 1) * 128)
        nope, grad = nope_ref[rows, :], grad_ref[rows, :]
        spread = jnp.concatenate([one_head(nope, head) for head in range(HEADS)], axis=1)
        up = key_up_ref[...].reshape(spread.shape[1], latent)
        query_ref[rows, :latent] = dot(spread, up, 1, 0).astype(bf16)
        latent_ref[rows, :] = total(
            *[dot(one_head(grad, head), value_up_ref[head], 1, 1) for head in range(HEADS)]
        ).astype(bf16)
        query = (iota((128, 128), 0) + step * 128) // HEADS
        pick = (iota((128, 128), 1) == query).astype(f32).astype(bf16)
        every = dot(pick, rope_ref[...], 1, 1)
        shape = every.shape
        mine = iota(shape, 1) // rope == lax.rem(iota(shape, 0), HEADS)
        fold = (lax.rem(iota((shape[1], rope), 0), rope) == iota((shape[1], rope), 1)).astype(f32).astype(bf16)
        query_ref[rows, latent:] = dot(jnp.where(mine, every, 0.0).astype(bf16), fold, 1, 0).astype(bf16)

    for copy in fetches:
        copy.wait()
    project(0)
    project(1)
    to_behind = [copies.start(own_half[part], slot(0, part), at(behind, core)) for part in halves]
    project(2)
    onward, from_behind = [], []
    for part in halves:
        to_ahead[part].wait_recv()
        onward.append(copies.start(slot(behind, part), slot(behind, part), at(ahead, core)))
        from_behind.append(copies.start(slot(behind, part), slot(behind, part), sibling))
        if part == 0:
            project(3)

    blocks = table_ref.shape[1]
    page = all_ref.shape[0] // blocks
    spread = (iota((count // HEADS, count), 0) == iota((count // HEADS, count), 1) // HEADS).astype(f32).astype(bf16)
    pos = jnp.broadcast_to(pos_ref[...], (8, count // HEADS))
    query_pos = (
        dot((pos // 32).astype(f32).astype(bf16), spread, 1, 0) * 32.0
        + dot(lax.rem(pos, 32).astype(f32).astype(bf16), spread, 1, 0)
    )
    row_max[...] = jnp.full(row_max.shape, -jnp.inf, f32)

    def score(source, first, start):
        rows = pl.ds(start, rows_each)
        keys = source[pl.ds(first, rows_each), :]
        raw = dot(keys, query_ref[...], 1, 1) * softmax_scale
        index = iota((rows_each, 1), 0)
        key_pos = lax.rem(index, page)
        for part in range(rows_each // page):
            here = start // page + part
            base = sum(jnp.where(table_ref[0, b] == here, b * page, 0) for b in range(blocks))
            key_pos = key_pos + jnp.where(index // page == part, base, 0)
        raw = jnp.where(key_pos.astype(f32) <= query_pos[0:1, :], raw, -jnp.inf)
        scores[rows, :] = raw
        grad_probs[rows, :] = dot(keys[:, :latent], latent_ref[...], 1, 1)
        row_max[...] = jnp.maximum(row_max[...], jnp.max(raw, axis=0, keepdims=True))

    keep.wait()
    score(all_ref, place(0, core), place(0, core))
    pair_own.wait_recv()
    score(all_ref, place(0, 1 - core), place(0, 1 - core))
    from_ahead = []
    for part in halves:
        to_behind[part].wait_recv()
        from_ahead.append(copies.start(slot(ahead, part), slot(ahead, part), sibling))
    score(all_ref, place(behind, core), place(behind, core))
    far = []
    for part in halves:
        onward[part].wait_recv()
        far.append(copies.start(slot(2, part), slot(2, part), sibling))
    score(all_ref, place(ahead, core), place(ahead, core))
    for copy in from_behind:
        copy.wait_recv()
    score(all_ref, place(ahead, 1 - core), place(ahead, 1 - core))
    for copy in from_ahead:
        copy.wait_recv()
    score(all_ref, place(behind, 1 - core), place(behind, 1 - core))
    score(all_ref, place(2, core), place(2, core))
    for copy in far:
        copy.wait_recv()
    score(all_ref, place(2, 1 - core), place(2, 1 - core))
    copies.finish()


def gather_and_score(table, pos, own_rows, nope, grad, rope, key_up, value_up):
    rows, width = own_rows.shape
    latent = key_up.shape[2]
    count = nope.shape[0]
    n_keys = 2 * NY * rows
    vmem = pl.BlockSpec(memory_space=pltpu.VMEM)
    hbm = pl.BlockSpec(memory_space=pltpu.HBM)
    return pl.pallas_call(
        gather_kernel,
        out_shape=(
            pltpu.VMEM((n_keys, width), bf16),
            pltpu.VMEM((count, width), bf16),
            pltpu.VMEM((count, latent), bf16),
            pltpu.VMEM((n_keys, count), f32),
            pltpu.VMEM((n_keys, count), f32),
            pltpu.VMEM((1, count), f32),
        ),
        in_specs=[hbm] * 8,
        out_specs=(vmem,) * 6,
        scratch_shapes=[pltpu.SMEM(table.shape, jnp.int32), pltpu.VMEM(pos.shape, jnp.int32)]
        + [pltpu.VMEM(array.shape, bf16) for array in (nope, grad, rope, key_up, value_up)]
        + [
            pltpu.SemaphoreType.DMA((13,)),
            pltpu.SemaphoreType.DMA((13,)),
            pltpu.SemaphoreType.DMA,
            pltpu.SemaphoreType.DMA((7,)),
        ],
        compiler_params=pltpu.CompilerParams(
            collective_id=0, has_side_effects=True, vmem_limit_bytes=VMEM_LIMIT
        ),
    )(table, pos, own_rows, nope, grad, rope, key_up, value_up)


def tiles_of(rows):
    wide = rows.shape[1] // 128
    tiles = [rows[top:top + 4, lane * 128:lane * 128 + 128] for lane in range(wide) for top in (0, 4)]
    return tiles + [jnp.concatenate([rows[0:4, wide * 128:], rows[4:8, wide * 128:]], axis=1)]


def main_kernel(
    keys_ref, query_ref, latent_ref, scores, grad_probs, row_max_ref, nope_hbm, grad_hbm, key_up_hbm,
    nope_out, rope_out, final, key_out, value_out,
    score_t, prob_t, query_grad, rope_parts, out_t,
    rows_out, pair_rows, acc, ring_half, ring_in, block, z_in, piece, piece_in, done,
    key_part, value_part,
    pair_key, pair_value, key_acc, value_acc, key_half, value_half, key_in, value_in,
    key_sum, value_sum, key_far, value_far,
    nope_ref, grad_ref, key_up_ref,
    send_sems, recv_sems, fetch_sems,
):
    ctx = lax.axis_index("ctx")
    head = lax.axis_index("head")
    dp = lax.axis_index("dp")
    y, core = ctx // 2, ctx % 2
    z = lax.rem(head, NZ)
    x_lo = head // NZ
    chips = [lax.rem(y + step, NY) for step in range(NY)]
    sibling = {"ctx": y * 2 + 1 - core}
    up = {"ctx": chips[1] * 2 + core}
    down = {"ctx": chips[3] * 2 + core}
    z_at = [lax.rem(z + step, NZ) for step in range(NZ)]
    z_device = [{"head": x_lo * NZ + place} for place in z_at]
    x_pair = {"head": (1 - x_lo) * NZ + z}
    dp_pair = {"dp": 1 - dp}
    far_first = sorted(range(1, NZ), key=lambda step: -min(step, NZ - step))
    friends = [z_device[step] for step in far_first] + [x_pair, dp_pair, up, down, sibling]
    barrier = pltpu.get_barrier_semaphore()
    for device in friends:
        pl.semaphore_signal(barrier, inc=1, device_id=device, device_id_type=MESH)

    fetches = fetch([nope_hbm, grad_hbm, key_up_hbm], [nope_ref, grad_ref, key_up_ref], fetch_sems)
    count = query_ref.shape[0]
    latent = latent_ref.shape[1]
    width = keys_ref.shape[1]
    n_keys = keys_ref.shape[0]
    chunk = 64
    n_chunks = n_keys // chunk
    row_max = row_max_ref[...]

    def weight_step(step, sums):
        rows = pl.ds(step * chunk, chunk)
        weights = jnp.exp(scores[rows, :] - row_max)
        pair = weights * grad_probs[rows, :]
        return sums[0] + by_eight(weights), sums[1] + by_eight(pair)

    def by_eight(values):
        return jnp.sum(values.reshape(-1, 8, values.shape[1]), axis=0)

    zero = jnp.zeros((8, count), f32)
    sums = lax.fori_loop(0, n_chunks, weight_step, (zero, zero))
    denominator, weighted = [jnp.sum(part, axis=0, keepdims=True) for part in sums]
    scale = 1.0 / denominator
    row_delta = weighted * scale

    def grad_step(step, carry):
        rows = pl.ds(step * chunk, chunk)
        probs = jnp.exp(scores[rows, :] - row_max) * scale
        prob_t[rows, :] = probs.astype(bf16)
        score_t[rows, :] = (probs * (grad_probs[rows, :] - row_delta) * softmax_scale).astype(bf16)
        return carry

    lax.fori_loop(0, n_chunks, grad_step, 0)

    pl.semaphore_wait(barrier, len(friends))
    copies = Copies(send_sems, recv_sems)

    def grad_rows(chip, which):
        rows = pl.ds(pl.multiple_of((chip * 2 + which) * 128, 128), 128)
        by_score = dot(score_t[rows, :], query_ref[...], 1, 0)
        by_prob = dot(prob_t[rows, :], latent_ref[...], 1, 0)
        return by_score[:, :latent] + by_prob, by_score[:, latent:]

    pair = {}
    for step in (2, 1, 3, 0):
        low, high = grad_rows(chips[step], 1 - core)
        rows_out[step, :, :, :latent] = low.astype(bf16).reshape(2, 64, latent)
        rows_out[step, :, :, latent:] = high.astype(bf16).reshape(2, 64, width - latent)
        pair[step] = copies.start(rows_out.at[step], pair_rows.at[step], sibling)

    def join(step):
        low, high = grad_rows(chips[step], core)
        pair[step].wait_recv()
        acc[step, :, :, :latent] = total(low.reshape(2, 64, latent), pair_rows[step, :, :, :latent]).astype(bf16)
        acc[step, :, :, latent:] = total(
            high.reshape(2, 64, width - latent), pair_rows[step, :, :, latent:]
        ).astype(bf16)

    join(2)
    up_far = copies.start(acc.at[2, 0], ring_half.at[0], up)
    down_far = copies.start(acc.at[2, 1], ring_half.at[1], down)
    join(1)
    up_own = copies.start(acc.at[1, 1], ring_in.at[0, 1], up)
    join(3)
    down_own = copies.start(acc.at[3, 0], ring_in.at[1, 0], down)
    join(0)
    up_far.wait_recv()
    acc[1, 0] = total(acc[1, 0], ring_half[0]).astype(bf16)
    up_both = copies.start(acc.at[1, 0], ring_in.at[0, 0], up)
    down_far.wait_recv()
    acc[3, 1] = total(acc[3, 1], ring_half[1]).astype(bf16)
    down_both = copies.start(acc.at[3, 1], ring_in.at[1, 1], down)

    @pl.loop(0, count // 128)
    def _(step):
        lane = pl.ds(pl.multiple_of(step * 128, 128), 128)
        grad = dot(score_t[:, lane], keys_ref[...], 0, 0)
        query_grad[lane, :] = grad[:, :latent].astype(bf16)
        rope_high = grad[:, latent:].astype(bf16)
        rope_parts[lane, :width - latent] = rope_high
        rope_parts[lane, width - latent:] = (grad[:, latent:] - rope_high.astype(f32)).astype(bf16)

    for copy in (up_own, down_own, up_both, down_both):
        copy.wait_recv()
    for half in range(2):
        mine = total(acc[0, half], ring_in[0, half], ring_in[1, half])
        for at in range(NZ // 2):
            for tile, part in enumerate(tiles_of(mine[at * 8:at * 8 + 8])):
                block[half * (NZ // 2) + at, tile] = part.astype(bf16)
    scatter = [copies.start(block.at[z_at[step]], z_in.at[step], z_device[step]) for step in far_first]

    for copy in fetches:
        copy.wait()

    @pl.loop(0, HEADS)
    def _(at):
        part = dot(one_head(nope_ref[...], at), query_grad[...], 0, 0)
        key_part[at] = part.astype(bf16).reshape(key_part.shape[1:])

    pair_weights = [copies.start(key_part.at[:, :, 1 - core], pair_key, sibling)]

    @pl.loop(0, latent // 128)
    def _(step):
        lane = pl.ds(pl.multiple_of(step * 128, 128), 128)
        out_t[lane, :] = dot(keys_ref[:, lane], prob_t[...], 0, 0).astype(bf16)

    @pl.loop(0, HEADS)
    def _(at):
        part = dot(out_t[...], one_head(grad_ref[...], at), 1, 0)
        value_part[at] = part.astype(bf16).reshape(value_part.shape[1:])

    pair_weights.append(copies.start(value_part.at[:, :, 1 - core], pair_value, sibling))

    for copy in pair_weights:
        copy.wait_recv()
    for step in range(NY):
        key_acc[step] = total(key_part[:, chips[step], core], pair_key[:, chips[step]]).astype(bf16)
        value_acc[step] = total(value_part[:, chips[step], core], pair_value[:, chips[step]]).astype(bf16)
    low, high = pl.ds(0, 2), pl.ds(2, 2)
    weights_far = [
        copies.start(key_acc.at[2, low], key_half.at[0], up),
        copies.start(value_acc.at[2, low], value_half.at[0], up),
        copies.start(key_acc.at[2, high], key_half.at[1], down),
        copies.start(value_acc.at[2, high], value_half.at[1], down),
    ]
    weights_in = [
        copies.start(key_acc.at[1, high], key_in.at[0, high], up),
        copies.start(value_acc.at[1, high], value_in.at[0, high], up),
        copies.start(key_acc.at[3, low], key_in.at[1, low], down),
        copies.start(value_acc.at[3, low], value_in.at[1, low], down),
    ]
    @pl.loop(0, count // 128)
    def _(step):
        rows = pl.ds(step * 128, 128)
        every = dot(query_grad[rows, :], key_up_ref[...].reshape(-1, latent), 1, 1)
        n = nope_out.shape[1]
        which = lax.rem(iota((128, n), 0), HEADS)
        nope_out[rows, :] = total(
            *[jnp.where(which == at, every[:, at * n:(at + 1) * n], 0.0) for at in range(HEADS)]
        )

    rope = width - latent
    queries = count // HEADS
    for at in range(HEADS):
        order = (iota((count, queries), 0) == iota((count, queries), 1) * HEADS + at).astype(f32).astype(bf16)
        turned = dot(rope_parts[...], order, 0, 0)
        rope_out[at * rope:(at + 1) * rope, :] = turned[:rope] + turned[rope:]

    for copy in scatter:
        copy.wait_recv()
    piece[...] = total(block[z], *[z_in[step] for step in range(1, NZ)]).astype(bf16)
    across = copies.start(piece, piece_in, x_pair)
    for copy in weights_far:
        copy.wait_recv()
    key_acc[1, low] = total(key_acc[1, low], key_half[0]).astype(bf16)
    value_acc[1, low] = total(value_acc[1, low], value_half[0]).astype(bf16)
    key_acc[3, high] = total(key_acc[3, high], key_half[1]).astype(bf16)
    value_acc[3, high] = total(value_acc[3, high], value_half[1]).astype(bf16)
    weights_in += [
        copies.start(key_acc.at[1, low], key_in.at[0, low], up),
        copies.start(value_acc.at[1, low], value_in.at[0, low], up),
        copies.start(key_acc.at[3, high], key_in.at[1, high], down),
        copies.start(value_acc.at[3, high], value_in.at[1, high], down),
    ]

    across.wait_recv()
    done[...] = total(piece[...], piece_in[...]).astype(bf16)
    final[z] = done[...]
    gather = [copies.start(done, final.at[z], z_device[step]) for step in far_first]

    for copy in weights_in:
        copy.wait_recv()
    key_sum[...] = total(key_acc[0], key_in[0], key_in[1]).astype(bf16)
    value_sum[...] = total(value_acc[0], value_in[0], value_in[1]).astype(bf16)
    weights_pair = [
        copies.start(key_sum.at[:, 1 - dp], key_far, dp_pair),
        copies.start(value_sum.at[:, 1 - dp], value_far, dp_pair),
    ]
    for copy in weights_pair:
        copy.wait_recv()
    key_out[...] = total(key_sum[:, dp], key_far[...])
    value_out[...] = total(value_sum[:, dp], value_far[...])
    for copy in gather:
        copy.wait_recv()
    copies.finish()


def attend_and_reduce(keys, query_rows, grad_latent, scores, grad_probs, row_max, nope, grad, key_up):
    n_keys, width = keys.shape
    count, n_nope = nope.shape
    heads, _, latent = key_up.shape
    values = grad.shape[1]
    key_piece = (heads, 2, n_nope // 16, latent)
    value_piece = (heads, 2, latent // 16, values)
    half_key = (heads // 2,) + key_piece[1:]
    half_value = (heads // 2,) + value_piece[1:]
    packed = (8 * width // 512, 4, 128)
    n_copies = 4 + 2 + 6 + 8 + 4 + 15 + 1 + 2 + 15
    vmem = pl.BlockSpec(memory_space=pltpu.VMEM)
    hbm = pl.BlockSpec(memory_space=pltpu.HBM)
    return pl.pallas_call(
        main_kernel,
        out_shape=(
            pltpu.VMEM((count, n_nope), f32),
            pltpu.VMEM((heads * (width - latent), count // heads), f32),
            pltpu.VMEM((NZ,) + packed, bf16),
            pltpu.VMEM((heads, n_nope // 16, latent), f32),
            pltpu.VMEM((heads, latent // 16, values), f32),
        ),
        in_specs=[vmem] * 6 + [hbm] * 3,
        out_specs=(vmem,) * 5,
        scratch_shapes=[
            pltpu.VMEM((n_keys, count), bf16),
            pltpu.VMEM((n_keys, count), bf16),
            pltpu.VMEM((count, latent), bf16),
            pltpu.VMEM((count, 2 * (width - latent)), bf16),
            pltpu.VMEM((latent, count), bf16),
            pltpu.VMEM((NY, 2, 64, width), bf16),
            pltpu.VMEM((NY, 2, 64, width), bf16),
            pltpu.VMEM((NY, 2, 64, width), bf16),
            pltpu.VMEM((2, 64, width), bf16),
            pltpu.VMEM((2, 2, 64, width), bf16),
            pltpu.VMEM((NZ,) + packed, bf16),
            pltpu.VMEM((NZ,) + packed, bf16),
            pltpu.VMEM(packed, bf16),
            pltpu.VMEM(packed, bf16),
            pltpu.VMEM(packed, bf16),
            pltpu.VMEM((heads, NY, 2) + key_piece[1:], bf16),
            pltpu.VMEM((heads, NY, 2) + value_piece[1:], bf16),
            pltpu.VMEM((heads, NY) + key_piece[1:], bf16),
            pltpu.VMEM((heads, NY) + value_piece[1:], bf16),
            pltpu.VMEM((NY,) + key_piece, bf16),
            pltpu.VMEM((NY,) + value_piece, bf16),
            pltpu.VMEM((2,) + half_key, bf16),
            pltpu.VMEM((2,) + half_value, bf16),
            pltpu.VMEM((2,) + key_piece, bf16),
            pltpu.VMEM((2,) + value_piece, bf16),
            pltpu.VMEM(key_piece, bf16),
            pltpu.VMEM(value_piece, bf16),
            pltpu.VMEM((heads, n_nope // 16, latent), bf16),
            pltpu.VMEM((heads, latent // 16, values), bf16),
            pltpu.VMEM(nope.shape, bf16),
            pltpu.VMEM(grad.shape, bf16),
            pltpu.VMEM(key_up.shape, bf16),
            pltpu.SemaphoreType.DMA((n_copies,)),
            pltpu.SemaphoreType.DMA((n_copies,)),
            pltpu.SemaphoreType.DMA((3,)),
        ],
        compiler_params=pltpu.CompilerParams(
            collective_id=1, has_side_effects=True, vmem_limit_bytes=VMEM_LIMIT
        ),
    )(*in_vmem(keys, query_rows, grad_latent, scores, grad_probs, row_max), nope, grad, key_up)


def in_vmem(*arrays):
    return [pltpu.with_memory_space_constraint(array, pltpu.VMEM) for array in arrays]


def store_kernel(*refs):
    for source, target in zip(refs[:5], refs[5:10]):
        if source.dtype != bf16:
            target[...] = source[...]
            continue
        for piece in range(source.shape[0]):
            for top in (0, 4):
                rows = slice(piece * 8 + top, piece * 8 + top + 4)
                wide = source.shape[1] // 2
                for lane in range(wide):
                    target[rows, lane * 128:lane * 128 + 128] = source[piece, 2 * lane + top // 4].astype(f32)
                last = source[piece, 2 * wide].astype(f32)
                target[rows, wide * 128:] = last[:, top * 16:top * 16 + 64]


def store_results(*results):
    vmem = pl.BlockSpec(memory_space=pltpu.VMEM)
    return pl.pallas_call(
        store_kernel,
        out_shape=tuple(
            jax.ShapeDtypeStruct(
                result.shape if result.dtype != bf16 else (result.shape[0] * 8, result.shape[1] * 64), f32
            )
            for result in results
        ),
        in_specs=[vmem] * len(results),
        out_specs=(vmem,) * len(results),
        compiler_params=pltpu.CompilerParams(vmem_limit_bytes=VMEM_LIMIT),
    )(*in_vmem(*results))


def on_device(
    query_nope, query_rope, query_pos, latent_cache, block_table, key_up, value_up, grad_out
):
    row_width = latent_cache.shape[3]
    nope = query_nope.reshape(-1, query_nope.shape[3])
    grad = grad_out.reshape(-1, grad_out.shape[3])
    rope = jnp.transpose(query_rope[0], (1, 2, 0))
    heads, rope_width, queries = rope.shape
    own_rows = latent_cache.reshape(-1, row_width)
    shared = gather_and_score(
        block_table, query_pos, own_rows, nope, grad, rope.reshape(-1, queries), key_up, value_up
    )
    results = attend_and_reduce(*shared, nope, grad, key_up)
    grad_nope, grad_rope, cache_grad, grad_key_map, grad_value_map = store_results(*results)
    return (
        grad_nope.reshape(query_nope.shape),
        jnp.transpose(grad_rope.reshape(heads, rope_width, queries), (2, 0, 1))[None],
        cache_grad.reshape(latent_cache.shape),
        grad_key_map,
        grad_value_map,
    )


def solution(mesh):
    placed = (
        P("dp", "ctx", "head", None),
        P("dp", "ctx", "head", None),
        P("dp", "ctx"),
        P("dp", "ctx", None, None),
        P("dp", None),
        P("head", None, None),
        P("head", None, None),
        P("dp", "ctx", "head", None),
    )
    return jax.shard_map(
        on_device,
        mesh=mesh,
        in_specs=placed,
        out_specs=(
            P("dp", "ctx", "head", None),
            P("dp", "ctx", "head", None),
            P("dp", "ctx", None, None),
            P("head", ("ctx", "dp"), None),
            P("head", ("ctx", "dp"), None),
        ),
        check_vma=False,
    )
```
